512 devices in a mesh: hyp: 8 (over x, core), rows: 64 (over z, y).
Axes of the slice: x: 4, y: 8, z: 8, core: 2. Of those that a mesh axis runs over, the one named last changes fastest.
Arguments:
- offsets: float32 [2, 262144], P(None, 'rows'), may hold values from 0 to 1
- tile_cell: int32 [2048], P('rows'), may hold values from 0 to 31, as said below
- probes: int32 [8, 262144], P(None, 'rows'), may hold values from 0 to 1
- target: float32 [262144], P('rows'), may hold values from -6 to 6
- lengthscale: float32 [8], P('hyp'), parts along dimension 0, may hold values from 0.5 to 1
- amplitude: float32 [8], P('hyp'), parts along dimension 0, may hold values from 0.02 to 0.08
- noise: float32 [8], P('hyp'), parts along dimension 0, may hold values from 0.1 to 0.4
Outputs:
- solutions: float32 [72, 262144], P('hyp', 'rows'), parts along dimension 0
- quadratic: float32 [72], P('hyp'), parts along dimension 0
The draws below stay inside these ranges and needn't reach their ends.
There are 8 independent parts, one for each index of `hyp`. The reference program is written for one: setup_inputs(seed, part) draws one part's arguments, and reference() takes and returns one part's arrays. A program takes and returns all parts, laid end to end along the dimension named above; an argument that names none is the same for every part. Nothing has to cross between parts.
Inputs may be any that keep to these rules, and one draw needn't show every extreme that they name: `tile_cell`: each aligned block of 32 entries (one device's tiles) is a permutation of 0 to 31.
All inputs are finite; a program needn't handle non-finite values.
Results may differ from the reference program's by a relative error of at most 0.0003.
Values sent between devices are 32-bit elements; how exact they have to be, the bound alone decides.
No kernel may reach another device: no remote copies, remote signals or barrier semaphores. Data moves between devices by JAX's collectives and lax.ppermute only.
A program may use at most 64 MiB of HBM per device.

```python
import math
import jax
import jax.numpy as jnp
from jax import lax

TILE = 128
GX = 16
PROBES = 8
ITERS = 3
RHS = 9
TPD = 32
NTR = 128
NTILES = 2048
NPTS = 262144


def draw_tile_cell(key, part):
    scores = jax.random.randint(jax.random.fold_in(key, 17), (NTILES // TPD, TPD), 0, 1 << 30)
    placing = jnp.argsort(scores, axis=1, stable=True)
    return placing.reshape(NTILES).astype(jnp.int32)


def set_ends(drawn, key, least, top_value):
    place = [jax.random.randint(jax.random.fold_in(key, axis), (), 0, length) for axis, length in enumerate(drawn.shape)]
    main_axis = drawn.shape.index(max(drawn.shape))
    neighbour = place[:main_axis] + [(place[main_axis] + 1) % drawn.shape[main_axis]] + place[main_axis + 1:]
    return drawn.at[tuple(place)].set(least).at[tuple(neighbour)].set(top_value)


def block_scale(key, dims, shards, low, largest):
    def one(dim, shards_of):
        draws = jax.random.uniform(jax.random.fold_in(jax.random.fold_in(key, 6), dim), (shards_of,), jnp.float32, low / len(shards), largest / len(shards))
        return jnp.repeat(jnp.exp(draws), dims[dim] // shards_of).reshape((-1,) + (1,) * (len(dims) - dim - 1))

    factor_of = one(*shards[0])
    for cut in shards[1:]:
        factor_of = factor_of * one(*cut)
    return factor_of


def scatter_about(key, extent, scale, reach, shards=(), kind=jnp.bfloat16):
    array = scale * jax.random.normal(key, extent, jnp.float32)
    if shards:
        array = array * block_scale(key, extent, shards, -0.22, 0.18)
    return jnp.clip(array, -reach, reach).astype(kind)


def setup_inputs(seed: int = 0, part: int = 0) -> dict:
    streams_of = jax.random.split(jax.random.key(seed), 8)
    part_splits = jax.random.split(jax.random.fold_in(streams_of[7], part), 8)
    offsets = jnp.clip(1.0 * jax.random.uniform(streams_of[0], (2, NPTS), jnp.float32) ** block_scale(streams_of[0], (2, NPTS), ((1, 64),), -0.2, 0.2), 0.0, 1.0)
    tile_cell = draw_tile_cell(jax.random.fold_in(streams_of[7], 71), part)
    probes = set_ends(jax.random.randint(streams_of[2], (PROBES, NPTS), 0, 2), jax.random.fold_in(streams_of[2], 1), 0, 1).astype(jnp.int32)
    target = scatter_about(streams_of[3], (NPTS,), 1.0, 6.0, ((0, 64),), jnp.float32)
    lengthscale = jnp.clip(jnp.exp(jax.random.uniform(part_splits[4], (1,), jnp.float32, math.log(0.5), math.log(1.0))), 0.5, 1.0)
    amplitude = jnp.clip(jnp.exp(jax.random.uniform(part_splits[5], (1,), jnp.float32, math.log(0.02), math.log(0.08))), 0.02, 0.08)
    noise = jnp.clip(jnp.exp(jax.random.uniform(part_splits[6], (1,), jnp.float32, math.log(0.1), math.log(0.4))), 0.1, 0.4)
    return {"offsets": offsets, "tile_cell": tile_cell, "probes": probes, "target": target, "lengthscale": lengthscale, "amplitude": amplitude, "noise": noise}


def wendland(distance):
    closeness = jnp.maximum(1.0 - distance, 0.0)
    return closeness ** 4 * (4.0 * distance + 1.0)

def kernel_sum(vectors, padded_vectors, coords, padded_coords, inverse_length, amplitude, noise):
    row_count = vectors.shape[1]
    col_count = vectors.shape[2]
    total = noise * vectors
    for row_shift in (-1, 0, 1):
        for col_shift in (-1, 0, 1):
            other = padded_coords[:, 1 + row_shift:1 + row_shift + row_count, 1 + col_shift:1 + col_shift + col_count, :]
            values = padded_vectors[:, 1 + row_shift:1 + row_shift + row_count, 1 + col_shift:1 + col_shift + col_count, :]
            delta_rows = coords[0][..., :, None] - other[0][..., None, :]
            delta_cols = coords[1][..., :, None] - other[1][..., None, :]
            distance = jnp.sqrt(delta_rows * delta_rows + delta_cols * delta_cols) * inverse_length
            weights = amplitude * wendland(distance)
            total = total + jnp.einsum('rabj,abij->rabi', values, weights, precision=lax.Precision.HIGHEST)
    return total

def to_grid(stored, order):
    lead = stored.shape[0]
    tiles = stored.reshape(lead, NTILES, TILE)[:, order]
    return tiles.reshape(lead, NTR, GX, TILE)

def reference(offsets, tile_cell, probes, target, lengthscale, amplitude, noise):
    device_base = jnp.arange(NTILES, dtype=jnp.int32) // TPD * TPD
    cell = (tile_cell + device_base).astype(jnp.int32)
    order = jnp.argsort(cell).astype(jnp.int32)
    grid_offsets = to_grid(offsets, order)
    row_place = jnp.arange(NTR, dtype=jnp.float32)[:, None, None]
    col_place = jnp.arange(GX, dtype=jnp.float32)[None, :, None]
    coords = jnp.stack([grid_offsets[0] + row_place, grid_offsets[1] + col_place])
    padded_coords = jnp.pad(coords, ((0, 0), (1, 1), (1, 1), (0, 0)))
    signs = 2.0 * probes.astype(jnp.float32) - 1.0
    right_sides = to_grid(jnp.concatenate([signs, target[None, :]], axis=0), order)
    inverse_length = 1.0 / lengthscale[0]

    def operate(vectors):
        padded = jnp.pad(vectors, ((0, 0), (1, 1), (1, 1), (0, 0)))
        return kernel_sum(vectors, padded, coords, padded_coords, inverse_length, amplitude[0], noise[0])

    def widen(scalars):
        return scalars[:, None, None, None]
    iterate = jnp.zeros_like(right_sides)
    residual = right_sides
    direction = right_sides
    norm_now = lax.optimization_barrier(jnp.sum(residual * residual, axis=(1, 2, 3)))
    for iteration in range(ITERS):
        image = operate(direction)
        alpha = norm_now / lax.optimization_barrier(jnp.sum(direction * image, axis=(1, 2, 3)))
        iterate = iterate + widen(alpha) * direction
        residual = residual - widen(alpha) * image
        if iteration + 1 < ITERS:
            norm_next = lax.optimization_barrier(jnp.sum(residual * residual, axis=(1, 2, 3)))
            direction = residual + widen(norm_next / norm_now) * direction
            norm_now = norm_next
    quadratic = lax.optimization_barrier(jnp.sum(right_sides * iterate, axis=(1, 2, 3))) / NPTS
    solutions = iterate.reshape(RHS, NTILES, TILE)[:, cell].reshape(RHS, NPTS)
    return (solutions, quadratic)
```

```python
import jax
import jax.numpy as jnp
from jax import lax
from jax.experimental import pallas as pl
from jax.experimental.pallas import tpu as pltpu
from jax.sharding import PartitionSpec as P

TILE = 128
GX = 16
RHS = 9
ROWS = 16
WIDE = GX * TILE
FEATURES = 32
PAD = GX + 2
BAND = 3 * 2 * TILE
F32 = jnp.float32
BF16 = jnp.bfloat16
TINY = 1e-30

VMEM = pl.BlockSpec(memory_space=pltpu.VMEM)
SMEM = pl.BlockSpec(memory_space=pltpu.SMEM)


def call(kernel, name, out_shape, in_specs, scratch=(), flops=0, limit=12):
    return pl.pallas_call(
        kernel,
        name=name,
        out_shape=out_shape,
        in_specs=in_specs,
        out_specs=jax.tree.map(lambda _: VMEM, out_shape),
        scratch_shapes=list(scratch),
        cost_estimate=pl.CostEstimate(flops=flops, bytes_accessed=1 << 20, transcendentals=0),
        compiler_params=pltpu.CompilerParams(vmem_limit_bytes=limit << 20),
    )


def grid_row(dtype=F32):
    return jax.ShapeDtypeStruct((ROWS, WIDE), dtype)


def lanes(tile, width=TILE):
    return pl.ds(pl.multiple_of(tile * width, width), width)


def pack_kernel(cell_ref, offsets_ref, probes_ref, target_ref, first_ref, second_ref):
    filler = jnp.zeros((ROWS - RHS - 2, TILE), F32)
    for s in range(cell_ref.shape[0]):
        here = slice(s * TILE, (s + 1) * TILE)
        signs = 2.0 * probes_ref[:, here].astype(F32) - 1.0
        rest = jnp.concatenate([target_ref[:, here], offsets_ref[:, here], filler], axis=0)
        cell = cell_ref[s]

        def put(ref, column, signs=signs, rest=rest):
            ref[0:8, lanes(column)] = signs
            ref[8:16, lanes(column)] = rest

        @pl.when(cell < GX)
        def _():
            put(first_ref, cell)

        @pl.when(cell >= GX)
        def _():
            put(second_ref, cell - GX)


def constants(scale_ref, amp_ref):
    amp = jnp.full((1, TILE), amp_ref[0], F32)
    reach = jnp.exp(0.2 * jnp.log(4.0 * amp))
    square = reach * reach
    top = 5.0 * amp / (square * square)
    factor = reach / jnp.full((1, TILE), scale_ref[0], F32)
    return reach, top, factor


def split_rows(values, level):
    first = values.astype(BF16).astype(F32)
    rest = values - first
    second = rest.astype(BF16).astype(F32)
    third = rest - second
    return jnp.where(level == 0, first, jnp.where(level == 1, second, third))


def feature_rows():
    row = lax.broadcasted_iota(jnp.int32, (FEATURES, TILE), 0)

    def level(order):
        out = jnp.zeros_like(row)
        for k, v in enumerate(order):
            if v:
                out = jnp.where(row == k, v, out)
        return out

    source = level([0, 0, 1, 1, 0, 2] * 2 + [0, 1, 2] + [0, 0, 0])
    target = level([0, 1, 0, 1, 2, 0] * 2 + [0, 0, 0] + [0, 1, 2])
    kind = jnp.where(row < 6, 0, jnp.where(row < 12, 1, jnp.where(row < 15, 2, jnp.where(row < 18, 3, 4))))
    return kind, source, target


def choose(kind, a, b, c, d):
    return jnp.where(
        kind == 0, a, jnp.where(kind == 1, b, jnp.where(kind == 2, c, jnp.where(kind == 3, d, 0.0)))
    )


def source_features(row_ref, factor, rows, out_ref, slot):
    kind, source, _ = rows
    zero = jnp.zeros((TILE, FEATURES), BF16)
    out_ref[slot, 0] = zero
    out_ref[slot, PAD - 1] = zero

    def one(tile, carry):
        a = factor * (row_ref[9:10, lanes(tile)] - 0.5)
        b = factor * (row_ref[10:11, lanes(tile)] - 0.5)
        values = choose(kind, a, b, a * a + b * b, 1.0)
        out_ref[slot, tile + 1] = split_rows(values, source).T.astype(BF16)
        return carry

    lax.fori_loop(0, GX, one, 0, unroll=2)


def target_features(row_ref, tile, row_shift, col_shift, factor, rows):
    kind, _, target = rows
    a = factor * ((row_shift + 0.5) - row_ref[9:10, lanes(tile)])
    b = factor * ((col_shift + 0.5) - row_ref[10:11, lanes(tile)])
    values = choose(kind, 2.0 * a, 2.0 * b, 1.0, a * a + b * b)
    return split_rows(values, target).astype(BF16)


def fill_weights(target_ref, row_shift, feats_ref, slot, weights_ref, combo, consts, rows):
    reach, top, factor = consts
    reach = jnp.broadcast_to(reach, (16, TILE))
    top = jnp.broadcast_to(top, (16, TILE))

    def one(tile, carry):
        for k in range(3):
            wanted = target_features(target_ref, tile, float(row_shift), float(k - 1), factor, rows)
            square = lax.dot_general(
                feats_ref[slot, tile + k],
                wanted,
                (((1,), (0,)), ((), ())),
                preferred_element_type=F32,
            )
            for part in range(TILE // 16):
                here = jnp.maximum(square[part * 16 : (part + 1) * 16, :], 1e-12)
                close = jnp.maximum(reach - here * lax.rsqrt(here), 0.0)
                second = close * close
                weight = (second * second) * (top - close)
                high = weight.astype(BF16)
                low = (weight - high.astype(F32)).astype(BF16)
                base = k * 2 * TILE + part * 16
                weights_ref[combo, tile, base : base + 16, :] = high
                weights_ref[combo, tile, base + TILE : base + TILE + 16, :] = low
        return carry

    lax.fori_loop(0, GX, one, 0, unroll=2)


def spread(row_ref, out_ref, slot):
    empty = jnp.zeros((2 * ROWS, 2 * TILE), BF16)
    out_ref[slot, :, 0 : 2 * TILE] = empty
    out_ref[slot, :, (PAD - 1) * 2 * TILE :] = empty
    for tile in range(GX):
        values = row_ref[:, tile * TILE : (tile + 1) * TILE]
        high = values.astype(BF16)
        low = (values - high.astype(F32)).astype(BF16)
        both = jnp.concatenate([high, low], axis=0)
        at = (tile + 1) * 2 * TILE
        out_ref[slot, :, at : at + TILE] = both
        out_ref[slot, :, at + TILE : at + 2 * TILE] = both


def banded(spread_ref, slot, weights_ref, combo, tile):
    at = pl.multiple_of(tile * 2 * TILE, 2 * TILE)
    both = jnp.dot(
        spread_ref[slot, :, pl.ds(at, BAND)],
        weights_ref[combo, tile],
        preferred_element_type=F32,
    )
    return both[0:ROWS] + both[ROWS:]


GROUP = 4


def apply_rows(first_ref, second_ref, spread_ref, inner_ref, outer_ref, noise, out_refs):
    def group(g, carry):
        for j in range(GROUP):
            tile = g * GROUP + j
            here = lanes(tile)
            out_refs[0][:, here] = (
                noise * first_ref[:, here]
                + banded(spread_ref, 0, outer_ref, 0, tile)
                + banded(spread_ref, 1, inner_ref, 0, tile)
                + banded(spread_ref, 2, inner_ref, 1, tile)
            )
            out_refs[1][:, here] = (
                noise * second_ref[:, here]
                + banded(spread_ref, 1, inner_ref, 2, tile)
                + banded(spread_ref, 2, inner_ref, 3, tile)
                + banded(spread_ref, 3, outer_ref, 1, tile)
            )
        return carry

    lax.fori_loop(0, GX // GROUP, group, 0)


def two_sum(a, b):
    total = a + b
    part = total - a
    return total, (a - (total - part)) + (b - part)


def quick_sum(a, b):
    total = a + b
    return total, b - (total - a)


def halves(a):
    scaled = 4097.0 * a
    high = scaled - (scaled - a)
    return high, a - high


def two_product(a, b, a_halves=None, b_halves=None):
    a1, a2 = halves(a) if a_halves is None else a_halves
    b1, b2 = halves(b) if b_halves is None else b_halves
    product = a * b
    return product, ((a1 * b1 - product) + a1 * b2 + a2 * b1) + a2 * b2


class Pair:
    def __init__(self, high, low):
        self.high, self.low = high, low

    def __add__(self, other):
        total, error = two_sum(self.high, other.high)
        return Pair(*quick_sum(total, error + (self.low + other.low)))

    def __neg__(self):
        return Pair(-self.high, -self.low)

    def __sub__(self, other):
        return self + (-other)

    def __mul__(self, other):
        if not isinstance(other, Pair):
            return Pair(self.high * other, self.low * other)
        product, error = two_product(self.high, other.high)
        return Pair(*quick_sum(product, error + (self.high * other.low + self.low * other.high)))

    def __truediv__(self, other):
        first = self.high / other.high
        rest = self - other * Pair(first, jnp.zeros_like(first))
        return Pair(*quick_sum(first, rest.high / other.high))

    def where(self, keep, other):
        return Pair(jnp.where(keep, self.high, other.high), jnp.where(keep, self.low, other.low))


def grid_mask(k):
    lane = lax.broadcasted_iota(jnp.int32, (ROWS, TILE), 1)
    row = lax.broadcasted_iota(jnp.int32, (ROWS, TILE), 0)
    return lane == row + ROWS * k


def add_product(sums, a, b, a_halves, b_halves):
    product, error = two_product(a, b, a_halves, b_halves)
    total, left = two_sum(sums[0], product)
    return total, sums[1] + (left + error)


def lines(sums, first):
    placed = [jnp.zeros((ROWS, TILE), F32), jnp.zeros((ROWS, TILE), F32)]
    for k, (high, low) in enumerate(sums):
        for shift in (64, 32, 16, 8, 4, 2, 1):
            high, left = two_sum(high, pltpu.roll(high, shift, 1))
            low = (low + pltpu.roll(low, shift, 1)) + left
        high, low = quick_sum(high, low)
        mask = grid_mask(first + k)
        placed = [jnp.where(mask, high, placed[0]), jnp.where(mask, low, placed[1])]
    return [jnp.sum(p, axis=0, keepdims=True) for p in placed]


def inner_kernel(scale_ref, amp_ref, first_ref, second_ref, inner_ref, feats_ref):
    rows = feature_rows()
    consts = constants(scale_ref, amp_ref)
    source_features(first_ref, consts[2], rows, feats_ref, 0)
    source_features(second_ref, consts[2], rows, feats_ref, 1)
    fill_weights(first_ref, 0, feats_ref, 0, inner_ref, 0, consts, rows)
    fill_weights(first_ref, 1, feats_ref, 1, inner_ref, 1, consts, rows)
    fill_weights(second_ref, -1, feats_ref, 0, inner_ref, 2, consts, rows)
    fill_weights(second_ref, 0, feats_ref, 1, inner_ref, 3, consts, rows)


def outer_kernel(
    scale_ref,
    amp_ref,
    noise_ref,
    above_ref,
    first_ref,
    second_ref,
    below_ref,
    inner_ref,
    outer_ref,
    one_ref,
    two_ref,
    feats_ref,
    spread_ref,
):
    rows = feature_rows()
    consts = constants(scale_ref, amp_ref)
    source_features(above_ref, consts[2], rows, feats_ref, 0)
    source_features(below_ref, consts[2], rows, feats_ref, 1)
    fill_weights(first_ref, -1, feats_ref, 0, outer_ref, 0, consts, rows)
    fill_weights(second_ref, 1, feats_ref, 1, outer_ref, 1, consts, rows)
    for slot, ref in enumerate((above_ref, first_ref, second_ref, below_ref)):
        spread(ref, spread_ref, slot)
    apply_rows(
        first_ref, second_ref, spread_ref, inner_ref, outer_ref, noise_ref[0], (one_ref, two_ref)
    )


def product_kernel(
    noise_ref, above_ref, first_ref, second_ref, below_ref, inner_ref, outer_ref, one_ref, two_ref, spread_ref
):
    for slot, ref in enumerate((above_ref, first_ref, second_ref, below_ref)):
        spread(ref, spread_ref, slot)
    apply_rows(
        first_ref, second_ref, spread_ref, inner_ref, outer_ref, noise_ref[0], (one_ref, two_ref)
    )


def gram_kernel(b0_ref, b1_ref, f0_ref, f1_ref, g0_ref, g1_ref, sums_ref):
    zero = jnp.zeros((ROWS, TILE), F32)

    def one(tile, sums):
        sums = list(sums)
        here = lanes(tile)
        for refs in ((b0_ref, f0_ref, g0_ref), (b1_ref, f1_ref, g1_ref)):
            values = [ref[:, here] for ref in refs]
            parts = [halves(v) for v in values]
            for k, (i, j) in enumerate(((0, 0), (0, 1), (0, 2), (1, 1), (1, 2), (2, 2))):
                sums[k] = add_product(sums[k], values[i], values[j], parts[i], parts[j])
        return tuple(sums)

    high, low = lines(lax.fori_loop(0, GX, one, ((zero, zero),) * 6), 0)
    sums_ref[0:1, :] = high
    sums_ref[1:2, :] = low


def moment_kernel(
    noise_ref, sums_ref, g0_ref, g1_ref, below_ref, inner_ref, outer_ref, out_ref, spread_ref
):
    spread(g0_ref, spread_ref, 0)
    spread(g1_ref, spread_ref, 1)
    spread(below_ref, spread_ref, 2)
    noise = noise_ref[0]

    def group(g, sums):
        for j in range(GROUP):
            tile = g * GROUP + j
            here = lanes(tile)
            own0 = banded(spread_ref, 0, inner_ref, 0, tile)
            next0 = banded(spread_ref, 1, inner_ref, 1, tile)
            own1 = banded(spread_ref, 1, inner_ref, 3, tile)
            next1 = banded(spread_ref, 2, outer_ref, 1, tile)
            for ref, own, after in ((g0_ref, own0, next0), (g1_ref, own1, next1)):
                v = ref[:, here]
                image = noise * v + own + 2.0 * after
                sums = add_product(sums, v, image, halves(v), halves(image))
        return sums

    zero = jnp.zeros((ROWS, TILE), F32)
    high, low = lines((lax.fori_loop(0, GX // GROUP, group, (zero, zero)),), 6)
    both = jnp.concatenate([high + sums_ref[0:1, :], low + sums_ref[1:2, :]], axis=0)
    out_ref[...] = jnp.broadcast_to(both[None], out_ref.shape)


def finish_kernel(
    points,
    cell_ref,
    noise_ref,
    parts_ref,
    b0_ref,
    b1_ref,
    f0_ref,
    f1_ref,
    g0_ref,
    g1_ref,
    out_ref,
    quad_ref,
    grid_ref,
):
    high, low = parts_ref[:, 0, :], parts_ref[:, 1, :]
    while high.shape[0] > 8:
        half = high.shape[0] // 2
        high, left = two_sum(high[:half], high[half:])
        low = (low[:half] + low[half:]) + left
    for shift in (4, 2, 1):
        high, left = two_sum(high, pltpu.roll(high, shift, 0))
        low = (low + pltpu.roll(low, shift, 0)) + left
    high, low = quick_sum(high, low)
    bb, bf, bg, ff, fg, gg, gag = (
        Pair(high, low)
        if k == 0
        else Pair(pltpu.roll(high, TILE - ROWS * k, 1), pltpu.roll(low, TILE - ROWS * k, 1))
        for k in range(7)
    )
    zero = jnp.zeros_like(high)
    none = Pair(zero, zero)
    one = Pair(zero + 1.0, zero)
    most = 1.0 / jnp.full(high.shape, noise_ref[0], F32)

    floor = bb.high * 1e-11

    def step(square, product):
        good = (square.high > floor) & (product.high > 0.0)
        ratio = square / product.where(good, one)
        fits = ratio.high < most
        return ratio.where(fits, Pair(most, zero)).where(good, none), good

    def over(a, b, good):
        return (a / b.where(good, one)).where(good, none)

    alpha0, good0 = step(bb, bf)
    rr1 = bb - alpha0 * (bf * 2.0 - alpha0 * ff)
    beta0 = over(rr1, bb, good0)
    p0, p1 = one + beta0, -alpha0
    alpha1, good1 = step(rr1, p0 * (p0 * bf + p1 * (bg + ff)) + p1 * p1 * fg)
    r1, r2 = -(alpha0 + alpha1 * p0), -(alpha1 * p1)
    rr2 = bb + r1 * (bf * 2.0 + r1 * ff) + r2 * (bg * 2.0 + r1 * fg * 2.0 + r2 * gg)
    beta1 = over(rr2, rr1, good1)
    q0, q1, q2 = one + beta1 * p0, r1 + beta1 * p1, r2
    alpha2, good2 = step(
        rr2,
        q0 * (q0 * bf + q1 * (bg + ff) + q2 * fg * 2.0)
        + q1 * (q1 * fg + q2 * gg * 2.0)
        + q2 * q2 * gag,
    )
    alpha2 = alpha2.where(good1, none)
    on_b = alpha0 + alpha1 * p0 + alpha2 * q0
    on_f = alpha1 * p1 + alpha2 * q1
    on_g = alpha2 * q2
    quad = on_b * bb + on_f * bf + on_g * bg
    quad_ref[...] = (quad.high / points)[0:1, 0:RHS]
    mask = grid_mask(0)
    c0, c1, c2 = (
        jnp.broadcast_to(
            jnp.sum(
                jnp.where(mask, jnp.concatenate([c.high, c.high], axis=0), 0.0), axis=1, keepdims=True
            ),
            (ROWS, TILE),
        )
        for c in (on_b, on_f, on_g)
    )
    for half, (b_ref, f_ref, g_ref) in enumerate(
        ((b0_ref, f0_ref, g0_ref), (b1_ref, f1_ref, g1_ref))
    ):
        for tile in range(GX):
            here = slice(tile * TILE, (tile + 1) * TILE)
            grid_ref[half * GX + tile] = (
                c0 * b_ref[:, here] + c1 * f_ref[:, here] + c2 * g_ref[:, here]
            )
    for s in range(cell_ref.shape[0]):
        out_ref[:, s * TILE : (s + 1) * TILE] = grid_ref[cell_ref[s], 0:RHS, :]


def shards(offsets, tile_cell, probes, target, lengthscale, amplitude, noise):
    size = lax.axis_size("rows")
    points = size * tile_cell.shape[0] * TILE
    down = [(i, i + 1) for i in range(size - 1)]
    up = [(i + 1, i) for i in range(size - 1)]

    first, second = call(
        pack_kernel, "pack", (grid_row(), grid_row()), [SMEM, VMEM, VMEM, VMEM], flops=1 << 20
    )(tile_cell, offsets, probes, target.reshape(1, -1))
    above = lax.ppermute(second, "rows", down)
    below = lax.ppermute(first, "rows", up)
    feats = pltpu.VMEM((2, PAD, TILE, FEATURES), BF16)
    inner = call(
        inner_kernel,
        "inner",
        pltpu.VMEM((4, GX, BAND, TILE), BF16),
        [SMEM, SMEM, VMEM, VMEM],
        [feats],
        flops=1 << 30,
    )(lengthscale, amplitude, first, second)
    spread4 = pltpu.VMEM((4, 2 * ROWS, PAD * 2 * TILE), BF16)
    outer, f0, f1 = call(
        outer_kernel,
        "outer",
        (pltpu.VMEM((2, GX, BAND, TILE), BF16), grid_row(), grid_row()),
        [SMEM, SMEM, SMEM, VMEM, VMEM, VMEM, VMEM, VMEM],
        [feats, spread4],
        flops=1 << 30,
    )(lengthscale, amplitude, noise, above, first, second, below, inner)
    f_above = lax.ppermute(f1, "rows", down)
    f_below = lax.ppermute(f0, "rows", up)
    g0, g1 = call(
        product_kernel,
        "product",
        (grid_row(), grid_row()),
        [SMEM] + [VMEM] * 6,
        [spread4],
        flops=1 << 30,
    )(noise, f_above, f0, f1, f_below, inner, outer)
    g_below = lax.ppermute(g0, "rows", up)
    sums = call(
        gram_kernel, "gram", jax.ShapeDtypeStruct((2, TILE), F32), [VMEM] * 6, flops=1 << 28
    )(first, second, f0, f1, g0, g1)
    parts = call(
        moment_kernel,
        "moment",
        jax.ShapeDtypeStruct((size, 2, TILE), F32),
        [SMEM] + [VMEM] * 6,
        [pltpu.VMEM((3, 2 * ROWS, PAD * 2 * TILE), BF16)],
        flops=1 << 29,
    )(noise, sums, g0, g1, g_below, inner, outer)
    parts = lax.all_to_all(parts, "rows", split_axis=0, concat_axis=0, tiled=True)

    def finish(*refs):
        finish_kernel(float(points), *refs)

    solutions, quad = call(
        finish,
        "finish",
        (
            jax.ShapeDtypeStruct((RHS, tile_cell.shape[0] * TILE), F32),
            jax.ShapeDtypeStruct((1, RHS), F32),
        ),
        [SMEM, SMEM] + [VMEM] * 7,
        [pltpu.VMEM((tile_cell.shape[0], ROWS, TILE), F32)],
        flops=1 << 20,
    )(tile_cell, noise, parts, first, second, f0, f1, g0, g1)
    return (solutions, quad.reshape(RHS))


def solution(mesh):
    return jax.shard_map(
        shards,
        mesh=mesh,
        in_specs=(
            P(None, "rows"),
            P("rows"),
            P(None, "rows"),
            P("rows"),
            P("hyp"),
            P("hyp"),
            P("hyp"),
        ),
        out_specs=(P("hyp", "rows"), P("hyp")),
        check_vma=False,
    )
```

```python
import jax
import jax.numpy as jnp
from jax import lax
from jax.experimental import pallas as pl
from jax.experimental.pallas import tpu as pltpu
from jax.sharding import PartitionSpec as P

TILE = 128
GX = 16
RHS = 9
ROWS = 16
WIDE = GX * TILE
FEATURES = 32
PAD = GX + 2
BAND = 3 * 2 * TILE
F32 = jnp.float32
BF16 = jnp.bfloat16
TINY = 1e-30

VMEM = pl.BlockSpec(memory_space=pltpu.VMEM)
HBM = pl.BlockSpec(memory_space=pltpu.HBM)
SMEM = pl.BlockSpec(memory_space=pltpu.SMEM)
REACH, TOP, FACTOR, NOISE = range(4)


def call(kernel, name, out_shape, in_specs, scratch=(), flops=0, limit=12):
    return pl.pallas_call(
        kernel,
        name=name,
        out_shape=out_shape,
        in_specs=in_specs,
        out_specs=jax.tree.map(lambda _: VMEM, out_shape),
        scratch_shapes=list(scratch),
        cost_estimate=pl.CostEstimate(flops=flops, bytes_accessed=1 << 20, transcendentals=0),
        compiler_params=pltpu.CompilerParams(vmem_limit_bytes=int(limit * 2**20)),
    )


def grid_row():
    return jax.ShapeDtypeStruct((ROWS, WIDE), F32)


def spread_row():
    return pltpu.VMEM((2 * ROWS, PAD * 2 * TILE), BF16)


def weight_rows(count):
    return pltpu.VMEM((count, GX, BAND, TILE), BF16)


def feature_tiles():
    return pltpu.VMEM((PAD, TILE, FEATURES), BF16)


def lanes(tile, width=TILE):
    return pl.ds(pl.multiple_of(tile * width, width), width)


def pack_kernel(
    cell_hbm,
    offsets_hbm,
    probes_hbm,
    target_hbm,
    scale_ref,
    amp_ref,
    noise_ref,
    first_ref,
    second_ref,
    consts_ref,
    cell_ref,
    offsets_ref,
    probes_ref,
    target_ref,
    sems,
):
    copies = [
        pltpu.make_async_copy(source, dest, sems.at[i])
        for i, (source, dest) in enumerate(
            (
                (cell_hbm, cell_ref),
                (offsets_hbm, offsets_ref),
                (probes_hbm, probes_ref),
                (target_hbm, target_ref),
            )
        )
    ]
    for copy in copies:
        copy.start()
    for copy in copies:
        copy.wait()
    filler = jnp.zeros((ROWS - RHS - 2, TILE), F32)
    for s in range(cell_ref.shape[0]):
        here = slice(s * TILE, (s + 1) * TILE)
        signs = 2.0 * probes_ref[:, here].astype(F32) - 1.0
        rest = jnp.concatenate([target_ref[:, here], offsets_ref[:, here], filler], axis=0)
        cell = cell_ref[s]

        def put(ref, column, signs=signs, rest=rest):
            ref[0:8, lanes(column)] = signs
            ref[8:16, lanes(column)] = rest

        @pl.when(cell < GX)
        def _():
            put(first_ref, cell)

        @pl.when(cell >= GX)
        def _():
            put(second_ref, cell - GX)

    amp = jnp.full((1, TILE), amp_ref[0], F32)
    reach = jnp.exp(0.2 * jnp.log(4.0 * amp))
    square = reach * reach
    consts_ref[REACH : REACH + 1, :] = reach
    consts_ref[TOP : TOP + 1, :] = 5.0 * amp / (square * square)
    consts_ref[FACTOR : FACTOR + 1, :] = reach / jnp.full((1, TILE), scale_ref[0], F32)
    consts_ref[NOISE : NOISE + 1, :] = jnp.full((1, TILE), noise_ref[0], F32)


def constant(consts_ref, which):
    return consts_ref[which : which + 1, :]


def split_rows(values, level):
    first = values.astype(BF16).astype(F32)
    rest = values - first
    second = rest.astype(BF16).astype(F32)
    third = rest - second
    return jnp.where(level == 0, first, jnp.where(level == 1, second, third))


def feature_rows():
    row = lax.broadcasted_iota(jnp.int32, (FEATURES, TILE), 0)

    def level(order):
        out = jnp.zeros_like(row)
        for k, v in enumerate(order):
            if v:
                out = jnp.where(row == k, v, out)
        return out

    source = level([0, 0, 1, 1, 0, 2] * 2 + [0, 1, 2] + [0, 0, 0])
    target = level([0, 1, 0, 1, 2, 0] * 2 + [0, 0, 0] + [0, 1, 2])
    kind = jnp.where(row < 6, 0, jnp.where(row < 12, 1, jnp.where(row < 15, 2, jnp.where(row < 18, 3, 4))))
    return kind, source, target


def choose(kind, a, b, c, d):
    return jnp.where(
        kind == 0, a, jnp.where(kind == 1, b, jnp.where(kind == 2, c, jnp.where(kind == 3, d, 0.0)))
    )


def source_features(row_ref, factor, rows, out_ref):
    kind, source, _ = rows
    zero = jnp.zeros((TILE, FEATURES), BF16)
    out_ref[0] = zero
    out_ref[PAD - 1] = zero

    def one(tile, carry):
        a = factor * (row_ref[9:10, lanes(tile)] - 0.5)
        b = factor * (row_ref[10:11, lanes(tile)] - 0.5)
        values = choose(kind, a, b, a * a + b * b, 1.0)
        out_ref[tile + 1] = split_rows(values, source).T.astype(BF16)
        return carry

    lax.fori_loop(0, GX, one, 0, unroll=4)


def target_features(row_ref, tile, row_shift, col_shift, factor, rows):
    kind, _, target = rows
    a = factor * ((row_shift + 0.5) - row_ref[9:10, lanes(tile)])
    b = factor * ((col_shift + 0.5) - row_ref[10:11, lanes(tile)])
    values = choose(kind, 2.0 * a, 2.0 * b, 1.0, a * a + b * b)
    return split_rows(values, target).astype(BF16)


def fill_weights(target_ref, row_shift, feats_ref, weights_ref, combo, consts_ref, rows):
    factor = constant(consts_ref, FACTOR)
    reach = jnp.broadcast_to(constant(consts_ref, REACH), (16, TILE))
    top = jnp.broadcast_to(constant(consts_ref, TOP), (16, TILE))

    def one(tile, carry):
        for k in range(3):
            wanted = target_features(target_ref, tile, float(row_shift), float(k - 1), factor, rows)
            square = lax.dot_general(
                feats_ref[tile + k],
                wanted,
                (((1,), (0,)), ((), ())),
                preferred_element_type=F32,
            )
            for part in range(TILE // 16):
                here = jnp.maximum(square[part * 16 : (part + 1) * 16, :], 1e-12)
                close = jnp.maximum(reach - here * lax.rsqrt(here), 0.0)
                second = close * close
                weight = (second * second) * (top - close)
                high = weight.astype(BF16)
                low = (weight - high.astype(F32)).astype(BF16)
                base = k * 2 * TILE + part * 16
                weights_ref[combo, tile, base : base + 16, :] = high
                weights_ref[combo, tile, base + TILE : base + TILE + 16, :] = low
        return carry

    lax.fori_loop(0, GX, one, 0, unroll=8)


def spread_ends(out_ref):
    empty = jnp.zeros((2 * ROWS, 2 * TILE), BF16)
    out_ref[:, 0 : 2 * TILE] = empty
    out_ref[:, (PAD - 1) * 2 * TILE :] = empty


def spread_tile(values, out_ref, tile):
    high = values.astype(BF16)
    low = (values - high.astype(F32)).astype(BF16)
    both = jnp.concatenate([high, low], axis=0)
    at = pl.multiple_of((tile + 1) * 2 * TILE, 2 * TILE)
    out_ref[:, pl.ds(at, 2 * TILE)] = jnp.concatenate([both, both], axis=1)


def spread(row_ref, out_ref):
    spread_ends(out_ref)
    for tile in range(GX):
        spread_tile(row_ref[:, tile * TILE : (tile + 1) * TILE], out_ref, tile)


def banded(spread_ref, weights_ref, combo, tile):
    at = pl.multiple_of(tile * 2 * TILE, 2 * TILE)
    both = jnp.dot(
        spread_ref[:, pl.ds(at, BAND)],
        weights_ref[combo, tile],
        preferred_element_type=F32,
    )
    return both[0:ROWS] + both[ROWS:]


GROUP = 8


def apply_row(own_ref, terms, consts_ref, out_ref, out_spread_ref):
    noise = constant(consts_ref, NOISE)
    spread_ends(out_spread_ref)

    def group(g, carry):
        for j in range(GROUP):
            tile = g * GROUP + j
            here = lanes(tile)
            total = noise * own_ref[:, here]
            for term in terms:
                total = total + banded(*term, tile)
            out_ref[:, here] = total
            spread_tile(total, out_spread_ref, tile)
        return carry

    lax.fori_loop(0, GX // GROUP, group, 0)


def two_sum(a, b):
    total = a + b
    part = total - a
    return total, (a - (total - part)) + (b - part)


def quick_sum(a, b):
    total = a + b
    return total, b - (total - a)


def halves(a):
    scaled = 4097.0 * a
    high = scaled - (scaled - a)
    return high, a - high


def two_product(a, b, a_halves=None, b_halves=None):
    a1, a2 = halves(a) if a_halves is None else a_halves
    b1, b2 = halves(b) if b_halves is None else b_halves
    product = a * b
    return product, ((a1 * b1 - product) + a1 * b2 + a2 * b1) + a2 * b2


class Pair:
    def __init__(self, high, low):
        self.high, self.low = high, low

    def __add__(self, other):
        total, error = two_sum(self.high, other.high)
        return Pair(*quick_sum(total, error + (self.low + other.low)))

    def __neg__(self):
        return Pair(-self.high, -self.low)

    def __sub__(self, other):
        return self + (-other)

    def __mul__(self, other):
        if not isinstance(other, Pair):
            return Pair(self.high * other, self.low * other)
        product, error = two_product(self.high, other.high)
        return Pair(*quick_sum(product, error + (self.high * other.low + self.low * other.high)))

    def __truediv__(self, other):
        first = self.high / other.high
        rest = self - other * Pair(first, jnp.zeros_like(first))
        return Pair(*quick_sum(first, rest.high / other.high))

    def where(self, keep, other):
        return Pair(jnp.where(keep, self.high, other.high), jnp.where(keep, self.low, other.low))


def grid_mask(k):
    lane = lax.broadcasted_iota(jnp.int32, (ROWS, TILE), 1)
    row = lax.broadcasted_iota(jnp.int32, (ROWS, TILE), 0)
    return lane == row + ROWS * k


def add_product(sums, a, b, a_halves, b_halves):
    product, error = two_product(a, b, a_halves, b_halves)
    total, left = two_sum(sums[0], product)
    return total, sums[1] + (left + error)


def lines(sums, first):
    placed = [jnp.zeros((ROWS, TILE), F32), jnp.zeros((ROWS, TILE), F32)]
    for k, (high, low) in enumerate(sums):
        for shift in (64, 32, 16, 8, 4, 2, 1):
            high, left = two_sum(high, pltpu.roll(high, shift, 1))
            low = (low + pltpu.roll(low, shift, 1)) + left
        high, low = quick_sum(high, low)
        mask = grid_mask(first + k)
        placed = [jnp.where(mask, high, placed[0]), jnp.where(mask, low, placed[1])]
    return [jnp.sum(p, axis=0, keepdims=True) for p in placed]


def inner_kernel(slot, first_ref, second_ref, consts_ref, weights_ref, spread_ref, feats_ref):
    rows = feature_rows()
    own_ref = (first_ref, second_ref)[slot]
    source_features(own_ref, constant(consts_ref, FACTOR), rows, feats_ref)
    fill_weights(first_ref, slot, feats_ref, weights_ref, 0, consts_ref, rows)
    fill_weights(second_ref, slot - 1, feats_ref, weights_ref, 1, consts_ref, rows)
    spread(own_ref, spread_ref)


def outer_kernel(
    slot,
    other_ref,
    own_ref,
    consts_ref,
    left_ref,
    right_ref,
    spread0_ref,
    spread1_ref,
    weights_ref,
    out_ref,
    out_spread_ref,
    feats_ref,
    spread_ref,
):
    rows = feature_rows()
    source_features(other_ref, constant(consts_ref, FACTOR), rows, feats_ref)
    fill_weights(own_ref, 2 * slot - 1, feats_ref, weights_ref, 0, consts_ref, rows)
    spread(other_ref, spread_ref)
    terms = ((spread_ref, weights_ref, 0), (spread0_ref, left_ref, slot), (spread1_ref, right_ref, slot))
    apply_row(own_ref, terms, consts_ref, out_ref, out_spread_ref)


def product_kernel(
    slot,
    other_ref,
    own_ref,
    consts_ref,
    left_ref,
    right_ref,
    weights_ref,
    spread0_ref,
    spread1_ref,
    out_ref,
    out_spread_ref,
    spread_ref,
):
    spread(other_ref, spread_ref)
    terms = ((spread_ref, weights_ref, 0), (spread0_ref, left_ref, slot), (spread1_ref, right_ref, slot))
    apply_row(own_ref, terms, consts_ref, out_ref, out_spread_ref)


def gram_kernel(
    b0_ref,
    b1_ref,
    f0_ref,
    f1_ref,
    g0_ref,
    g1_ref,
    consts_ref,
    left_ref,
    right_ref,
    spread0_ref,
    spread1_ref,
    sums_ref,
):
    zero = jnp.zeros((ROWS, TILE), F32)
    noise = constant(consts_ref, NOISE)

    def group(g, sums):
        sums = list(sums)
        for j in range(4):
            tile = g * 4 + j
            here = lanes(tile)
            for half, refs in enumerate(((b0_ref, f0_ref, g0_ref), (b1_ref, f1_ref, g1_ref))):
                values = [ref[:, here] for ref in refs]
                parts = [halves(v) for v in values]
                for k, (i, j2) in enumerate(((0, 0), (0, 1), (0, 2), (1, 1), (1, 2), (2, 2))):
                    sums[k] = add_product(sums[k], values[i], values[j2], parts[i], parts[j2])
                image = noise * values[2]
                if half == 0:
                    image = image + banded(spread0_ref, left_ref, 0, tile)
                    image = image + 2.0 * banded(spread1_ref, right_ref, 0, tile)
                else:
                    image = image + banded(spread1_ref, right_ref, 1, tile)
                sums[6] = add_product(sums[6], values[2], image, parts[2], halves(image))
        return tuple(sums)

    high, low = lines(lax.fori_loop(0, GX // 4, group, ((zero, zero),) * 7), 0)
    sums_ref[0:1, :] = high
    sums_ref[1:2, :] = low


def moment_kernel(sums_ref, below_ref, own_ref, weights_ref, out_ref, spread_ref):
    spread(below_ref, spread_ref)

    def group(g, sums):
        for j in range(GROUP):
            tile = g * GROUP + j
            v = own_ref[:, lanes(tile)]
            image = 2.0 * banded(spread_ref, weights_ref, 0, tile)
            sums = add_product(sums, v, image, halves(v), halves(image))
        return sums

    zero = jnp.zeros((ROWS, TILE), F32)
    high, low = lines((lax.fori_loop(0, GX // GROUP, group, (zero, zero)),), 6)
    total, left = two_sum(sums_ref[0:1, :], high)
    both = jnp.concatenate([total, left + (low + sums_ref[1:2, :])], axis=0)
    out_ref[...] = jnp.broadcast_to(both[None], out_ref.shape)


def finish_kernel(
    points,
    cell_hbm,
    consts_ref,
    parts_ref,
    b0_ref,
    b1_ref,
    f0_ref,
    f1_ref,
    g0_ref,
    g1_ref,
    out_ref,
    quad_ref,
    cell_ref,
    grid_ref,
    sem,
):
    copy = pltpu.make_async_copy(cell_hbm, cell_ref, sem)
    copy.start()
    high, low = parts_ref[:, 0, :], parts_ref[:, 1, :]
    while high.shape[0] > 8:
        half = high.shape[0] // 2
        high, left = two_sum(high[:half], high[half:])
        low = (low[:half] + low[half:]) + left
    for shift in (4, 2, 1):
        high, left = two_sum(high, pltpu.roll(high, shift, 0))
        low = (low + pltpu.roll(low, shift, 0)) + left
    high, low = quick_sum(high, low)
    bb, bf, bg, ff, fg, gg, gag = (
        Pair(high, low)
        if k == 0
        else Pair(pltpu.roll(high, TILE - ROWS * k, 1), pltpu.roll(low, TILE - ROWS * k, 1))
        for k in range(7)
    )
    zero = jnp.zeros_like(high)
    none = Pair(zero, zero)
    one = Pair(zero + 1.0, zero)
    most = jnp.broadcast_to(1.0 / constant(consts_ref, NOISE), high.shape)

    floor = bb.high * 1e-11

    def step(square, product):
        good = (square.high > floor) & (product.high > 0.0)
        ratio = square / product.where(good, one)
        fits = ratio.high < most
        return ratio.where(fits, Pair(most, zero)).where(good, none), good

    def over(a, b, good):
        return (a / b.where(good, one)).where(good, none)

    alpha0, good0 = step(bb, bf)
    rr1 = bb - alpha0 * (bf * 2.0 - alpha0 * ff)
    beta0 = over(rr1, bb, good0)
    p0, p1 = one + beta0, -alpha0
    alpha1, good1 = step(rr1, p0 * (p0 * bf + p1 * (bg + ff)) + p1 * p1 * fg)
    r1, r2 = -(alpha0 + alpha1 * p0), -(alpha1 * p1)
    rr2 = bb + r1 * (bf * 2.0 + r1 * ff) + r2 * (bg * 2.0 + r1 * fg * 2.0 + r2 * gg)
    beta1 = over(rr2, rr1, good1)
    q0, q1, q2 = one + beta1 * p0, r1 + beta1 * p1, r2
    alpha2, good2 = step(
        rr2,
        q0 * (q0 * bf + q1 * (bg + ff) + q2 * fg * 2.0)
        + q1 * (q1 * fg + q2 * gg * 2.0)
        + q2 * q2 * gag,
    )
    alpha2 = alpha2.where(good1, none)
    on_b = alpha0 + alpha1 * p0 + alpha2 * q0
    on_f = alpha1 * p1 + alpha2 * q1
    on_g = alpha2 * q2
    quad = on_b * bb + on_f * bf + on_g * bg
    quad_ref[...] = (quad.high / points)[0:1, 0:RHS]
    mask = grid_mask(0)
    c0, c1, c2 = (
        jnp.broadcast_to(
            jnp.sum(
                jnp.where(mask, jnp.concatenate([c.high, c.high], axis=0), 0.0), axis=1, keepdims=True
            ),
            (ROWS, TILE),
        )
        for c in (on_b, on_f, on_g)
    )
    for half, (b_ref, f_ref, g_ref) in enumerate(
        ((b0_ref, f0_ref, g0_ref), (b1_ref, f1_ref, g1_ref))
    ):
        for tile in range(GX):
            here = slice(tile * TILE, (tile + 1) * TILE)
            grid_ref[half * GX + tile] = (
                c0 * b_ref[:, here] + c1 * f_ref[:, here] + c2 * g_ref[:, here]
            )
    copy.wait()
    for s in range(cell_ref.shape[0]):
        out_ref[:, s * TILE : (s + 1) * TILE] = grid_ref[cell_ref[s], 0:RHS, :]


def shards(offsets, tile_cell, probes, target, lengthscale, amplitude, noise):
    size = lax.axis_size("rows")
    points = size * tile_cell.shape[0] * TILE
    down = [(i, i + 1) for i in range(size - 1)]
    up = [(i + 1, i) for i in range(size - 1)]

    tiles = tile_cell.shape[0]
    first, second, consts = call(
        pack_kernel,
        "pack",
        (pltpu.VMEM((ROWS, WIDE), F32), pltpu.VMEM((ROWS, WIDE), F32), pltpu.VMEM((8, TILE), F32)),
        [HBM] * 4 + [SMEM] * 3,
        [
            pltpu.SMEM((tiles,), jnp.int32),
            pltpu.VMEM((2, tiles * TILE), F32),
            pltpu.VMEM((8, tiles * TILE), jnp.int32),
            pltpu.VMEM((1, tiles * TILE), F32),
            pltpu.SemaphoreType.DMA((4,)),
        ],
        flops=1 << 20,
        limit=60.5,
    )(
        tile_cell,
        offsets,
        probes,
        target.reshape(1, -1),
        lengthscale,
        amplitude,
        noise,
    )

    def inner(slot):
        return call(
            lambda *refs: inner_kernel(slot, *refs),
            f"inner{slot}",
            (weight_rows(2), spread_row()),
            [VMEM] * 3,
            [feature_tiles()],
            flops=1 << 30,
        )(first, second, consts)

    def outer(slot, other, own):
        return call(
            lambda *refs: outer_kernel(slot, *refs),
            f"outer{slot}",
            (weight_rows(1), grid_row(), spread_row()),
            [VMEM] * 7,
            [feature_tiles(), spread_row()],
            flops=1 << 30,
        )(other, own, consts, left, right, b0_spread, b1_spread)

    def product(slot, other, own, weights):
        return call(
            lambda *refs: product_kernel(slot, *refs),
            f"product{slot}",
            (grid_row(), spread_row()),
            [VMEM] * 8,
            [spread_row()],
            flops=1 << 29,
        )(other, own, consts, left, right, weights, f0_spread, f1_spread)

    above = lax.ppermute(second, "rows", down)
    left, b0_spread = inner(0)
    gated, left = lax.optimization_barrier((first, left))
    below = lax.ppermute(gated, "rows", up)
    right, b1_spread = inner(1)
    over, f0, f0_spread = outer(0, above, first)
    f_below = lax.ppermute(f0, "rows", up)
    under, f1, f1_spread = outer(1, below, second)
    f_above = lax.ppermute(f1, "rows", down)
    g1, g1_spread = product(1, f_below, f1, under)
    g0, g0_spread = product(0, f_above, f0, over)
    g_below = lax.ppermute(g0, "rows", up)
    sums = call(
        gram_kernel, "gram", jax.ShapeDtypeStruct((2, TILE), F32), [VMEM] * 11, flops=1 << 29
    )(first, second, f0, f1, g0, g1, consts, left, right, g0_spread, g1_spread)
    parts = call(
        moment_kernel,
        "moment",
        jax.ShapeDtypeStruct((size, 2, TILE), F32),
        [VMEM] * 4,
        [spread_row()],
        flops=1 << 29,
    )(sums, g_below, g1, under)
    parts = lax.all_to_all(parts, "rows", split_axis=0, concat_axis=0, tiled=True)

    solutions, quad = call(
        lambda *refs: finish_kernel(float(points), *refs),
        "finish",
        (
            jax.ShapeDtypeStruct((RHS, tiles * TILE), F32),
            jax.ShapeDtypeStruct((1, RHS), F32),
        ),
        [HBM] + [VMEM] * 8,
        [
            pltpu.SMEM((tiles,), jnp.int32),
            pltpu.VMEM((tiles, ROWS, TILE), F32),
            pltpu.SemaphoreType.DMA,
        ],
        flops=1 << 20,
    )(tile_cell, consts, parts, first, second, f0, f1, g0, g1)
    return (solutions, quad.reshape(RHS))


def solution(mesh):
    return jax.shard_map(
        shards,
        mesh=mesh,
        in_specs=(
            P(None, "rows"),
            P("rows"),
            P(None, "rows"),
            P("rows"),
            P("hyp"),
            P("hyp"),
            P("hyp"),
        ),
        out_specs=(P("hyp", "rows"), P("hyp")),
        check_vma=False,
    )
```

```python
import jax
import jax.numpy as jnp
from jax import lax
from jax.experimental import pallas as pl
from jax.experimental.pallas import tpu as pltpu
from jax.sharding import PartitionSpec as P

TILE = 128
GX = 16
RHS = 9
ROWS = 16
WIDE = GX * TILE
FEATURES = 32
PAD = GX + 2
BAND = 3 * 2 * TILE
F32 = jnp.float32
BF16 = jnp.bfloat16
TINY = 1e-30

VMEM = pl.BlockSpec(memory_space=pltpu.VMEM)
HBM = pl.BlockSpec(memory_space=pltpu.HBM)
SMEM = pl.BlockSpec(memory_space=pltpu.SMEM)
REACH, TOP, FACTOR, NOISE = range(4)


def call(kernel, name, out_shape, in_specs, scratch=(), flops=0, limit=12):
    return pl.pallas_call(
        kernel,
        name=name,
        out_shape=out_shape,
        in_specs=in_specs,
        out_specs=jax.tree.map(lambda _: VMEM, out_shape),
        scratch_shapes=list(scratch),
        cost_estimate=pl.CostEstimate(flops=flops, bytes_accessed=1 << 20, transcendentals=0),
        compiler_params=pltpu.CompilerParams(vmem_limit_bytes=int(limit * 2**20)),
    )


def grid_row():
    return jax.ShapeDtypeStruct((ROWS, WIDE), F32)


def spread_row(rows=2 * ROWS):
    return pltpu.VMEM((rows, PAD * 2 * TILE), BF16)


def weight_rows(count):
    return pltpu.VMEM((count, GX, BAND, TILE), BF16)


def feature_tiles():
    return pltpu.VMEM((PAD, TILE, FEATURES), BF16)


def lanes(tile, width=TILE):
    return pl.ds(pl.multiple_of(tile * width, width), width)


def pack_kernel(
    cell_hbm,
    offsets_hbm,
    probes_hbm,
    target_hbm,
    scale_ref,
    amp_ref,
    noise_ref,
    first_ref,
    second_ref,
    consts_ref,
    cell_ref,
    offsets_ref,
    probes_ref,
    target_ref,
    sems,
):
    copies = [
        pltpu.make_async_copy(source, dest, sems.at[i])
        for i, (source, dest) in enumerate(
            (
                (cell_hbm, cell_ref),
                (offsets_hbm, offsets_ref),
                (probes_hbm, probes_ref),
                (target_hbm, target_ref),
            )
        )
    ]
    for copy in copies:
        copy.start()
    for copy in copies:
        copy.wait()
    filler = jnp.zeros((ROWS - RHS - 2, TILE), F32)
    for s in range(cell_ref.shape[0]):
        here = slice(s * TILE, (s + 1) * TILE)
        signs = 2.0 * probes_ref[:, here].astype(F32) - 1.0
        rest = jnp.concatenate([target_ref[:, here], offsets_ref[:, here], filler], axis=0)
        cell = cell_ref[s]

        def put(ref, column, signs=signs, rest=rest):
            ref[0:8, lanes(column)] = signs
            ref[8:16, lanes(column)] = rest

        @pl.when(cell < GX)
        def _():
            put(first_ref, cell)

        @pl.when(cell >= GX)
        def _():
            put(second_ref, cell - GX)

    amp = jnp.full((1, TILE), amp_ref[0], F32)
    reach = jnp.exp(0.2 * jnp.log(4.0 * amp))
    square = reach * reach
    consts_ref[REACH : REACH + 1, :] = reach
    consts_ref[TOP : TOP + 1, :] = 5.0 * amp / (square * square)
    consts_ref[FACTOR : FACTOR + 1, :] = reach / jnp.full((1, TILE), scale_ref[0], F32)
    consts_ref[NOISE : NOISE + 1, :] = jnp.full((1, TILE), noise_ref[0], F32)


def constant(consts_ref, which):
    return consts_ref[which : which + 1, :]


def split_rows(values, level):
    first = values.astype(BF16).astype(F32)
    rest = values - first
    second = rest.astype(BF16).astype(F32)
    third = rest - second
    return jnp.where(level == 0, first, jnp.where(level == 1, second, third))


def feature_rows():
    row = lax.broadcasted_iota(jnp.int32, (FEATURES, TILE), 0)

    def level(order):
        out = jnp.zeros_like(row)
        for k, v in enumerate(order):
            if v:
                out = jnp.where(row == k, v, out)
        return out

    source = level([0, 0, 1, 1, 0, 2] * 2 + [0, 1, 2] + [0, 0, 0])
    target = level([0, 1, 0, 1, 2, 0] * 2 + [0, 0, 0] + [0, 1, 2])
    kind = jnp.where(row < 6, 0, jnp.where(row < 12, 1, jnp.where(row < 15, 2, jnp.where(row < 18, 3, 4))))
    return kind, source, target


def choose(kind, a, b, c, d):
    return jnp.where(
        kind == 0, a, jnp.where(kind == 1, b, jnp.where(kind == 2, c, jnp.where(kind == 3, d, 0.0)))
    )


def source_features(row_ref, factor, rows, out_ref):
    kind, source, _ = rows
    zero = jnp.zeros((TILE, FEATURES), BF16)
    out_ref[0] = zero
    out_ref[PAD - 1] = zero

    def one(tile, carry):
        a = factor * (row_ref[9:10, lanes(tile)] - 0.5)
        b = factor * (row_ref[10:11, lanes(tile)] - 0.5)
        values = choose(kind, a, b, a * a + b * b, 1.0)
        out_ref[tile + 1] = split_rows(values, source).T.astype(BF16)
        return carry

    lax.fori_loop(0, GX, one, 0, unroll=8)


def target_features(row_ref, tile, row_shift, col_shift, factor, rows):
    kind, _, target = rows
    a = factor * ((row_shift + 0.5) - row_ref[9:10, lanes(tile)])
    b = factor * ((col_shift + 0.5) - row_ref[10:11, lanes(tile)])
    values = choose(kind, 2.0 * a, 2.0 * b, 1.0, a * a + b * b)
    return split_rows(values, target).astype(BF16)


def fill_weights(target_ref, row_shift, feats_ref, weights_ref, combo, consts_ref, rows):
    factor = constant(consts_ref, FACTOR)
    reach = jnp.broadcast_to(constant(consts_ref, REACH), (16, TILE))
    top = jnp.broadcast_to(constant(consts_ref, TOP), (16, TILE))

    def one(tile, carry):
        for k in range(3):
            wanted = target_features(target_ref, tile, float(row_shift), float(k - 1), factor, rows)
            square = lax.dot_general(
                feats_ref[tile + k],
                wanted,
                (((1,), (0,)), ((), ())),
                preferred_element_type=F32,
            )
            for part in range(TILE // 16):
                here = jnp.maximum(square[part * 16 : (part + 1) * 16, :], 1e-12)
                close = jnp.maximum(reach - here * lax.rsqrt(here), 0.0)
                second = close * close
                weight = (second * second) * (top - close)
                high = weight.astype(BF16)
                low = (weight - high.astype(F32)).astype(BF16)
                base = k * 2 * TILE + part * 16
                weights_ref[combo, tile, base : base + 16, :] = high
                weights_ref[combo, tile, base + TILE : base + TILE + 16, :] = low
        return carry

    lax.fori_loop(0, GX, one, 0, unroll=8)


def spread_ends(out_ref):
    empty = jnp.zeros((2 * ROWS, 2 * TILE), BF16)
    out_ref[:, 0 : 2 * TILE] = empty
    out_ref[:, (PAD - 1) * 2 * TILE :] = empty


def spread_tile(values, out_ref, tile):
    high = values.astype(BF16)
    low = (values - high.astype(F32)).astype(BF16)
    both = jnp.concatenate([high, low], axis=0)
    at = pl.multiple_of((tile + 1) * 2 * TILE, 2 * TILE)
    out_ref[:, pl.ds(at, 2 * TILE)] = jnp.concatenate([both, both], axis=1)


def spread(row_ref, out_ref):
    spread_ends(out_ref)
    for tile in range(GX):
        spread_tile(row_ref[:, tile * TILE : (tile + 1) * TILE], out_ref, tile)


def spread_sides(row_ref, out_ref):
    empty = jnp.zeros((ROWS, 2 * TILE), BF16)
    out_ref[:, 0 : 2 * TILE] = empty
    out_ref[:, (PAD - 1) * 2 * TILE :] = empty
    row = lax.broadcasted_iota(jnp.int32, (8, TILE), 0)
    for tile in range(GX):
        here = slice(tile * TILE, (tile + 1) * TILE)
        target = row_ref[8:9, here]
        high = target.astype(BF16).astype(F32)
        rest = jnp.where(row == 0, high, jnp.where(row == 1, target - high, 0.0))
        both = jnp.concatenate([row_ref[0:8, here], rest], axis=0).astype(BF16)
        at = (tile + 1) * 2 * TILE
        out_ref[:, at : at + 2 * TILE] = jnp.concatenate([both, both], axis=1)


def banded(spread_ref, weights_ref, combo, tile):
    at = pl.multiple_of(tile * 2 * TILE, 2 * TILE)
    return jnp.dot(
        spread_ref[:, pl.ds(at, BAND)],
        weights_ref[combo, tile],
        preferred_element_type=F32,
    )


def joined(both):
    if both.shape[0] == 2 * ROWS:
        return both[0:ROWS] + both[ROWS:]
    row = lax.broadcasted_iota(jnp.int32, both.shape, 0)
    return both + jnp.where(row == 8, pltpu.roll(both, ROWS - 1, 0), 0.0)


GROUP = 16


def apply_row(own_ref, terms, consts_ref, out_ref, out_spread_ref):
    noise = constant(consts_ref, NOISE)
    spread_ends(out_spread_ref)

    def group(g, carry):
        for j in range(GROUP):
            tile = g * GROUP + j
            here = lanes(tile)
            both = banded(*terms[0], tile)
            for term in terms[1:]:
                both = both + banded(*term, tile)
            total = noise * own_ref[:, here] + joined(both)
            out_ref[:, here] = total
            spread_tile(total, out_spread_ref, tile)
        return carry

    lax.fori_loop(0, GX // GROUP, group, 0)


def two_sum(a, b):
    total = a + b
    part = total - a
    return total, (a - (total - part)) + (b - part)


def quick_sum(a, b):
    total = a + b
    return total, b - (total - a)


def halves(a):
    scaled = 4097.0 * a
    high = scaled - (scaled - a)
    return high, a - high


def two_product(a, b):
    a1, a2 = halves(a)
    b1, b2 = halves(b)
    product = a * b
    return product, ((a1 * b1 - product) + a1 * b2 + a2 * b1) + a2 * b2


class Pair:
    def __init__(self, high, low):
        self.high, self.low = high, low

    def __add__(self, other):
        total, error = two_sum(self.high, other.high)
        return Pair(*quick_sum(total, error + (self.low + other.low)))

    def __neg__(self):
        return Pair(-self.high, -self.low)

    def __sub__(self, other):
        return self + (-other)

    def __mul__(self, other):
        if not isinstance(other, Pair):
            return Pair(self.high * other, self.low * other)
        product, error = two_product(self.high, other.high)
        return Pair(*quick_sum(product, error + (self.high * other.low + self.low * other.high)))

    def __truediv__(self, other):
        first = self.high / other.high
        rest = self - other * Pair(first, jnp.zeros_like(first))
        return Pair(*quick_sum(first, rest.high / other.high))

    def where(self, keep, other):
        return Pair(jnp.where(keep, self.high, other.high), jnp.where(keep, self.low, other.low))


def grid_mask(k):
    lane = lax.broadcasted_iota(jnp.int32, (ROWS, TILE), 1)
    row = lax.broadcasted_iota(jnp.int32, (ROWS, TILE), 0)
    return lane == row + ROWS * k


def accumulate(sums, term):
    total, left = two_sum(sums[0], term)
    return total, sums[1] + left


def lines(sums, first):
    placed = [jnp.zeros((ROWS, TILE), F32), jnp.zeros((ROWS, TILE), F32)]
    for k, (high, low) in enumerate(sums):
        for shift in (64, 32, 16, 8, 4, 2, 1):
            high, left = two_sum(high, pltpu.roll(high, shift, 1))
            low = (low + pltpu.roll(low, shift, 1)) + left
        high, low = quick_sum(high, low)
        mask = grid_mask(first + k)
        placed = [jnp.where(mask, high, placed[0]), jnp.where(mask, low, placed[1])]
    return [jnp.sum(p, axis=0, keepdims=True) for p in placed]


def inner_kernel(
    first_ref, second_ref, consts_ref, left_ref, right_ref, spread0_ref, spread1_ref, feats_ref
):
    rows = feature_rows()
    for slot, (own_ref, weights_ref, spread_ref) in enumerate(
        ((first_ref, left_ref, spread0_ref), (second_ref, right_ref, spread1_ref))
    ):
        source_features(own_ref, constant(consts_ref, FACTOR), rows, feats_ref)
        fill_weights(first_ref, slot, feats_ref, weights_ref, 0, consts_ref, rows)
        fill_weights(second_ref, slot - 1, feats_ref, weights_ref, 1, consts_ref, rows)
        spread_sides(own_ref, spread_ref)


def outer_kernel(
    slot,
    other_ref,
    own_ref,
    consts_ref,
    left_ref,
    right_ref,
    spread0_ref,
    spread1_ref,
    weights_ref,
    out_ref,
    out_spread_ref,
    feats_ref,
    spread_ref,
):
    rows = feature_rows()
    source_features(other_ref, constant(consts_ref, FACTOR), rows, feats_ref)
    fill_weights(own_ref, 2 * slot - 1, feats_ref, weights_ref, 0, consts_ref, rows)
    spread_sides(other_ref, spread_ref)
    terms = ((spread_ref, weights_ref, 0), (spread0_ref, left_ref, slot), (spread1_ref, right_ref, slot))
    apply_row(own_ref, terms, consts_ref, out_ref, out_spread_ref)


def product_kernel(
    other_ref,
    own_ref,
    consts_ref,
    left_ref,
    right_ref,
    weights_ref,
    spread0_ref,
    spread1_ref,
    out_ref,
    out_spread_ref,
    spread_ref,
):
    spread(other_ref, spread_ref)
    terms = ((spread_ref, weights_ref, 0), (spread0_ref, left_ref, 0), (spread1_ref, right_ref, 0))
    apply_row(own_ref, terms, consts_ref, out_ref, out_spread_ref)


def gram_kernel(
    below_ref,
    b0_ref,
    b1_ref,
    f0_ref,
    f1_ref,
    g0_ref,
    consts_ref,
    left_ref,
    right_ref,
    under_ref,
    f0_spread_ref,
    f1_spread_ref,
    g0_spread_ref,
    g1_ref,
    sums_ref,
    spread_ref,
    g1_spread_ref,
):
    spread(below_ref, spread_ref)
    terms = ((spread_ref, under_ref, 0), (f0_spread_ref, left_ref, 1), (f1_spread_ref, right_ref, 1))
    apply_row(f1_ref, terms, consts_ref, g1_ref, g1_spread_ref)
    zero = jnp.zeros((ROWS, TILE), F32)
    noise = constant(consts_ref, NOISE)

    def group(g, sums):
        sums = list(sums)
        terms = [zero] * 7
        for j in range(8):
            tile = g * 8 + j
            here = lanes(tile)
            for half, refs in enumerate(((b0_ref, f0_ref, g0_ref), (b1_ref, f1_ref, g1_ref))):
                v = [ref[:, here] for ref in refs]
                for k, (i, m) in enumerate(((0, 0), (0, 1), (0, 2), (1, 1), (1, 2), (2, 2))):
                    terms[k] = terms[k] + v[i] * v[m]
                if half == 0:
                    both = banded(g0_spread_ref, left_ref, 0, tile)
                    both = both + 2.0 * banded(g1_spread_ref, right_ref, 0, tile)
                else:
                    both = banded(g1_spread_ref, right_ref, 1, tile)
                terms[6] = terms[6] + v[2] * (noise * v[2] + joined(both))
            if j % 2 == 1:
                sums = [accumulate(s, t) for s, t in zip(sums, terms)]
                terms = [zero] * 7
        return tuple(sums)

    high, low = lines(lax.fori_loop(0, GX // 8, group, ((zero, zero),) * 7), 0)
    sums_ref[0:1, :] = high
    sums_ref[1:2, :] = low


def moment_kernel(sums_ref, below_ref, own_ref, weights_ref, out_ref, spread_ref):
    spread(below_ref, spread_ref)
    zero = jnp.zeros((ROWS, TILE), F32)
    sums, term = (zero, zero), zero
    for tile in range(GX):
        image = joined(banded(spread_ref, weights_ref, 0, tile))
        term = term + own_ref[:, tile * TILE : (tile + 1) * TILE] * (2.0 * image)
        if tile % 4 == 3:
            sums, term = accumulate(sums, term), zero
    high, low = lines((sums,), 6)
    total, left = two_sum(sums_ref[0:1, :], high)
    both = jnp.concatenate([total, left + (low + sums_ref[1:2, :])], axis=1)
    out_ref[...] = jnp.broadcast_to(both[None], out_ref.shape)


def finish_kernel(
    points,
    cell_hbm,
    consts_ref,
    parts_ref,
    b0_ref,
    b1_ref,
    f0_ref,
    f1_ref,
    g0_ref,
    g1_ref,
    out_ref,
    quad_ref,
    cell_ref,
    grid_ref,
    sem,
):
    copy = pltpu.make_async_copy(cell_hbm, cell_ref, sem)
    copy.start()
    high, low = parts_ref[:, 0, 0:TILE], parts_ref[:, 0, TILE:]
    while high.shape[0] > 8:
        half = high.shape[0] // 2
        high, left = two_sum(high[:half], high[half:])
        low = (low[:half] + low[half:]) + left
    for shift in (4, 2, 1):
        high, left = two_sum(high, pltpu.roll(high, shift, 0))
        low = (low + pltpu.roll(low, shift, 0)) + left
    high, low = quick_sum(high, low)
    bb, bf, bg, ff, fg, gg, gag = (
        Pair(high, low)
        if k == 0
        else Pair(pltpu.roll(high, TILE - ROWS * k, 1), pltpu.roll(low, TILE - ROWS * k, 1))
        for k in range(7)
    )
    zero = jnp.zeros_like(high)
    none = Pair(zero, zero)
    one = Pair(zero + 1.0, zero)
    most = jnp.broadcast_to(1.0 / constant(consts_ref, NOISE), high.shape)

    floor = bb.high * 1e-11

    def step(square, product):
        good = (square.high > floor) & (product.high > 0.0)
        ratio = square / product.where(good, one)
        fits = ratio.high < most
        return ratio.where(fits, Pair(most, zero)).where(good, none), good

    def over(a, b, good):
        return (a / b.where(good, one)).where(good, none)

    alpha0, good0 = step(bb, bf)
    rr1 = bb - alpha0 * (bf * 2.0 - alpha0 * ff)
    beta0 = over(rr1, bb, good0)
    p0, p1 = one + beta0, -alpha0
    alpha1, good1 = step(rr1, p0 * (p0 * bf + p1 * (bg + ff)) + p1 * p1 * fg)
    r1, r2 = -(alpha0 + alpha1 * p0), -(alpha1 * p1)
    rr2 = bb + r1 * (bf * 2.0 + r1 * ff) + r2 * (bg * 2.0 + r1 * fg * 2.0 + r2 * gg)
    beta1 = over(rr2, rr1, good1)
    q0, q1, q2 = one + beta1 * p0, r1 + beta1 * p1, r2
    alpha2, good2 = step(
        rr2,
        q0 * (q0 * bf + q1 * (bg + ff) + q2 * fg * 2.0)
        + q1 * (q1 * fg + q2 * gg * 2.0)
        + q2 * q2 * gag,
    )
    alpha2 = alpha2.where(good1, none)
    on_b = alpha0 + alpha1 * p0 + alpha2 * q0
    on_f = alpha1 * p1 + alpha2 * q1
    on_g = alpha2 * q2
    quad = on_b * bb + on_f * bf + on_g * bg
    quad_ref[...] = (quad.high / points)[0:1, 0:RHS]
    mask = grid_mask(0)
    c0, c1, c2 = (
        jnp.broadcast_to(
            jnp.sum(
                jnp.where(mask, jnp.concatenate([c.high, c.high], axis=0), 0.0), axis=1, keepdims=True
            ),
            (ROWS, TILE),
        )
        for c in (on_b, on_f, on_g)
    )
    for half, (b_ref, f_ref, g_ref) in enumerate(
        ((b0_ref, f0_ref, g0_ref), (b1_ref, f1_ref, g1_ref))
    ):
        for tile in range(GX):
            here = slice(tile * TILE, (tile + 1) * TILE)
            grid_ref[half * GX + tile] = (
                c0 * b_ref[:, here] + c1 * f_ref[:, here] + c2 * g_ref[:, here]
            )
    copy.wait()
    for s in range(cell_ref.shape[0]):
        out_ref[:, s * TILE : (s + 1) * TILE] = grid_ref[cell_ref[s], 0:RHS, :]


def shards(offsets, tile_cell, probes, target, lengthscale, amplitude, noise):
    size = lax.axis_size("rows")
    points = size * tile_cell.shape[0] * TILE
    down = [(i, i + 1) for i in range(size - 1)]
    up = [(i + 1, i) for i in range(size - 1)]

    tiles = tile_cell.shape[0]
    first, second, consts = call(
        pack_kernel,
        "pack",
        (pltpu.VMEM((ROWS, WIDE), F32), pltpu.VMEM((ROWS, WIDE), F32), pltpu.VMEM((8, TILE), F32)),
        [HBM] * 4 + [SMEM] * 3,
        [
            pltpu.SMEM((tiles,), jnp.int32),
            pltpu.VMEM((2, tiles * TILE), F32),
            pltpu.VMEM((8, tiles * TILE), jnp.int32),
            pltpu.VMEM((1, tiles * TILE), F32),
            pltpu.SemaphoreType.DMA((4,)),
        ],
        flops=1 << 20,
        limit=60.5,
    )(
        tile_cell,
        offsets,
        probes,
        target.reshape(1, -1),
        lengthscale,
        amplitude,
        noise,
    )

    def outer(slot, other, own):
        return call(
            lambda *refs: outer_kernel(slot, *refs),
            f"outer{slot}",
            (weight_rows(1), grid_row(), spread_row()),
            [VMEM] * 7,
            [feature_tiles(), spread_row(ROWS)],
            flops=1 << 30,
        )(other, own, consts, left, right, b0_spread, b1_spread)

    above = lax.ppermute(second, "rows", down)
    below = lax.ppermute(first, "rows", up)
    left, right, b0_spread, b1_spread = call(
        inner_kernel,
        "inner",
        (weight_rows(2), weight_rows(2), spread_row(ROWS), spread_row(ROWS)),
        [VMEM] * 3,
        [feature_tiles()],
        flops=1 << 30,
    )(first, second, consts)
    over, f0, f0_spread = outer(0, above, first)
    f_below = lax.ppermute(f0, "rows", up)
    under, f1, f1_spread = outer(1, below, second)
    f_above = lax.ppermute(f1, "rows", down)
    g0, g0_spread = call(
        product_kernel,
        "product",
        (grid_row(), spread_row()),
        [VMEM] * 8,
        [spread_row()],
        flops=1 << 29,
    )(f_above, f0, consts, left, right, over, f0_spread, f1_spread)
    g_below = lax.ppermute(g0, "rows", up)
    g1, sums = call(
        gram_kernel,
        "gram",
        (grid_row(), jax.ShapeDtypeStruct((2, TILE), F32)),
        [VMEM] * 13,
        [spread_row(), spread_row()],
        flops=1 << 29,
    )(f_below, first, second, f0, f1, g0, consts, left, right, under, f0_spread, f1_spread, g0_spread)
    parts = call(
        moment_kernel,
        "moment",
        jax.ShapeDtypeStruct((size, 1, 2 * TILE), F32),
        [VMEM] * 4,
        [spread_row()],
        flops=1 << 29,
    )(sums, g_below, g1, under)
    parts = lax.all_to_all(parts, "rows", split_axis=0, concat_axis=0, tiled=True)

    solutions, quad = call(
        lambda *refs: finish_kernel(float(points), *refs),
        "finish",
        (
            jax.ShapeDtypeStruct((RHS, tiles * TILE), F32),
            jax.ShapeDtypeStruct((1, RHS), F32),
        ),
        [HBM] + [VMEM] * 8,
        [
            pltpu.SMEM((tiles,), jnp.int32),
            pltpu.VMEM((tiles, ROWS, TILE), F32),
            pltpu.SemaphoreType.DMA,
        ],
        flops=1 << 20,
    )(tile_cell, consts, parts, first, second, f0, f1, g0, g1)
    return (solutions, quad.reshape(RHS))


def solution(mesh):
    return jax.shard_map(
        shards,
        mesh=mesh,
        in_specs=(
            P(None, "rows"),
            P("rows"),
            P(None, "rows"),
            P("rows"),
            P("hyp"),
            P("hyp"),
            P("hyp"),
        ),
        out_specs=(P("hyp", "rows"), P("hyp")),
        check_vma=False,
    )
```

```python
import jax
import jax.numpy as jnp
from jax import lax
from jax.experimental import pallas as pl
from jax.experimental.pallas import tpu as pltpu
from jax.sharding import PartitionSpec as P

TILE = 128
GX = 16
RHS = 9
ROWS = 16
WIDE = GX * TILE
FEATURES = 32
PAD = GX + 2
BAND = 3 * 2 * TILE
F32 = jnp.float32
BF16 = jnp.bfloat16
TINY = 1e-30

VMEM = pl.BlockSpec(memory_space=pltpu.VMEM)
HBM = pl.BlockSpec(memory_space=pltpu.HBM)
SMEM = pl.BlockSpec(memory_space=pltpu.SMEM)
REACH, TOP, FACTOR, NOISE = range(4)


def call(kernel, name, out_shape, in_specs, scratch=(), flops=0, limit=12):
    return pl.pallas_call(
        kernel,
        name=name,
        out_shape=out_shape,
        in_specs=in_specs,
        out_specs=jax.tree.map(lambda _: VMEM, out_shape),
        scratch_shapes=list(scratch),
        cost_estimate=pl.CostEstimate(flops=flops, bytes_accessed=1 << 20, transcendentals=0),
        compiler_params=pltpu.CompilerParams(vmem_limit_bytes=int(limit * 2**20)),
    )


def grid_row():
    return jax.ShapeDtypeStruct((ROWS, WIDE), F32)


def spread_row(rows=2 * ROWS):
    return pltpu.VMEM((rows, PAD * 2 * TILE), BF16)


def weight_rows(count):
    return pltpu.VMEM((count, GX, BAND, TILE), BF16)


def feature_tiles():
    return pltpu.VMEM((PAD, TILE, FEATURES), BF16)


def lanes(tile, width=TILE):
    return pl.ds(pl.multiple_of(tile * width, width), width)


def pack_kernel(
    cell_hbm,
    offsets_hbm,
    probes_hbm,
    target_hbm,
    scale_ref,
    amp_ref,
    noise_ref,
    first_ref,
    second_ref,
    consts_ref,
    cell_ref,
    offsets_ref,
    probes_ref,
    target_ref,
    sems,
):
    copies = [
        pltpu.make_async_copy(source, dest, sems.at[i])
        for i, (source, dest) in enumerate(
            (
                (cell_hbm, cell_ref),
                (offsets_hbm, offsets_ref),
                (probes_hbm, probes_ref),
                (target_hbm, target_ref),
            )
        )
    ]
    for copy in copies:
        copy.start()
    for copy in copies:
        copy.wait()
    filler = jnp.zeros((ROWS - RHS - 2, TILE), F32)
    for s in range(cell_ref.shape[0]):
        here = slice(s * TILE, (s + 1) * TILE)
        signs = 2.0 * probes_ref[:, here].astype(F32) - 1.0
        rest = jnp.concatenate([target_ref[:, here], offsets_ref[:, here], filler], axis=0)
        cell = cell_ref[s]

        def put(ref, column, signs=signs, rest=rest):
            ref[0:8, lanes(column)] = signs
            ref[8:16, lanes(column)] = rest

        @pl.when(cell < GX)
        def _():
            put(first_ref, cell)

        @pl.when(cell >= GX)
        def _():
            put(second_ref, cell - GX)

    amp = jnp.full((1, TILE), amp_ref[0], F32)
    reach = jnp.exp(0.2 * jnp.log(4.0 * amp))
    square = reach * reach
    consts_ref[REACH : REACH + 1, :] = reach
    consts_ref[TOP : TOP + 1, :] = 5.0 * amp / (square * square)
    consts_ref[FACTOR : FACTOR + 1, :] = reach / jnp.full((1, TILE), scale_ref[0], F32)
    consts_ref[NOISE : NOISE + 1, :] = jnp.full((1, TILE), noise_ref[0], F32)


def constant(consts_ref, which):
    return consts_ref[which : which + 1, :]


def split_rows(values, level):
    first = values.astype(BF16).astype(F32)
    rest = values - first
    second = rest.astype(BF16).astype(F32)
    third = rest - second
    return jnp.where(level == 0, first, jnp.where(level == 1, second, third))


def feature_rows():
    row = lax.broadcasted_iota(jnp.int32, (FEATURES, TILE), 0)

    def level(order):
        out = jnp.zeros_like(row)
        for k, v in enumerate(order):
            if v:
                out = jnp.where(row == k, v, out)
        return out

    source = level([0, 0, 1, 1, 0, 2] * 2 + [0, 1, 2] + [0, 0, 0])
    target = level([0, 1, 0, 1, 2, 0] * 2 + [0, 0, 0] + [0, 1, 2])
    kind = jnp.where(row < 6, 0, jnp.where(row < 12, 1, jnp.where(row < 15, 2, jnp.where(row < 18, 3, 4))))
    return kind, source, target


def choose(kind, a, b, c, d):
    return jnp.where(
        kind == 0, a, jnp.where(kind == 1, b, jnp.where(kind == 2, c, jnp.where(kind == 3, d, 0.0)))
    )


def source_features(row_ref, factor, rows, out_ref):
    kind, source, _ = rows
    zero = jnp.zeros((TILE, FEATURES), BF16)
    out_ref[0] = zero
    out_ref[PAD - 1] = zero

    def one(tile, carry):
        a = factor * (row_ref[9:10, lanes(tile)] - 0.5)
        b = factor * (row_ref[10:11, lanes(tile)] - 0.5)
        values = choose(kind, a, b, a * a + b * b, 1.0)
        out_ref[tile + 1] = split_rows(values, source).T.astype(BF16)
        return carry

    lax.fori_loop(0, GX, one, 0, unroll=8)


def target_features(row_ref, tile, row_shift, col_shift, factor, rows):
    kind, _, target = rows
    a = factor * ((row_shift + 0.5) - row_ref[9:10, lanes(tile)])
    b = factor * ((col_shift + 0.5) - row_ref[10:11, lanes(tile)])
    values = choose(kind, 2.0 * a, 2.0 * b, 1.0, a * a + b * b)
    return split_rows(values, target).astype(BF16)


def fill_weights(target_ref, row_shift, feats_ref, weights_ref, combo, consts_ref, rows):
    factor = constant(consts_ref, FACTOR)
    reach = jnp.broadcast_to(constant(consts_ref, REACH), (16, TILE))
    top = jnp.broadcast_to(constant(consts_ref, TOP), (16, TILE))

    def one(tile, carry):
        for k in range(3):
            wanted = target_features(target_ref, tile, float(row_shift), float(k - 1), factor, rows)
            square = lax.dot_general(
                feats_ref[tile + k],
                wanted,
                (((1,), (0,)), ((), ())),
                preferred_element_type=F32,
            )
            for part in range(TILE // 16):
                here = jnp.maximum(square[part * 16 : (part + 1) * 16, :], 1e-12)
                close = jnp.maximum(reach - here * lax.rsqrt(here), 0.0)
                second = close * close
                weight = (second * second) * (top - close)
                high = weight.astype(BF16)
                low = (weight - high.astype(F32)).astype(BF16)
                base = k * 2 * TILE + part * 16
                weights_ref[combo, tile, base : base + 16, :] = high
                weights_ref[combo, tile, base + TILE : base + TILE + 16, :] = low
        return carry

    lax.fori_loop(0, GX, one, 0, unroll=8)


def spread_ends(out_ref):
    empty = jnp.zeros((2 * ROWS, 2 * TILE), BF16)
    out_ref[:, 0 : 2 * TILE] = empty
    out_ref[:, (PAD - 1) * 2 * TILE :] = empty


def spread_tile(values, out_ref, tile):
    high = values.astype(BF16)
    low = (values - high.astype(F32)).astype(BF16)
    both = jnp.concatenate([high, low], axis=0)
    at = pl.multiple_of((tile + 1) * 2 * TILE, 2 * TILE)
    out_ref[:, pl.ds(at, 2 * TILE)] = jnp.concatenate([both, both], axis=1)


def spread(row_ref, out_ref):
    spread_ends(out_ref)
    for tile in range(GX):
        spread_tile(row_ref[:, tile * TILE : (tile + 1) * TILE], out_ref, tile)


def spread_sides(row_ref, out_ref):
    empty = jnp.zeros((ROWS, 2 * TILE), BF16)
    out_ref[:, 0 : 2 * TILE] = empty
    out_ref[:, (PAD - 1) * 2 * TILE :] = empty
    row = lax.broadcasted_iota(jnp.int32, (8, TILE), 0)
    for tile in range(GX):
        here = slice(tile * TILE, (tile + 1) * TILE)
        target = row_ref[8:9, here]
        high = target.astype(BF16).astype(F32)
        rest = jnp.where(row == 0, high, jnp.where(row == 1, target - high, 0.0))
        both = jnp.concatenate([row_ref[0:8, here], rest], axis=0).astype(BF16)
        at = (tile + 1) * 2 * TILE
        out_ref[:, at : at + 2 * TILE] = jnp.concatenate([both, both], axis=1)


def banded(spread_ref, weights_ref, combo, tile):
    at = pl.multiple_of(tile * 2 * TILE, 2 * TILE)
    return jnp.dot(
        spread_ref[:, pl.ds(at, BAND)],
        weights_ref[combo, tile],
        preferred_element_type=F32,
    )


def joined(both):
    if both.shape[0] == 2 * ROWS:
        return both[0:ROWS] + both[ROWS:]
    row = lax.broadcasted_iota(jnp.int32, both.shape, 0)
    return both + jnp.where(row == 8, pltpu.roll(both, ROWS - 1, 0), 0.0)


GROUP = 16


def apply_row(own_ref, terms, consts_ref, out_ref, out_spread_ref, beside_ref=None):
    noise = constant(consts_ref, NOISE)
    spread_ends(out_spread_ref)

    def group(g, carry):
        for j in range(GROUP):
            tile = g * GROUP + j
            here = lanes(tile)
            both = banded(*terms[0], tile)
            if beside_ref is not None:
                beside_ref[:, here] = joined(both)
            for term in terms[1:]:
                both = both + banded(*term, tile)
            total = noise * own_ref[:, here] + joined(both)
            out_ref[:, here] = total
            spread_tile(total, out_spread_ref, tile)
        return carry

    lax.fori_loop(0, GX // GROUP, group, 0)


def two_sum(a, b):
    total = a + b
    part = total - a
    return total, (a - (total - part)) + (b - part)


def quick_sum(a, b):
    total = a + b
    return total, b - (total - a)


def halves(a):
    scaled = 4097.0 * a
    high = scaled - (scaled - a)
    return high, a - high


def two_product(a, b):
    a1, a2 = halves(a)
    b1, b2 = halves(b)
    product = a * b
    return product, ((a1 * b1 - product) + a1 * b2 + a2 * b1) + a2 * b2


class Pair:
    def __init__(self, high, low):
        self.high, self.low = high, low

    def __add__(self, other):
        total, error = two_sum(self.high, other.high)
        return Pair(*quick_sum(total, error + (self.low + other.low)))

    def __neg__(self):
        return Pair(-self.high, -self.low)

    def __sub__(self, other):
        return self + (-other)

    def __mul__(self, other):
        if not isinstance(other, Pair):
            return Pair(self.high * other, self.low * other)
        product, error = two_product(self.high, other.high)
        return Pair(*quick_sum(product, error + (self.high * other.low + self.low * other.high)))

    def __truediv__(self, other):
        first = self.high / other.high
        rest = self - other * Pair(first, jnp.zeros_like(first))
        return Pair(*quick_sum(first, rest.high / other.high))

    def where(self, keep, other):
        return Pair(jnp.where(keep, self.high, other.high), jnp.where(keep, self.low, other.low))


SUMS = 9
STRIDE = TILE // SUMS


def grid_mask(k):
    lane = lax.broadcasted_iota(jnp.int32, (ROWS, TILE), 1)
    row = lax.broadcasted_iota(jnp.int32, (ROWS, TILE), 0)
    return (lane == row + STRIDE * k) & (row < RHS)


def accumulate(sums, term):
    total, left = two_sum(sums[0], term)
    return total, sums[1] + left


def lines(sums, first):
    placed = [jnp.zeros((ROWS, TILE), F32), jnp.zeros((ROWS, TILE), F32)]
    for k, (high, low) in enumerate(sums):
        for shift in (64, 32, 16, 8, 4, 2, 1):
            high, left = two_sum(high, pltpu.roll(high, shift, 1))
            low = (low + pltpu.roll(low, shift, 1)) + left
        high, low = quick_sum(high, low)
        mask = grid_mask(first + k)
        placed = [jnp.where(mask, high, placed[0]), jnp.where(mask, low, placed[1])]
    return [jnp.sum(p, axis=0, keepdims=True) for p in placed]


def inner_kernel(
    first_ref, second_ref, consts_ref, left_ref, right_ref, spread0_ref, spread1_ref, feats_ref
):
    rows = feature_rows()
    for slot, (own_ref, weights_ref, spread_ref) in enumerate(
        ((first_ref, left_ref, spread0_ref), (second_ref, right_ref, spread1_ref))
    ):
        source_features(own_ref, constant(consts_ref, FACTOR), rows, feats_ref)
        fill_weights(first_ref, slot, feats_ref, weights_ref, 0, consts_ref, rows)
        fill_weights(second_ref, slot - 1, feats_ref, weights_ref, 1, consts_ref, rows)
        spread_sides(own_ref, spread_ref)


def outer_kernel(
    slot,
    other_ref,
    own_ref,
    consts_ref,
    left_ref,
    right_ref,
    spread0_ref,
    spread1_ref,
    weights_ref,
    out_ref,
    out_spread_ref,
    beside_ref,
    feats_ref,
    spread_ref,
):
    rows = feature_rows()
    source_features(other_ref, constant(consts_ref, FACTOR), rows, feats_ref)
    fill_weights(own_ref, 2 * slot - 1, feats_ref, weights_ref, 0, consts_ref, rows)
    spread_sides(other_ref, spread_ref)
    terms = ((spread_ref, weights_ref, 0), (spread0_ref, left_ref, slot), (spread1_ref, right_ref, slot))
    apply_row(own_ref, terms, consts_ref, out_ref, out_spread_ref, beside_ref)


def product_kernel(
    other_ref,
    own_ref,
    consts_ref,
    left_ref,
    right_ref,
    weights_ref,
    spread0_ref,
    spread1_ref,
    out_ref,
    out_spread_ref,
    spread_ref,
):
    spread(other_ref, spread_ref)
    terms = ((spread_ref, weights_ref, 0), (spread0_ref, left_ref, 0), (spread1_ref, right_ref, 0))
    apply_row(own_ref, terms, consts_ref, out_ref, out_spread_ref)


def gram_kernel(
    below_ref,
    b0_ref,
    b1_ref,
    f0_ref,
    f1_ref,
    g0_ref,
    b_beside_ref,
    consts_ref,
    left_ref,
    right_ref,
    under_ref,
    f0_spread_ref,
    f1_spread_ref,
    g0_spread_ref,
    g1_ref,
    sums_ref,
    spread_ref,
    g1_spread_ref,
    f_beside_ref,
):
    spread(below_ref, spread_ref)
    terms = ((spread_ref, under_ref, 0), (f0_spread_ref, left_ref, 1), (f1_spread_ref, right_ref, 1))
    apply_row(f1_ref, terms, consts_ref, g1_ref, g1_spread_ref, f_beside_ref)
    zero = jnp.zeros((ROWS, TILE), F32)
    noise = constant(consts_ref, NOISE)

    def group(g, sums):
        sums = list(sums)
        terms = [zero] * SUMS
        for j in range(8):
            tile = g * 8 + j
            here = lanes(tile)
            for half, refs in enumerate(((b0_ref, f0_ref, g0_ref), (b1_ref, f1_ref, g1_ref))):
                v = [ref[:, here] for ref in refs]
                for k, (i, m) in enumerate(((0, 0), (0, 1), (0, 2), (1, 1), (1, 2), (2, 2))):
                    terms[k] = terms[k] + v[i] * v[m]
                both = banded(g0_spread_ref, left_ref, half, tile)
                both = both + banded(g1_spread_ref, right_ref, half, tile)
                image = noise * v[2] + joined(both)
                for k in range(3):
                    terms[6 + k] = terms[6 + k] + v[k] * image
                if half == 1:
                    terms[6] = terms[6] + v[2] * b_beside_ref[:, here]
                    terms[7] = terms[7] + v[2] * f_beside_ref[:, here]
            if j % 2 == 1:
                sums = [accumulate(s, t) for s, t in zip(sums, terms)]
                terms = [zero] * SUMS
        return tuple(sums)

    high, low = lines(lax.fori_loop(0, GX // 8, group, ((zero, zero),) * SUMS), 0)
    sums_ref[0:1, :] = high
    sums_ref[1:2, :] = low


def moment_kernel(sums_ref, below_ref, b_ref, f_ref, g_ref, weights_ref, out_ref, spread_ref):
    spread(below_ref, spread_ref)
    zero = jnp.zeros((ROWS, TILE), F32)
    sums, terms = [(zero, zero)] * 3, [zero] * 3
    for tile in range(GX):
        here = slice(tile * TILE, (tile + 1) * TILE)
        image = joined(banded(spread_ref, weights_ref, 0, tile))
        factors = (b_ref[:, here], f_ref[:, here], 2.0 * g_ref[:, here])
        terms = [t + v * image for t, v in zip(terms, factors)]
        if tile % 4 == 3:
            sums, terms = [accumulate(s, t) for s, t in zip(sums, terms)], [zero] * 3
    high, low = lines(sums, 6)
    total, left = two_sum(sums_ref[0:1, :], high)
    both = jnp.concatenate([total, left + (low + sums_ref[1:2, :])], axis=1)
    out_ref[...] = jnp.broadcast_to(both[None], out_ref.shape)


def finish_kernel(
    points,
    cell_hbm,
    consts_ref,
    parts_ref,
    b0_ref,
    b1_ref,
    f0_ref,
    f1_ref,
    g0_ref,
    g1_ref,
    out_ref,
    quad_ref,
    cell_ref,
    grid_ref,
    sem,
):
    copy = pltpu.make_async_copy(cell_hbm, cell_ref, sem)
    copy.start()
    high, low = parts_ref[:, 0, 0:TILE], parts_ref[:, 0, TILE:]
    while high.shape[0] > 8:
        half = high.shape[0] // 2
        high, left = two_sum(high[:half], high[half:])
        low = (low[:half] + low[half:]) + left
    for shift in (4, 2, 1):
        high, left = two_sum(high, pltpu.roll(high, shift, 0))
        low = (low + pltpu.roll(low, shift, 0)) + left
    high, low = quick_sum(high, low)
    bb, bf, bg, ff, fg, gg, bag, fag, gag = (
        Pair(high, low)
        if k == 0
        else Pair(pltpu.roll(high, TILE - STRIDE * k, 1), pltpu.roll(low, TILE - STRIDE * k, 1))
        for k in range(SUMS)
    )
    zero = jnp.zeros_like(high)
    none = Pair(zero, zero)
    one = Pair(zero + 1.0, zero)
    most = jnp.broadcast_to(1.0 / constant(consts_ref, NOISE), high.shape)

    floor = bb.high * 1e-11

    def step(square, product):
        good = (square.high > floor) & (product.high > 0.0)
        ratio = square / product.where(good, one)
        fits = ratio.high < most
        return ratio.where(fits, Pair(most, zero)).where(good, none), good

    def over(a, b, good):
        return (a / b.where(good, one)).where(good, none)

    alpha0, good0 = step(bb, bf)
    rr1 = bb - alpha0 * (bf * 2.0 - alpha0 * ff)
    beta0 = over(rr1, bb, good0)
    p0, p1 = one + beta0, -alpha0
    alpha1, good1 = step(rr1, p0 * (p0 * bf + p1 * (bg + ff)) + p1 * p1 * fg)
    r1, r2 = -(alpha0 + alpha1 * p0), -(alpha1 * p1)
    rr2 = bb + r1 * (bf * 2.0 + r1 * ff) + r2 * (bg * 2.0 + r1 * fg * 2.0 + r2 * gg)
    beta1 = over(rr2, rr1, good1)
    q0, q1, q2 = one + beta1 * p0, r1 + beta1 * p1, r2
    alpha2, good2 = step(
        rr2,
        q0 * (q0 * bf + q1 * (bg + ff) + q2 * (fg + bag)) + q1 * (q1 * fg + q2 * (gg + fag)) + q2 * q2 * gag,
    )
    alpha2 = alpha2.where(good1, none)
    on_b = alpha0 + alpha1 * p0 + alpha2 * q0
    on_f = alpha1 * p1 + alpha2 * q1
    on_g = alpha2 * q2
    quad = on_b * bb + on_f * bf + on_g * bg
    quad_ref[...] = (quad.high / points)[0:1, 0:RHS]
    mask = grid_mask(0)
    c0, c1, c2 = (
        jnp.broadcast_to(
            jnp.sum(
                jnp.where(mask, jnp.concatenate([c.high, c.high], axis=0), 0.0), axis=1, keepdims=True
            ),
            (ROWS, TILE),
        )
        for c in (on_b, on_f, on_g)
    )
    for half, (b_ref, f_ref, g_ref) in enumerate(
        ((b0_ref, f0_ref, g0_ref), (b1_ref, f1_ref, g1_ref))
    ):
        for tile in range(GX):
            here = slice(tile * TILE, (tile + 1) * TILE)
            grid_ref[half * GX + tile] = (
                c0 * b_ref[:, here] + c1 * f_ref[:, here] + c2 * g_ref[:, here]
            )
    copy.wait()
    for s in range(cell_ref.shape[0]):
        out_ref[:, s * TILE : (s + 1) * TILE] = grid_ref[cell_ref[s], 0:RHS, :]


def shards(offsets, tile_cell, probes, target, lengthscale, amplitude, noise):
    size = lax.axis_size("rows")
    points = size * tile_cell.shape[0] * TILE
    down = [(i, i + 1) for i in range(size - 1)]
    up = [(i + 1, i) for i in range(size - 1)]

    tiles = tile_cell.shape[0]
    first, second, consts = call(
        pack_kernel,
        "pack",
        (pltpu.VMEM((ROWS, WIDE), F32), pltpu.VMEM((ROWS, WIDE), F32), pltpu.VMEM((8, TILE), F32)),
        [HBM] * 4 + [SMEM] * 3,
        [
            pltpu.SMEM((tiles,), jnp.int32),
            pltpu.VMEM((2, tiles * TILE), F32),
            pltpu.VMEM((8, tiles * TILE), jnp.int32),
            pltpu.VMEM((1, tiles * TILE), F32),
            pltpu.SemaphoreType.DMA((4,)),
        ],
        flops=1 << 20,
        limit=60.5,
    )(
        tile_cell,
        offsets,
        probes,
        target.reshape(1, -1),
        lengthscale,
        amplitude,
        noise,
    )

    def outer(slot, other, own):
        return call(
            lambda *refs: outer_kernel(slot, *refs),
            f"outer{slot}",
            (weight_rows(1), grid_row(), spread_row(), grid_row()),
            [VMEM] * 7,
            [feature_tiles(), spread_row(ROWS)],
            flops=1 << 30,
        )(other, own, consts, left, right, b0_spread, b1_spread)

    above = lax.ppermute(second, "rows", down)
    below = lax.ppermute(first, "rows", up)
    left, right, b0_spread, b1_spread = call(
        inner_kernel,
        "inner",
        (weight_rows(2), weight_rows(2), spread_row(ROWS), spread_row(ROWS)),
        [VMEM] * 3,
        [feature_tiles()],
        flops=1 << 30,
    )(first, second, consts)
    over, f0, f0_spread, _ = outer(0, above, first)
    f_below = lax.ppermute(f0, "rows", up)
    under, f1, f1_spread, b_beside = outer(1, below, second)
    f_above = lax.ppermute(f1, "rows", down)
    g0, g0_spread = call(
        product_kernel,
        "product",
        (grid_row(), spread_row()),
        [VMEM] * 8,
        [spread_row()],
        flops=1 << 29,
    )(f_above, f0, consts, left, right, over, f0_spread, f1_spread)
    g_below = lax.ppermute(g0, "rows", up)
    g1, sums = call(
        gram_kernel,
        "gram",
        (grid_row(), jax.ShapeDtypeStruct((2, TILE), F32)),
        [VMEM] * 14,
        [spread_row(), spread_row(), pltpu.VMEM((ROWS, WIDE), F32)],
        flops=1 << 29,
    )(f_below, first, second, f0, f1, g0, b_beside, consts, left, right, under, f0_spread, f1_spread, g0_spread)
    parts = call(
        moment_kernel,
        "moment",
        jax.ShapeDtypeStruct((size, 1, 2 * TILE), F32),
        [VMEM] * 6,
        [spread_row()],
        flops=1 << 29,
    )(sums, g_below, second, f1, g1, under)
    parts = lax.all_to_all(parts, "rows", split_axis=0, concat_axis=0, tiled=True)

    solutions, quad = call(
        lambda *refs: finish_kernel(float(points), *refs),
        "finish",
        (
            jax.ShapeDtypeStruct((RHS, tiles * TILE), F32),
            jax.ShapeDtypeStruct((1, RHS), F32),
        ),
        [HBM] + [VMEM] * 8,
        [
            pltpu.SMEM((tiles,), jnp.int32),
            pltpu.VMEM((tiles, ROWS, TILE), F32),
            pltpu.SemaphoreType.DMA,
        ],
        flops=1 << 20,
    )(tile_cell, consts, parts, first, second, f0, f1, g0, g1)
    return (solutions, quad.reshape(RHS))


def solution(mesh):
    return jax.shard_map(
        shards,
        mesh=mesh,
        in_specs=(
            P(None, "rows"),
            P("rows"),
            P(None, "rows"),
            P("rows"),
            P("hyp"),
            P("hyp"),
            P("hyp"),
        ),
        out_specs=(P("hyp", "rows"), P("hyp")),
        check_vma=False,
    )
```

```python
import jax
import jax.numpy as jnp
from jax import lax
from jax.experimental import pallas as pl
from jax.experimental.pallas import tpu as pltpu
from jax.sharding import PartitionSpec as P

TILE = 128
GX = 16
RHS = 9
ROWS = 16
WIDE = GX * TILE
FEATURES = 32
PAD = GX + 2
BAND = 3 * 2 * TILE
F32 = jnp.float32
BF16 = jnp.bfloat16
TINY = 1e-30

VMEM = pl.BlockSpec(memory_space=pltpu.VMEM)
HBM = pl.BlockSpec(memory_space=pltpu.HBM)
SMEM = pl.BlockSpec(memory_space=pltpu.SMEM)
REACH, TOP, FACTOR, NOISE = range(4)


def call(kernel, name, out_shape, in_specs, scratch=(), flops=0, limit=12):
    return pl.pallas_call(
        kernel,
        name=name,
        out_shape=out_shape,
        in_specs=in_specs,
        out_specs=jax.tree.map(lambda _: VMEM, out_shape),
        scratch_shapes=list(scratch),
        cost_estimate=pl.CostEstimate(flops=flops, bytes_accessed=1 << 20, transcendentals=0),
        compiler_params=pltpu.CompilerParams(vmem_limit_bytes=int(limit * 2**20)),
    )


def grid_row():
    return jax.ShapeDtypeStruct((ROWS, WIDE), F32)


def spread_row(rows=2 * ROWS):
    return pltpu.VMEM((rows, PAD * 2 * TILE), BF16)


def weight_rows(count):
    return pltpu.VMEM((count, GX, BAND, TILE), BF16)


def feature_tiles():
    return pltpu.VMEM((PAD, TILE, FEATURES), BF16)


def lanes(tile, width=TILE):
    return pl.ds(pl.multiple_of(tile * width, width), width)


def pack_kernel(
    cell_hbm,
    offsets_hbm,
    probes_hbm,
    target_hbm,
    scale_ref,
    amp_ref,
    noise_ref,
    first_ref,
    second_ref,
    consts_ref,
    cell_ref,
    from_ref,
    offsets_ref,
    probes_ref,
    target_ref,
    sems,
):
    copies = [
        pltpu.make_async_copy(source, dest, sems.at[i])
        for i, (source, dest) in enumerate(
            (
                (cell_hbm, cell_ref),
                (offsets_hbm, offsets_ref),
                (probes_hbm, probes_ref),
                (target_hbm, target_ref),
            )
        )
    ]
    for copy in copies:
        copy.start()
    for copy in copies:
        copy.wait()
    for s in range(cell_ref.shape[0]):
        from_ref[cell_ref[s]] = s
    filler = jnp.zeros((ROWS - RHS - 2, TILE), F32)
    for cell in range(cell_ref.shape[0]):
        stored = lanes(from_ref[cell])
        here = slice(cell % GX * TILE, (cell % GX + 1) * TILE)
        ref = (first_ref, second_ref)[cell // GX]
        ref[0:8, here] = 2.0 * probes_ref[:, stored].astype(F32) - 1.0
        ref[8:16, here] = jnp.concatenate(
            [target_ref[:, stored], offsets_ref[:, stored], filler], axis=0
        )
    amp = jnp.full((1, TILE), amp_ref[0], F32)
    reach = jnp.exp(0.2 * jnp.log(4.0 * amp))
    square = reach * reach
    consts_ref[REACH : REACH + 1, :] = reach
    consts_ref[TOP : TOP + 1, :] = 5.0 * amp / (square * square)
    consts_ref[FACTOR : FACTOR + 1, :] = reach / jnp.full((1, TILE), scale_ref[0], F32)
    consts_ref[NOISE : NOISE + 1, :] = jnp.full((1, TILE), noise_ref[0], F32)


def constant(consts_ref, which):
    return consts_ref[which : which + 1, :]


def split_rows(values, level):
    first = values.astype(BF16).astype(F32)
    rest = values - first
    second = rest.astype(BF16).astype(F32)
    third = rest - second
    return jnp.where(level == 0, first, jnp.where(level == 1, second, third))


def feature_rows():
    row = lax.broadcasted_iota(jnp.int32, (FEATURES, TILE), 0)

    def level(order):
        out = jnp.zeros_like(row)
        for k, v in enumerate(order):
            if v:
                out = jnp.where(row == k, v, out)
        return out

    source = level([0, 0, 1, 1, 0, 2] * 2 + [0, 1, 2] + [0, 0, 0])
    target = level([0, 1, 0, 1, 2, 0] * 2 + [0, 0, 0] + [0, 1, 2])
    kind = jnp.where(row < 6, 0, jnp.where(row < 12, 1, jnp.where(row < 15, 2, jnp.where(row < 18, 3, 4))))
    return kind, source, target


def choose(kind, a, b, c, d):
    return jnp.where(
        kind == 0, a, jnp.where(kind == 1, b, jnp.where(kind == 2, c, jnp.where(kind == 3, d, 0.0)))
    )


def source_features(row_ref, factor, rows, out_ref):
    kind, source, _ = rows
    zero = jnp.zeros((TILE, FEATURES), BF16)
    out_ref[0] = zero
    out_ref[PAD - 1] = zero

    def one(tile, carry):
        a = factor * (row_ref[9:10, lanes(tile)] - 0.5)
        b = factor * (row_ref[10:11, lanes(tile)] - 0.5)
        values = choose(kind, a, b, a * a + b * b, 1.0)
        out_ref[tile + 1] = split_rows(values, source).T.astype(BF16)
        return carry

    lax.fori_loop(0, GX, one, 0, unroll=8)


def target_features(row_ref, tile, row_shift, col_shift, factor, rows):
    kind, _, target = rows
    a = factor * ((row_shift + 0.5) - row_ref[9:10, lanes(tile)])
    b = factor * ((col_shift + 0.5) - row_ref[10:11, lanes(tile)])
    values = choose(kind, 2.0 * a, 2.0 * b, 1.0, a * a + b * b)
    return split_rows(values, target).astype(BF16)


def fill_weights(targets, feats_ref, consts_ref, rows):
    factor = constant(consts_ref, FACTOR)
    reach = jnp.broadcast_to(constant(consts_ref, REACH), (TILE, TILE))
    top = jnp.broadcast_to(constant(consts_ref, TOP), (TILE, TILE))

    def one(tile, carry):
        for k in range(3):
            wanted = [
                target_features(ref, tile, float(row_shift), float(k - 1), factor, rows)
                for ref, row_shift, _, _ in targets
            ]
            squares = lax.dot_general(
                feats_ref[tile + k],
                wanted[0] if len(wanted) == 1 else jnp.concatenate(wanted, axis=1),
                (((1,), (0,)), ((), ())),
                preferred_element_type=F32,
            )
            for i, (_, _, weights_ref, combo) in enumerate(targets):
                here = jnp.maximum(squares[:, i * TILE : (i + 1) * TILE], 1e-12)
                close = jnp.maximum(reach - here * lax.rsqrt(here), 0.0)
                second = close * close
                weight = (second * second) * (top - close)
                high = weight.astype(BF16)
                low = (weight - high.astype(F32)).astype(BF16)
                base = k * 2 * TILE
                weights_ref[combo, tile, base : base + TILE, :] = high
                weights_ref[combo, tile, base + TILE : base + 2 * TILE, :] = low
        return carry

    lax.fori_loop(0, GX, one, 0, unroll=8 // len(targets))


def spread_ends(out_ref):
    empty = jnp.zeros((2 * ROWS, 2 * TILE), BF16)
    out_ref[:, 0 : 2 * TILE] = empty
    out_ref[:, (PAD - 1) * 2 * TILE :] = empty


def spread_tile(values, out_ref, tile):
    high = values.astype(BF16)
    low = (values - high.astype(F32)).astype(BF16)
    both = jnp.concatenate([high, low], axis=0)
    at = pl.multiple_of((tile + 1) * 2 * TILE, 2 * TILE)
    out_ref[:, pl.ds(at, 2 * TILE)] = jnp.concatenate([both, both], axis=1)


def spread(row_ref, out_ref):
    spread_ends(out_ref)
    for tile in range(GX):
        spread_tile(row_ref[:, tile * TILE : (tile + 1) * TILE], out_ref, tile)


def spread_sides(row_ref, out_ref):
    empty = jnp.zeros((ROWS, 2 * TILE), BF16)
    out_ref[:, 0 : 2 * TILE] = empty
    out_ref[:, (PAD - 1) * 2 * TILE :] = empty
    row = lax.broadcasted_iota(jnp.int32, (8, TILE), 0)
    for tile in range(GX):
        here = slice(tile * TILE, (tile + 1) * TILE)
        target = row_ref[8:9, here]
        high = target.astype(BF16).astype(F32)
        rest = jnp.where(row == 0, high, jnp.where(row == 1, target - high, 0.0))
        both = jnp.concatenate([row_ref[0:8, here], rest], axis=0).astype(BF16)
        at = (tile + 1) * 2 * TILE
        out_ref[:, at : at + 2 * TILE] = jnp.concatenate([both, both], axis=1)


def banded(spread_ref, weights_ref, combo, tile):
    at = pl.multiple_of(tile * 2 * TILE, 2 * TILE)
    return jnp.dot(
        spread_ref[:, pl.ds(at, BAND)],
        weights_ref[combo, tile],
        preferred_element_type=F32,
    )


def joined(both):
    if both.shape[0] == 2 * ROWS:
        return both[0:ROWS] + both[ROWS:]
    row = lax.broadcasted_iota(jnp.int32, both.shape, 0)
    return both + jnp.where(row == 8, pltpu.roll(both, ROWS - 1, 0), 0.0)


GROUP = 16


def apply_row(own_ref, terms, consts_ref, out_ref, out_spread_ref, beside_ref=None):
    noise = constant(consts_ref, NOISE)
    spread_ends(out_spread_ref)

    def group(g, carry):
        for j in range(GROUP):
            tile = g * GROUP + j
            here = lanes(tile)
            both = banded(*terms[0], tile)
            if beside_ref is not None:
                beside_ref[:, here] = joined(both)
            for term in terms[1:]:
                both = both + banded(*term, tile)
            total = noise * own_ref[:, here] + joined(both)
            out_ref[:, here] = total
            spread_tile(total, out_spread_ref, tile)
        return carry

    lax.fori_loop(0, GX // GROUP, group, 0)


def two_sum(a, b):
    total = a + b
    part = total - a
    return total, (a - (total - part)) + (b - part)


def quick_sum(a, b):
    total = a + b
    return total, b - (total - a)


def halves(a):
    scaled = 4097.0 * a
    high = scaled - (scaled - a)
    return high, a - high


def two_product(a, b):
    a1, a2 = halves(a)
    b1, b2 = halves(b)
    product = a * b
    return product, ((a1 * b1 - product) + a1 * b2 + a2 * b1) + a2 * b2


class Pair:
    def __init__(self, high, low):
        self.high, self.low = high, low

    def __add__(self, other):
        total, error = two_sum(self.high, other.high)
        return Pair(*quick_sum(total, error + (self.low + other.low)))

    def __neg__(self):
        return Pair(-self.high, -self.low)

    def __sub__(self, other):
        return self + (-other)

    def __mul__(self, other):
        if not isinstance(other, Pair):
            return Pair(self.high * other, self.low * other)
        product, error = two_product(self.high, other.high)
        return Pair(*quick_sum(product, error + (self.high * other.low + self.low * other.high)))

    def __truediv__(self, other):
        first = self.high / other.high
        rest = self - other * Pair(first, jnp.zeros_like(first))
        return Pair(*quick_sum(first, rest.high / other.high))

    def where(self, keep, other):
        return Pair(jnp.where(keep, self.high, other.high), jnp.where(keep, self.low, other.low))


SUMS = 9
STRIDE = TILE // SUMS


def grid_mask(k):
    lane = lax.broadcasted_iota(jnp.int32, (ROWS, TILE), 1)
    row = lax.broadcasted_iota(jnp.int32, (ROWS, TILE), 0)
    return (lane == row + STRIDE * k) & (row < RHS)


def accumulate(sums, term):
    total, left = two_sum(sums[0], term)
    return total, sums[1] + left


def lines(sums, first):
    row = lax.broadcasted_iota(jnp.int32, (8, TILE), 0)
    lane = lax.broadcasted_iota(jnp.int32, (8, TILE), 1)
    blocks = [[(high[0:8], low[0:8]), lane == row + STRIDE * (first + k)] for k, (high, low) in enumerate(sums)]
    for start in range(0, len(sums), 8):
        last = [jnp.zeros((8, TILE), F32), jnp.zeros((8, TILE), F32)]
        group = sums[start : start + 8]
        for k, pair in enumerate(group):
            last = [jnp.where(row == k, jnp.broadcast_to(v[8:9], (8, TILE)), t) for v, t in zip(pair, last)]
        mask = (lane == 8 + STRIDE * (first + start + row)) & (row < len(group))
        blocks.append([tuple(last), mask])
    placed = [jnp.zeros((8, TILE), F32), jnp.zeros((8, TILE), F32)]
    for (high, low), mask in blocks:
        for shift in (64, 32, 16, 8, 4, 2, 1):
            high, left = two_sum(high, pltpu.roll(high, shift, 1))
            low = (low + pltpu.roll(low, shift, 1)) + left
        high, low = quick_sum(high, low)
        placed = [jnp.where(mask, high, placed[0]), jnp.where(mask, low, placed[1])]
    return [jnp.sum(p, axis=0, keepdims=True) for p in placed]


def inner_kernel(
    first_ref, second_ref, consts_ref, left_ref, right_ref, spread0_ref, spread1_ref, feats_ref
):
    rows = feature_rows()
    for slot, (own_ref, weights_ref, spread_ref) in enumerate(
        ((first_ref, left_ref, spread0_ref), (second_ref, right_ref, spread1_ref))
    ):
        source_features(own_ref, constant(consts_ref, FACTOR), rows, feats_ref)
        targets = ((first_ref, slot, weights_ref, 0), (second_ref, slot - 1, weights_ref, 1))
        fill_weights(targets, feats_ref, consts_ref, rows)
        spread_sides(own_ref, spread_ref)


def outer_kernel(
    slot,
    other_ref,
    own_ref,
    consts_ref,
    left_ref,
    right_ref,
    spread0_ref,
    spread1_ref,
    weights_ref,
    out_ref,
    out_spread_ref,
    beside_ref,
    feats_ref,
    spread_ref,
):
    rows = feature_rows()
    source_features(other_ref, constant(consts_ref, FACTOR), rows, feats_ref)
    fill_weights(((own_ref, 2 * slot - 1, weights_ref, 0),), feats_ref, consts_ref, rows)
    spread_sides(other_ref, spread_ref)
    terms = ((spread_ref, weights_ref, 0), (spread0_ref, left_ref, slot), (spread1_ref, right_ref, slot))
    apply_row(own_ref, terms, consts_ref, out_ref, out_spread_ref, beside_ref)


def product_kernel(
    other_ref,
    own_ref,
    consts_ref,
    left_ref,
    right_ref,
    weights_ref,
    spread0_ref,
    spread1_ref,
    out_ref,
    out_spread_ref,
    spread_ref,
):
    spread(other_ref, spread_ref)
    terms = ((spread_ref, weights_ref, 0), (spread0_ref, left_ref, 0), (spread1_ref, right_ref, 0))
    apply_row(own_ref, terms, consts_ref, out_ref, out_spread_ref)


def gram_kernel(
    below_ref,
    b0_ref,
    b1_ref,
    f0_ref,
    f1_ref,
    g0_ref,
    b_beside_ref,
    consts_ref,
    left_ref,
    right_ref,
    under_ref,
    f0_spread_ref,
    f1_spread_ref,
    g0_spread_ref,
    g1_ref,
    sums_ref,
    spread_ref,
    g1_spread_ref,
    f_beside_ref,
):
    spread(below_ref, spread_ref)
    terms = ((spread_ref, under_ref, 0), (f0_spread_ref, left_ref, 1), (f1_spread_ref, right_ref, 1))
    apply_row(f1_ref, terms, consts_ref, g1_ref, g1_spread_ref, f_beside_ref)
    zero = jnp.zeros((ROWS, TILE), F32)
    noise = constant(consts_ref, NOISE)

    def group(g, sums):
        sums = list(sums)
        terms = [zero] * SUMS
        for j in range(8):
            tile = g * 8 + j
            here = lanes(tile)
            for half, refs in enumerate(((b0_ref, f0_ref, g0_ref), (b1_ref, f1_ref, g1_ref))):
                v = [ref[:, here] for ref in refs]
                for k, (i, m) in enumerate(((0, 0), (0, 1), (0, 2), (1, 1), (1, 2), (2, 2))):
                    terms[k] = terms[k] + v[i] * v[m]
                both = banded(g0_spread_ref, left_ref, half, tile)
                both = both + banded(g1_spread_ref, right_ref, half, tile)
                image = noise * v[2] + joined(both)
                for k in range(3):
                    terms[6 + k] = terms[6 + k] + v[k] * image
                if half == 1:
                    terms[6] = terms[6] + v[2] * b_beside_ref[:, here]
                    terms[7] = terms[7] + v[2] * f_beside_ref[:, here]
            if j % 2 == 1:
                sums = [accumulate(s, t) for s, t in zip(sums, terms)]
                terms = [zero] * SUMS
        return tuple(sums)

    high, low = lines(lax.fori_loop(0, GX // 8, group, ((zero, zero),) * SUMS), 0)
    sums_ref[0:1, :] = high
    sums_ref[1:2, :] = low


def moment_kernel(sums_ref, below_ref, b_ref, f_ref, g_ref, weights_ref, out_ref, spread_ref):
    spread(below_ref, spread_ref)
    zero = jnp.zeros((ROWS, TILE), F32)
    sums, terms = [(zero, zero)] * 3, [zero] * 3
    for tile in range(GX):
        here = slice(tile * TILE, (tile + 1) * TILE)
        image = joined(banded(spread_ref, weights_ref, 0, tile))
        factors = (b_ref[:, here], f_ref[:, here], 2.0 * g_ref[:, here])
        terms = [t + v * image for t, v in zip(terms, factors)]
        if tile % 4 == 3:
            sums, terms = [accumulate(s, t) for s, t in zip(sums, terms)], [zero] * 3
    high, low = lines(sums, 6)
    total, left = two_sum(sums_ref[0:1, :], high)
    both = jnp.concatenate([total, left + (low + sums_ref[1:2, :])], axis=1)
    out_ref[...] = jnp.broadcast_to(both[None], out_ref.shape)


def finish_kernel(
    points,
    cell_hbm,
    consts_ref,
    parts_ref,
    b0_ref,
    b1_ref,
    f0_ref,
    f1_ref,
    g0_ref,
    g1_ref,
    out_ref,
    quad_ref,
    cell_ref,
    grid_ref,
    sem,
):
    copy = pltpu.make_async_copy(cell_hbm, cell_ref, sem)
    copy.start()
    high, low = parts_ref[:, 0, 0:TILE], parts_ref[:, 0, TILE:]
    while high.shape[0] > 8:
        half = high.shape[0] // 2
        high, left = two_sum(high[:half], high[half:])
        low = (low[:half] + low[half:]) + left
    for shift in (4, 2, 1):
        high, left = two_sum(high, pltpu.roll(high, shift, 0))
        low = (low + pltpu.roll(low, shift, 0)) + left
    high, low = quick_sum(high, low)
    bb, bf, bg, ff, fg, gg, bag, fag, gag = (
        Pair(high, low)
        if k == 0
        else Pair(pltpu.roll(high, TILE - STRIDE * k, 1), pltpu.roll(low, TILE - STRIDE * k, 1))
        for k in range(SUMS)
    )
    zero = jnp.zeros_like(high)
    none = Pair(zero, zero)
    one = Pair(zero + 1.0, zero)
    most = jnp.broadcast_to(1.0 / constant(consts_ref, NOISE), high.shape)

    floor = bb.high * 1e-11

    def step(square, product):
        good = (square.high > floor) & (product.high > 0.0)
        ratio = square / product.where(good, one)
        fits = ratio.high < most
        return ratio.where(fits, Pair(most, zero)).where(good, none), good

    def over(a, b, good):
        return (a / b.where(good, one)).where(good, none)

    alpha0, good0 = step(bb, bf)
    rr1 = bb - alpha0 * (bf * 2.0 - alpha0 * ff)
    beta0 = over(rr1, bb, good0)
    p0, p1 = one + beta0, -alpha0
    alpha1, good1 = step(rr1, p0 * (p0 * bf + p1 * (bg + ff)) + p1 * p1 * fg)
    r1, r2 = -(alpha0 + alpha1 * p0), -(alpha1 * p1)
    rr2 = bb + r1 * (bf * 2.0 + r1 * ff) + r2 * (bg * 2.0 + r1 * fg * 2.0 + r2 * gg)
    beta1 = over(rr2, rr1, good1)
    q0, q1, q2 = one + beta1 * p0, r1 + beta1 * p1, r2
    alpha2, good2 = step(
        rr2,
        q0 * (q0 * bf + q1 * (bg + ff) + q2 * (fg + bag)) + q1 * (q1 * fg + q2 * (gg + fag)) + q2 * q2 * gag,
    )
    alpha2 = alpha2.where(good1, none)
    on_b = alpha0 + alpha1 * p0 + alpha2 * q0
    on_f = alpha1 * p1 + alpha2 * q1
    on_g = alpha2 * q2
    quad = on_b * bb + on_f * bf + on_g * bg
    quad_ref[...] = (quad.high / points)[0:1, 0:RHS]
    mask = grid_mask(0)
    c0, c1, c2 = (
        jnp.broadcast_to(
            jnp.sum(
                jnp.where(mask, jnp.concatenate([c.high, c.high], axis=0), 0.0), axis=1, keepdims=True
            ),
            (ROWS, TILE),
        )
        for c in (on_b, on_f, on_g)
    )
    for half, (b_ref, f_ref, g_ref) in enumerate(
        ((b0_ref, f0_ref, g0_ref), (b1_ref, f1_ref, g1_ref))
    ):
        for tile in range(GX):
            here = slice(tile * TILE, (tile + 1) * TILE)
            grid_ref[half * GX + tile] = (
                c0 * b_ref[:, here] + c1 * f_ref[:, here] + c2 * g_ref[:, here]
            )
    copy.wait()
    for s in range(cell_ref.shape[0]):
        out_ref[:, s * TILE : (s + 1) * TILE] = grid_ref[cell_ref[s], 0:RHS, :]


def shards(offsets, tile_cell, probes, target, lengthscale, amplitude, noise):
    size = lax.axis_size("rows")
    points = size * tile_cell.shape[0] * TILE
    down = [(i, i + 1) for i in range(size - 1)]
    up = [(i + 1, i) for i in range(size - 1)]

    tiles = tile_cell.shape[0]
    first, second, consts = call(
        pack_kernel,
        "pack",
        (pltpu.VMEM((ROWS, WIDE), F32), pltpu.VMEM((ROWS, WIDE), F32), pltpu.VMEM((8, TILE), F32)),
        [HBM] * 4 + [SMEM] * 3,
        [
            pltpu.SMEM((tiles,), jnp.int32),
            pltpu.SMEM((tiles,), jnp.int32),
            pltpu.VMEM((2, tiles * TILE), F32),
            pltpu.VMEM((8, tiles * TILE), jnp.int32),
            pltpu.VMEM((1, tiles * TILE), F32),
            pltpu.SemaphoreType.DMA((4,)),
        ],
        flops=1 << 20,
        limit=60.5,
    )(
        tile_cell,
        offsets,
        probes,
        target.reshape(1, -1),
        lengthscale,
        amplitude,
        noise,
    )

    def outer(slot, other, own):
        return call(
            lambda *refs: outer_kernel(slot, *refs),
            f"outer{slot}",
            (weight_rows(1), grid_row(), spread_row(), grid_row()),
            [VMEM] * 7,
            [feature_tiles(), spread_row(ROWS)],
            flops=1 << 30,
        )(other, own, consts, left, right, b0_spread, b1_spread)

    above = lax.ppermute(second, "rows", down)
    below = lax.ppermute(first, "rows", up)
    left, right, b0_spread, b1_spread = call(
        inner_kernel,
        "inner",
        (weight_rows(2), weight_rows(2), spread_row(ROWS), spread_row(ROWS)),
        [VMEM] * 3,
        [feature_tiles()],
        flops=1 << 30,
    )(first, second, consts)
    over, f0, f0_spread, _ = outer(0, above, first)
    f_below = lax.ppermute(f0, "rows", up)
    under, f1, f1_spread, b_beside = outer(1, below, second)
    f_above = lax.ppermute(f1, "rows", down)
    g0, g0_spread = call(
        product_kernel,
        "product",
        (grid_row(), spread_row()),
        [VMEM] * 8,
        [spread_row()],
        flops=1 << 29,
    )(f_above, f0, consts, left, right, over, f0_spread, f1_spread)
    g_below = lax.ppermute(g0, "rows", up)
    g1, sums = call(
        gram_kernel,
        "gram",
        (grid_row(), jax.ShapeDtypeStruct((2, TILE), F32)),
        [VMEM] * 14,
        [spread_row(), spread_row(), pltpu.VMEM((ROWS, WIDE), F32)],
        flops=1 << 29,
    )(f_below, first, second, f0, f1, g0, b_beside, consts, left, right, under, f0_spread, f1_spread, g0_spread)
    parts = call(
        moment_kernel,
        "moment",
        jax.ShapeDtypeStruct((size, 1, 2 * TILE), F32),
        [VMEM] * 6,
        [spread_row()],
        flops=1 << 29,
    )(sums, g_below, second, f1, g1, under)
    parts = lax.all_to_all(parts, "rows", split_axis=0, concat_axis=0, tiled=True)

    solutions, quad = call(
        lambda *refs: finish_kernel(float(points), *refs),
        "finish",
        (
            jax.ShapeDtypeStruct((RHS, tiles * TILE), F32),
            jax.ShapeDtypeStruct((1, RHS), F32),
        ),
        [HBM] + [VMEM] * 8,
        [
            pltpu.SMEM((tiles,), jnp.int32),
            pltpu.VMEM((tiles, ROWS, TILE), F32),
            pltpu.SemaphoreType.DMA,
        ],
        flops=1 << 20,
    )(tile_cell, consts, parts, first, second, f0, f1, g0, g1)
    return (solutions, quad.reshape(RHS))


def solution(mesh):
    return jax.shard_map(
        shards,
        mesh=mesh,
        in_specs=(
            P(None, "rows"),
            P("rows"),
            P(None, "rows"),
            P("rows"),
            P("hyp"),
            P("hyp"),
            P("hyp"),
        ),
        out_specs=(P("hyp", "rows"), P("hyp")),
        check_vma=False,
    )
```

```python
import jax
import jax.numpy as jnp
from jax import lax
from jax.experimental import pallas as pl
from jax.experimental.pallas import tpu as pltpu
from jax.sharding import PartitionSpec as P

TILE = 128
GX = 16
RHS = 9
ROWS = 16
WIDE = GX * TILE
FEATURES = 32
PAD = GX + 2
BAND = 3 * 2 * TILE
F32 = jnp.float32
BF16 = jnp.bfloat16
TINY = 1e-30

VMEM = pl.BlockSpec(memory_space=pltpu.VMEM)
HBM = pl.BlockSpec(memory_space=pltpu.HBM)
SMEM = pl.BlockSpec(memory_space=pltpu.SMEM)
REACH, TOP, FACTOR, NOISE = range(4)


def call(kernel, name, out_shape, in_specs, scratch=(), flops=0, limit=12):
    return pl.pallas_call(
        kernel,
        name=name,
        out_shape=out_shape,
        in_specs=in_specs,
        out_specs=jax.tree.map(lambda _: VMEM, out_shape),
        scratch_shapes=list(scratch),
        cost_estimate=pl.CostEstimate(flops=flops, bytes_accessed=1 << 20, transcendentals=0),
        compiler_params=pltpu.CompilerParams(vmem_limit_bytes=int(limit * 2**20)),
    )


def grid_row():
    return jax.ShapeDtypeStruct((ROWS, WIDE), F32)


def spread_row(rows=2 * ROWS):
    return pltpu.VMEM((rows, PAD * 2 * TILE), BF16)


def weight_rows(count):
    return pltpu.VMEM((count, GX, BAND, TILE), BF16)


def feature_tiles():
    return pltpu.VMEM((PAD, TILE, FEATURES), BF16)


def lanes(tile, width=TILE):
    return pl.ds(pl.multiple_of(tile * width, width), width)


def pack_kernel(
    cell_hbm,
    offsets_hbm,
    probes_hbm,
    target_hbm,
    scale_ref,
    amp_ref,
    noise_ref,
    first_ref,
    second_ref,
    consts_ref,
    cell_ref,
    from_ref,
    offsets_ref,
    probes_ref,
    target_ref,
    sems,
):
    copies = [
        pltpu.make_async_copy(source, dest, sems.at[i])
        for i, (source, dest) in enumerate(
            (
                (cell_hbm, cell_ref),
                (offsets_hbm, offsets_ref),
                (probes_hbm, probes_ref),
                (target_hbm, target_ref),
            )
        )
    ]
    for copy in copies:
        copy.start()
    for copy in copies:
        copy.wait()
    for s in range(cell_ref.shape[0]):
        from_ref[cell_ref[s]] = s
    filler = jnp.zeros((ROWS - RHS - 2, TILE), F32)
    for cell in range(cell_ref.shape[0]):
        stored = lanes(from_ref[cell])
        here = slice(cell % GX * TILE, (cell % GX + 1) * TILE)
        ref = (first_ref, second_ref)[cell // GX]
        ref[0:8, here] = 2.0 * probes_ref[:, stored].astype(F32) - 1.0
        ref[8:16, here] = jnp.concatenate(
            [target_ref[:, stored], offsets_ref[:, stored], filler], axis=0
        )
    amp = jnp.full((1, TILE), amp_ref[0], F32)
    reach = jnp.exp(0.2 * jnp.log(4.0 * amp))
    square = reach * reach
    consts_ref[REACH : REACH + 1, :] = reach
    consts_ref[TOP : TOP + 1, :] = 5.0 * amp / (square * square)
    consts_ref[FACTOR : FACTOR + 1, :] = reach / jnp.full((1, TILE), scale_ref[0], F32)
    consts_ref[NOISE : NOISE + 1, :] = jnp.full((1, TILE), noise_ref[0], F32)


def constant(consts_ref, which):
    return consts_ref[which : which + 1, :]


def split_rows(values, level):
    first = values.astype(BF16).astype(F32)
    rest = values - first
    second = rest.astype(BF16).astype(F32)
    third = rest - second
    return jnp.where(level == 0, first, jnp.where(level == 1, second, third))


def feature_rows():
    row = lax.broadcasted_iota(jnp.int32, (FEATURES, TILE), 0)

    def level(order):
        out = jnp.zeros_like(row)
        for k, v in enumerate(order):
            if v:
                out = jnp.where(row == k, v, out)
        return out

    source = level([0, 0, 1, 1, 0, 2] * 2 + [0, 1, 2] + [0, 0, 0])
    target = level([0, 1, 0, 1, 2, 0] * 2 + [0, 0, 0] + [0, 1, 2])
    kind = jnp.where(row < 6, 0, jnp.where(row < 12, 1, jnp.where(row < 15, 2, jnp.where(row < 18, 3, 4))))
    return kind, source, target


def choose(kind, a, b, c, d):
    return jnp.where(
        kind == 0, a, jnp.where(kind == 1, b, jnp.where(kind == 2, c, jnp.where(kind == 3, d, 0.0)))
    )


def source_features(row_ref, factor, rows, out_ref):
    kind, source, _ = rows
    zero = jnp.zeros((TILE, FEATURES), BF16)
    out_ref[0] = zero
    out_ref[PAD - 1] = zero

    def one(tile, carry):
        a = factor * (row_ref[9:10, lanes(tile)] - 0.5)
        b = factor * (row_ref[10:11, lanes(tile)] - 0.5)
        values = choose(kind, a, b, a * a + b * b, 1.0)
        out_ref[tile + 1] = split_rows(values, source).T.astype(BF16)
        return carry

    lax.fori_loop(0, GX, one, 0, unroll=8)


def target_features(row_ref, tile, row_shift, col_shift, factor, rows):
    kind, _, target = rows
    a = factor * ((row_shift + 0.5) - row_ref[9:10, lanes(tile)])
    b = factor * ((col_shift + 0.5) - row_ref[10:11, lanes(tile)])
    values = choose(kind, 2.0 * a, 2.0 * b, 1.0, a * a + b * b)
    return split_rows(values, target).astype(BF16)


def fill_weights(targets, feats_ref, consts_ref, rows):
    factor = constant(consts_ref, FACTOR)
    reach = jnp.broadcast_to(constant(consts_ref, REACH), (TILE, TILE))
    top = jnp.broadcast_to(constant(consts_ref, TOP), (TILE, TILE))

    def one(tile, carry):
        for k in range(3):
            wanted = [
                target_features(ref, tile, float(row_shift), float(k - 1), factor, rows)
                for ref, row_shift, _, _ in targets
            ]
            squares = lax.dot_general(
                feats_ref[tile + k],
                wanted[0] if len(wanted) == 1 else jnp.concatenate(wanted, axis=1),
                (((1,), (0,)), ((), ())),
                preferred_element_type=F32,
            )
            for i, (_, _, weights_ref, combo) in enumerate(targets):
                here = jnp.maximum(squares[:, i * TILE : (i + 1) * TILE], 1e-12)
                close = jnp.maximum(reach - here * lax.rsqrt(here), 0.0)
                second = close * close
                weight = (second * second) * (top - close)
                high = weight.astype(BF16)
                low = (weight - high.astype(F32)).astype(BF16)
                base = k * 2 * TILE
                weights_ref[combo, tile, base : base + TILE, :] = high
                weights_ref[combo, tile, base + TILE : base + 2 * TILE, :] = low
        return carry

    lax.fori_loop(0, GX, one, 0, unroll=8 // len(targets))


def spread_ends(out_ref):
    empty = jnp.zeros((2 * ROWS, 2 * TILE), BF16)
    out_ref[:, 0 : 2 * TILE] = empty
    out_ref[:, (PAD - 1) * 2 * TILE :] = empty


def spread_tile(values, out_ref, tile):
    high = values.astype(BF16)
    low = (values - high.astype(F32)).astype(BF16)
    both = jnp.concatenate([high, low], axis=0)
    at = pl.multiple_of((tile + 1) * 2 * TILE, 2 * TILE)
    out_ref[:, pl.ds(at, 2 * TILE)] = jnp.concatenate([both, both], axis=1)


def spread(row_ref, out_ref):
    spread_ends(out_ref)
    for tile in range(GX):
        spread_tile(row_ref[:, tile * TILE : (tile + 1) * TILE], out_ref, tile)


def spread_sides(row_ref, out_ref):
    empty = jnp.zeros((ROWS, 2 * TILE), BF16)
    out_ref[:, 0 : 2 * TILE] = empty
    out_ref[:, (PAD - 1) * 2 * TILE :] = empty
    row = lax.broadcasted_iota(jnp.int32, (8, TILE), 0)
    for tile in range(GX):
        here = slice(tile * TILE, (tile + 1) * TILE)
        target = row_ref[8:9, here]
        high = target.astype(BF16).astype(F32)
        rest = jnp.where(row == 0, high, jnp.where(row == 1, target - high, 0.0))
        both = jnp.concatenate([row_ref[0:8, here], rest], axis=0).astype(BF16)
        at = (tile + 1) * 2 * TILE
        out_ref[:, at : at + 2 * TILE] = jnp.concatenate([both, both], axis=1)


def banded(spread_ref, weights_ref, combo, tile):
    at = pl.multiple_of(tile * 2 * TILE, 2 * TILE)
    return jnp.dot(
        spread_ref[:, pl.ds(at, BAND)],
        weights_ref[combo, tile],
        preferred_element_type=F32,
    )


def joined(both):
    if both.shape[0] == 2 * ROWS:
        return both[0:ROWS] + both[ROWS:]
    row = lax.broadcasted_iota(jnp.int32, both.shape, 0)
    return both + jnp.where(row == 8, pltpu.roll(both, ROWS - 1, 0), 0.0)


GROUP = 16


def apply_row(own_ref, terms, consts_ref, out_ref, out_spread_ref, beside_ref=None):
    noise = constant(consts_ref, NOISE)
    spread_ends(out_spread_ref)

    def group(g, carry):
        for j in range(GROUP):
            tile = g * GROUP + j
            here = lanes(tile)
            both = banded(*terms[0], tile)
            if beside_ref is not None:
                beside_ref[:, here] = joined(both)
            for term in terms[1:]:
                both = both + banded(*term, tile)
            total = noise * own_ref[:, here] + joined(both)
            out_ref[:, here] = total
            spread_tile(total, out_spread_ref, tile)
        return carry

    lax.fori_loop(0, GX // GROUP, group, 0)


def two_sum(a, b):
    total = a + b
    part = total - a
    return total, (a - (total - part)) + (b - part)


def quick_sum(a, b):
    total = a + b
    return total, b - (total - a)


def halves(a):
    scaled = 4097.0 * a
    high = scaled - (scaled - a)
    return high, a - high


def two_product(a, b):
    a1, a2 = halves(a)
    b1, b2 = halves(b)
    product = a * b
    return product, ((a1 * b1 - product) + a1 * b2 + a2 * b1) + a2 * b2


class Pair:
    def __init__(self, high, low):
        self.high, self.low = high, low

    def __add__(self, other):
        total, error = two_sum(self.high, other.high)
        return Pair(*quick_sum(total, error + (self.low + other.low)))

    def __neg__(self):
        return Pair(-self.high, -self.low)

    def __sub__(self, other):
        return self + (-other)

    def __mul__(self, other):
        if not isinstance(other, Pair):
            return Pair(self.high * other, self.low * other)
        product, error = two_product(self.high, other.high)
        return Pair(*quick_sum(product, error + (self.high * other.low + self.low * other.high)))

    def __truediv__(self, other):
        first = self.high / other.high
        rest = self - other * Pair(first, jnp.zeros_like(first))
        return Pair(*quick_sum(first, rest.high / other.high))

    def where(self, keep, other):
        return Pair(jnp.where(keep, self.high, other.high), jnp.where(keep, self.low, other.low))


SUMS = 9
STRIDE = TILE // SUMS


def grid_mask(k):
    lane = lax.broadcasted_iota(jnp.int32, (ROWS, TILE), 1)
    row = lax.broadcasted_iota(jnp.int32, (ROWS, TILE), 0)
    return (lane == row + STRIDE * k) & (row < RHS)


def accumulate(sums, term):
    total, left = two_sum(sums[0], term)
    return total, sums[1] + left


def lines(sums, first):
    row = lax.broadcasted_iota(jnp.int32, (8, TILE), 0)
    lane = lax.broadcasted_iota(jnp.int32, (8, TILE), 1)
    blocks = [[(high[0:8], low[0:8]), lane == row + STRIDE * (first + k)] for k, (high, low) in enumerate(sums)]
    for start in range(0, len(sums), 8):
        last = [jnp.zeros((8, TILE), F32), jnp.zeros((8, TILE), F32)]
        group = sums[start : start + 8]
        for k, pair in enumerate(group):
            last = [jnp.where(row == k, jnp.broadcast_to(v[8:9], (8, TILE)), t) for v, t in zip(pair, last)]
        mask = (lane == 8 + STRIDE * (first + start + row)) & (row < len(group))
        blocks.append([tuple(last), mask])
    placed = [jnp.zeros((8, TILE), F32), jnp.zeros((8, TILE), F32)]
    for (high, low), mask in blocks:
        for shift in (64, 32, 16, 8, 4, 2, 1):
            high, left = two_sum(high, pltpu.roll(high, shift, 1))
            low = (low + pltpu.roll(low, shift, 1)) + left
        high, low = quick_sum(high, low)
        placed = [jnp.where(mask, high, placed[0]), jnp.where(mask, low, placed[1])]
    return [jnp.sum(p, axis=0, keepdims=True) for p in placed]


def inner_kernel(
    first_ref, second_ref, consts_ref, left_ref, right_ref, spread0_ref, spread1_ref, feats_ref
):
    rows = feature_rows()
    for slot, (own_ref, weights_ref, spread_ref) in enumerate(
        ((first_ref, left_ref, spread0_ref), (second_ref, right_ref, spread1_ref))
    ):
        source_features(own_ref, constant(consts_ref, FACTOR), rows, feats_ref)
        targets = ((first_ref, slot, weights_ref, 0), (second_ref, slot - 1, weights_ref, 1))
        fill_weights(targets, feats_ref, consts_ref, rows)
        spread_sides(own_ref, spread_ref)


def outer_kernel(
    slot,
    other_ref,
    own_ref,
    consts_ref,
    left_ref,
    right_ref,
    spread0_ref,
    spread1_ref,
    weights_ref,
    out_ref,
    out_spread_ref,
    *more,
):
    beside_ref, feats_ref, spread_ref = more if slot else (None, *more)
    rows = feature_rows()
    source_features(other_ref, constant(consts_ref, FACTOR), rows, feats_ref)
    fill_weights(((own_ref, 2 * slot - 1, weights_ref, 0),), feats_ref, consts_ref, rows)
    spread_sides(other_ref, spread_ref)
    terms = ((spread_ref, weights_ref, 0), (spread0_ref, left_ref, slot), (spread1_ref, right_ref, slot))
    apply_row(own_ref, terms, consts_ref, out_ref, out_spread_ref, beside_ref)


def product_kernel(
    other_ref,
    own_ref,
    consts_ref,
    left_ref,
    right_ref,
    weights_ref,
    spread0_ref,
    spread1_ref,
    out_ref,
    out_spread_ref,
    spread_ref,
):
    spread(other_ref, spread_ref)
    terms = ((spread_ref, weights_ref, 0), (spread0_ref, left_ref, 0), (spread1_ref, right_ref, 0))
    apply_row(own_ref, terms, consts_ref, out_ref, out_spread_ref)


def gram_kernel(
    below_ref,
    b0_ref,
    b1_ref,
    f0_ref,
    f1_ref,
    g0_ref,
    b_beside_ref,
    consts_ref,
    left_ref,
    right_ref,
    under_ref,
    f0_spread_ref,
    f1_spread_ref,
    g0_spread_ref,
    g1_ref,
    sums_ref,
    spread_ref,
    g1_spread_ref,
    f_beside_ref,
):
    spread(below_ref, spread_ref)
    terms = ((spread_ref, under_ref, 0), (f0_spread_ref, left_ref, 1), (f1_spread_ref, right_ref, 1))
    apply_row(f1_ref, terms, consts_ref, g1_ref, g1_spread_ref, f_beside_ref)
    zero = jnp.zeros((ROWS, TILE), F32)
    noise = constant(consts_ref, NOISE)

    def group(g, sums):
        sums = list(sums)
        terms = [zero] * SUMS
        for j in range(8):
            tile = g * 8 + j
            here = lanes(tile)
            for half, refs in enumerate(((b0_ref, f0_ref, g0_ref), (b1_ref, f1_ref, g1_ref))):
                v = [ref[:, here] for ref in refs]
                for k, (i, m) in enumerate(((0, 0), (0, 1), (0, 2), (1, 1), (1, 2), (2, 2))):
                    terms[k] = terms[k] + v[i] * v[m]
                both = banded(g0_spread_ref, left_ref, half, tile)
                both = both + banded(g1_spread_ref, right_ref, half, tile)
                image = noise * v[2] + joined(both)
                for k in range(3):
                    terms[6 + k] = terms[6 + k] + v[k] * image
                if half == 1:
                    terms[6] = terms[6] + v[2] * b_beside_ref[:, here]
                    terms[7] = terms[7] + v[2] * f_beside_ref[:, here]
            if j % 2 == 1:
                sums = [accumulate(s, t) for s, t in zip(sums, terms)]
                terms = [zero] * SUMS
        return tuple(sums)

    high, low = lines(lax.fori_loop(0, GX // 8, group, ((zero, zero),) * SUMS), 0)
    sums_ref[0:1, :] = high
    sums_ref[1:2, :] = low


def moment_kernel(sums_ref, below_ref, b_ref, f_ref, g_ref, weights_ref, out_ref, spread_ref):
    spread(below_ref, spread_ref)
    zero = jnp.zeros((ROWS, TILE), F32)
    sums, terms = [(zero, zero)] * 3, [zero] * 3
    for tile in range(GX):
        here = slice(tile * TILE, (tile + 1) * TILE)
        image = joined(banded(spread_ref, weights_ref, 0, tile))
        factors = (b_ref[:, here], f_ref[:, here], 2.0 * g_ref[:, here])
        terms = [t + v * image for t, v in zip(terms, factors)]
        if tile % 4 == 3:
            sums, terms = [accumulate(s, t) for s, t in zip(sums, terms)], [zero] * 3
    high, low = lines(sums, 6)
    total, left = two_sum(sums_ref[0:1, :], high)
    both = jnp.concatenate([total, left + (low + sums_ref[1:2, :])], axis=1)
    out_ref[...] = jnp.broadcast_to(both[None], out_ref.shape)


def finish_kernel(
    points,
    cell_hbm,
    consts_ref,
    parts_ref,
    b0_ref,
    b1_ref,
    f0_ref,
    f1_ref,
    g0_ref,
    g1_ref,
    out_ref,
    quad_ref,
    cell_ref,
    grid_ref,
    sem,
):
    copy = pltpu.make_async_copy(cell_hbm, cell_ref, sem)
    copy.start()
    high, low = parts_ref[:, 0, 0:TILE], parts_ref[:, 0, TILE:]
    while high.shape[0] > 8:
        half = high.shape[0] // 2
        high, left = two_sum(high[:half], high[half:])
        low = (low[:half] + low[half:]) + left
    for shift in (4, 2, 1):
        high, left = two_sum(high, pltpu.roll(high, shift, 0))
        low = (low + pltpu.roll(low, shift, 0)) + left
    high, low = quick_sum(high, low)
    bb, bf, bg, ff, fg, gg, bag, fag, gag = (
        Pair(high, low)
        if k == 0
        else Pair(pltpu.roll(high, TILE - STRIDE * k, 1), pltpu.roll(low, TILE - STRIDE * k, 1))
        for k in range(SUMS)
    )
    zero = jnp.zeros_like(high)
    none = Pair(zero, zero)
    one = Pair(zero + 1.0, zero)
    most = jnp.broadcast_to(1.0 / constant(consts_ref, NOISE), high.shape)

    floor = bb.high * 1e-11

    def step(square, product):
        good = (square.high > floor) & (product.high > 0.0)
        ratio = square / product.where(good, one)
        fits = ratio.high < most
        return ratio.where(fits, Pair(most, zero)).where(good, none), good

    def over(a, b, good):
        return (a / b.where(good, one)).where(good, none)

    alpha0, good0 = step(bb, bf)
    rr1 = bb - alpha0 * (bf * 2.0 - alpha0 * ff)
    beta0 = over(rr1, bb, good0)
    p0, p1 = one + beta0, -alpha0
    alpha1, good1 = step(rr1, p0 * (p0 * bf + p1 * (bg + ff)) + p1 * p1 * fg)
    r1, r2 = -(alpha0 + alpha1 * p0), -(alpha1 * p1)
    rr2 = bb + r1 * (bf * 2.0 + r1 * ff) + r2 * (bg * 2.0 + r1 * fg * 2.0 + r2 * gg)
    beta1 = over(rr2, rr1, good1)
    q0, q1, q2 = one + beta1 * p0, r1 + beta1 * p1, r2
    alpha2, good2 = step(
        rr2,
        q0 * (q0 * bf + q1 * (bg + ff) + q2 * (fg + bag)) + q1 * (q1 * fg + q2 * (gg + fag)) + q2 * q2 * gag,
    )
    alpha2 = alpha2.where(good1, none)
    on_b = alpha0 + alpha1 * p0 + alpha2 * q0
    on_f = alpha1 * p1 + alpha2 * q1
    on_g = alpha2 * q2
    quad = on_b * bb + on_f * bf + on_g * bg
    quad_ref[...] = (quad.high / points)[0:1, 0:RHS]
    mask = grid_mask(0)
    c0, c1, c2 = (
        jnp.broadcast_to(
            jnp.sum(
                jnp.where(mask, jnp.concatenate([c.high, c.high], axis=0), 0.0), axis=1, keepdims=True
            ),
            (ROWS, TILE),
        )
        for c in (on_b, on_f, on_g)
    )
    for half, (b_ref, f_ref, g_ref) in enumerate(
        ((b0_ref, f0_ref, g0_ref), (b1_ref, f1_ref, g1_ref))
    ):
        for tile in range(GX):
            here = slice(tile * TILE, (tile + 1) * TILE)
            grid_ref[half * GX + tile] = (
                c0 * b_ref[:, here] + c1 * f_ref[:, here] + c2 * g_ref[:, here]
            )
    copy.wait()
    for s in range(cell_ref.shape[0]):
        out_ref[:, s * TILE : (s + 1) * TILE] = grid_ref[cell_ref[s], 0:RHS, :]


def shards(offsets, tile_cell, probes, target, lengthscale, amplitude, noise):
    size = lax.axis_size("rows")
    points = size * tile_cell.shape[0] * TILE
    down = [(i, i + 1) for i in range(size - 1)]
    up = [(i + 1, i) for i in range(size - 1)]

    tiles = tile_cell.shape[0]
    first, second, consts = call(
        pack_kernel,
        "pack",
        (pltpu.VMEM((ROWS, WIDE), F32), pltpu.VMEM((ROWS, WIDE), F32), pltpu.VMEM((8, TILE), F32)),
        [HBM] * 4 + [SMEM] * 3,
        [
            pltpu.SMEM((tiles,), jnp.int32),
            pltpu.SMEM((tiles,), jnp.int32),
            pltpu.VMEM((2, tiles * TILE), F32),
            pltpu.VMEM((8, tiles * TILE), jnp.int32),
            pltpu.VMEM((1, tiles * TILE), F32),
            pltpu.SemaphoreType.DMA((4,)),
        ],
        flops=1 << 20,
        limit=60.5,
    )(
        tile_cell,
        offsets,
        probes,
        target.reshape(1, -1),
        lengthscale,
        amplitude,
        noise,
    )

    def outer(slot, other, own):
        return call(
            lambda *refs: outer_kernel(slot, *refs),
            f"outer{slot}",
            (weight_rows(1), grid_row(), spread_row()) + (grid_row(),) * slot,
            [VMEM] * 7,
            [feature_tiles(), spread_row(ROWS)],
            flops=1 << 30,
        )(other, own, consts, left, right, b0_spread, b1_spread)

    above = lax.ppermute(second, "rows", down)
    below = lax.ppermute(first, "rows", up)
    left, right, b0_spread, b1_spread = call(
        inner_kernel,
        "inner",
        (weight_rows(2), weight_rows(2), spread_row(ROWS), spread_row(ROWS)),
        [VMEM] * 3,
        [feature_tiles()],
        flops=1 << 30,
    )(first, second, consts)
    over, f0, f0_spread = outer(0, above, first)
    f_below = lax.ppermute(f0, "rows", up)
    under, f1, f1_spread, b_beside = outer(1, below, second)
    f_above = lax.ppermute(f1, "rows", down)
    g0, g0_spread = call(
        product_kernel,
        "product",
        (grid_row(), spread_row()),
        [VMEM] * 8,
        [spread_row()],
        flops=1 << 29,
    )(f_above, f0, consts, left, right, over, f0_spread, f1_spread)
    g_below = lax.ppermute(g0, "rows", up)
    g1, sums = call(
        gram_kernel,
        "gram",
        (grid_row(), jax.ShapeDtypeStruct((2, TILE), F32)),
        [VMEM] * 14,
        [spread_row(), spread_row(), pltpu.VMEM((ROWS, WIDE), F32)],
        flops=1 << 29,
    )(f_below, first, second, f0, f1, g0, b_beside, consts, left, right, under, f0_spread, f1_spread, g0_spread)
    parts = call(
        moment_kernel,
        "moment",
        jax.ShapeDtypeStruct((size, 1, 2 * TILE), F32),
        [VMEM] * 6,
        [spread_row()],
        flops=1 << 29,
    )(sums, g_below, second, f1, g1, under)
    parts = lax.all_to_all(parts, "rows", split_axis=0, concat_axis=0, tiled=True)

    solutions, quad = call(
        lambda *refs: finish_kernel(float(points), *refs),
        "finish",
        (
            jax.ShapeDtypeStruct((RHS, tiles * TILE), F32),
            jax.ShapeDtypeStruct((1, RHS), F32),
        ),
        [HBM] + [VMEM] * 8,
        [
            pltpu.SMEM((tiles,), jnp.int32),
            pltpu.VMEM((tiles, ROWS, TILE), F32),
            pltpu.SemaphoreType.DMA,
        ],
        flops=1 << 20,
    )(tile_cell, consts, parts, first, second, f0, f1, g0, g1)
    return (solutions, quad.reshape(RHS))


def solution(mesh):
    return jax.shard_map(
        shards,
        mesh=mesh,
        in_specs=(
            P(None, "rows"),
            P("rows"),
            P(None, "rows"),
            P("rows"),
            P("hyp"),
            P("hyp"),
            P("hyp"),
        ),
        out_specs=(P("hyp", "rows"), P("hyp")),
        check_vma=False,
    )
```

```python
import jax
import jax.numpy as jnp
from jax import lax
from jax.experimental import pallas as pl
from jax.experimental.pallas import tpu as pltpu
from jax.sharding import PartitionSpec as P

TILE = 128
GX = 16
RHS = 9
ROWS = 16
WIDE = GX * TILE
FEATURES = 32
PAD = GX + 2
BAND = 3 * 2 * TILE
F32 = jnp.float32
BF16 = jnp.bfloat16
TINY = 1e-30

VMEM = pl.BlockSpec(memory_space=pltpu.VMEM)
HBM = pl.BlockSpec(memory_space=pltpu.HBM)
SMEM = pl.BlockSpec(memory_space=pltpu.SMEM)
REACH, TOP, FACTOR, NOISE = range(4)


def call(kernel, name, out_shape, in_specs, scratch=(), flops=0, limit=12):
    return pl.pallas_call(
        kernel,
        name=name,
        out_shape=out_shape,
        in_specs=in_specs,
        out_specs=jax.tree.map(lambda _: VMEM, out_shape),
        scratch_shapes=list(scratch),
        cost_estimate=pl.CostEstimate(flops=flops, bytes_accessed=1 << 20, transcendentals=0),
        compiler_params=pltpu.CompilerParams(vmem_limit_bytes=int(limit * 2**20)),
    )


def grid_row():
    return jax.ShapeDtypeStruct((ROWS, WIDE), F32)


def spread_row(rows=2 * ROWS):
    return pltpu.VMEM((rows, PAD * 2 * TILE), BF16)


def weight_rows(count):
    return pltpu.VMEM((count, GX, BAND, TILE), BF16)


def feature_tiles():
    return pltpu.VMEM((PAD, TILE, FEATURES), BF16)


def lanes(tile, width=TILE):
    return pl.ds(pl.multiple_of(tile * width, width), width)


def pack_kernel(
    cell_hbm,
    offsets_hbm,
    probes_hbm,
    target_hbm,
    scale_ref,
    amp_ref,
    noise_ref,
    first_ref,
    second_ref,
    consts_ref,
    cell_ref,
    from_ref,
    offsets_ref,
    probes_ref,
    target_ref,
    sems,
):
    copies = [
        pltpu.make_async_copy(source, dest, sems.at[i])
        for i, (source, dest) in enumerate(
            (
                (cell_hbm, cell_ref),
                (offsets_hbm, offsets_ref),
                (probes_hbm, probes_ref),
                (target_hbm, target_ref),
            )
        )
    ]
    for copy in copies:
        copy.start()
    for copy in copies:
        copy.wait()
    for s in range(cell_ref.shape[0]):
        from_ref[cell_ref[s]] = s
    filler = jnp.zeros((ROWS - RHS - 2, TILE), F32)
    for cell in range(cell_ref.shape[0]):
        stored = lanes(from_ref[cell])
        here = slice(cell % GX * TILE, (cell % GX + 1) * TILE)
        ref = (first_ref, second_ref)[cell // GX]
        ref[0:8, here] = 2.0 * probes_ref[:, stored].astype(F32) - 1.0
        ref[8:16, here] = jnp.concatenate(
            [target_ref[:, stored], offsets_ref[:, stored], filler], axis=0
        )
    amp = jnp.full((1, TILE), amp_ref[0], F32)
    reach = jnp.exp(0.2 * jnp.log(4.0 * amp))
    square = reach * reach
    consts_ref[REACH : REACH + 1, :] = reach
    consts_ref[TOP : TOP + 1, :] = 5.0 * amp / (square * square)
    consts_ref[FACTOR : FACTOR + 1, :] = reach / jnp.full((1, TILE), scale_ref[0], F32)
    consts_ref[NOISE : NOISE + 1, :] = jnp.full((1, TILE), noise_ref[0], F32)


def constant(consts_ref, which):
    return consts_ref[which : which + 1, :]


def split_rows(values, level):
    first = values.astype(BF16).astype(F32)
    rest = values - first
    second = rest.astype(BF16).astype(F32)
    third = rest - second
    return jnp.where(level == 0, first, jnp.where(level == 1, second, third))


def feature_rows():
    row = lax.broadcasted_iota(jnp.int32, (FEATURES, TILE), 0)

    def level(order):
        out = jnp.zeros_like(row)
        for k, v in enumerate(order):
            if v:
                out = jnp.where(row == k, v, out)
        return out

    source = level([0, 0, 1, 1, 0, 2] * 2 + [0, 1, 2] + [0, 0, 0])
    target = level([0, 1, 0, 1, 2, 0] * 2 + [0, 0, 0] + [0, 1, 2])
    kind = jnp.where(row < 6, 0, jnp.where(row < 12, 1, jnp.where(row < 15, 2, jnp.where(row < 18, 3, 4))))
    return kind, source, target


def choose(kind, a, b, c, d):
    return jnp.where(
        kind == 0, a, jnp.where(kind == 1, b, jnp.where(kind == 2, c, jnp.where(kind == 3, d, 0.0)))
    )


def source_features(row_ref, factor, rows, out_ref):
    kind, source, _ = rows
    zero = jnp.zeros((TILE, FEATURES), BF16)
    out_ref[0] = zero
    out_ref[PAD - 1] = zero

    def one(tile, carry):
        a = factor * (row_ref[9:10, lanes(tile)] - 0.5)
        b = factor * (row_ref[10:11, lanes(tile)] - 0.5)
        values = choose(kind, a, b, a * a + b * b, 1.0)
        out_ref[tile + 1] = split_rows(values, source).T.astype(BF16)
        return carry

    lax.fori_loop(0, GX, one, 0, unroll=8)


def target_features(row_ref, tile, row_shift, col_shift, factor, rows):
    kind, _, target = rows
    a = factor * ((row_shift + 0.5) - row_ref[9:10, lanes(tile)])
    b = factor * ((col_shift + 0.5) - row_ref[10:11, lanes(tile)])
    values = choose(kind, 2.0 * a, 2.0 * b, 1.0, a * a + b * b)
    return split_rows(values, target).astype(BF16)


def fill_weights(targets, feats_ref, consts_ref, rows):
    factor = constant(consts_ref, FACTOR)
    reach = jnp.broadcast_to(constant(consts_ref, REACH), (TILE, TILE))
    top = jnp.broadcast_to(constant(consts_ref, TOP), (TILE, TILE))

    def one(tile, carry):
        for k in range(3):
            wanted = [
                target_features(ref, tile, float(row_shift), float(k - 1), factor, rows)
                for ref, row_shift, _, _ in targets
            ]
            squares = lax.dot_general(
                feats_ref[tile + k],
                wanted[0] if len(wanted) == 1 else jnp.concatenate(wanted, axis=1),
                (((1,), (0,)), ((), ())),
                preferred_element_type=F32,
            )
            for i, (_, _, weights_ref, combo) in enumerate(targets):
                here = jnp.maximum(squares[:, i * TILE : (i + 1) * TILE], 1e-12)
                close = jnp.maximum(reach - here * lax.rsqrt(here), 0.0)
                second = close * close
                weight = (second * second) * (top - close)
                high = weight.astype(BF16)
                low = (weight - high.astype(F32)).astype(BF16)
                base = k * 2 * TILE
                weights_ref[combo, tile, base : base + TILE, :] = high
                weights_ref[combo, tile, base + TILE : base + 2 * TILE, :] = low
        return carry

    lax.fori_loop(0, GX, one, 0, unroll=8 // len(targets))


def spread_ends(out_ref):
    empty = jnp.zeros((2 * ROWS, 2 * TILE), BF16)
    out_ref[:, 0 : 2 * TILE] = empty
    out_ref[:, (PAD - 1) * 2 * TILE :] = empty


def spread_tile(values, out_ref, tile):
    high = values.astype(BF16)
    low = (values - high.astype(F32)).astype(BF16)
    both = jnp.concatenate([high, low], axis=0)
    at = pl.multiple_of((tile + 1) * 2 * TILE, 2 * TILE)
    out_ref[:, pl.ds(at, 2 * TILE)] = jnp.concatenate([both, both], axis=1)


def spread(row_ref, out_ref):
    spread_ends(out_ref)
    for tile in range(GX):
        spread_tile(row_ref[:, tile * TILE : (tile + 1) * TILE], out_ref, tile)


def spread_sides(row_ref, out_ref):
    empty = jnp.zeros((ROWS, 2 * TILE), BF16)
    out_ref[:, 0 : 2 * TILE] = empty
    out_ref[:, (PAD - 1) * 2 * TILE :] = empty
    row = lax.broadcasted_iota(jnp.int32, (8, TILE), 0)
    for tile in range(GX):
        here = slice(tile * TILE, (tile + 1) * TILE)
        target = row_ref[8:9, here]
        high = target.astype(BF16).astype(F32)
        rest = jnp.where(row == 0, high, jnp.where(row == 1, target - high, 0.0))
        both = jnp.concatenate([row_ref[0:8, here], rest], axis=0).astype(BF16)
        at = (tile + 1) * 2 * TILE
        out_ref[:, at : at + 2 * TILE] = jnp.concatenate([both, both], axis=1)


def banded(spread_ref, weights_ref, combo, tile):
    at = pl.multiple_of(tile * 2 * TILE, 2 * TILE)
    return jnp.dot(
        spread_ref[:, pl.ds(at, BAND)],
        weights_ref[combo, tile],
        preferred_element_type=F32,
    )


def joined(both):
    if both.shape[0] == 2 * ROWS:
        return both[0:ROWS] + both[ROWS:]
    row = lax.broadcasted_iota(jnp.int32, both.shape, 0)
    return both + jnp.where(row == 8, pltpu.roll(both, ROWS - 1, 0), 0.0)


GROUP = 16


def apply_row(own_ref, terms, consts_ref, out_ref, out_spread_ref, beside_ref=None):
    noise = constant(consts_ref, NOISE)
    spread_ends(out_spread_ref)

    def group(g, carry):
        for j in range(GROUP):
            tile = g * GROUP + j
            here = lanes(tile)
            both = banded(*terms[0], tile)
            if beside_ref is not None:
                beside_ref[:, here] = joined(both)
            for term in terms[1:]:
                both = both + banded(*term, tile)
            total = noise * own_ref[:, here] + joined(both)
            out_ref[:, here] = total
            spread_tile(total, out_spread_ref, tile)
        return carry

    lax.fori_loop(0, GX // GROUP, group, 0)


def two_sum(a, b):
    total = a + b
    part = total - a
    return total, (a - (total - part)) + (b - part)


def quick_sum(a, b):
    total = a + b
    return total, b - (total - a)


def halves(a):
    scaled = 4097.0 * a
    high = scaled - (scaled - a)
    return high, a - high


def two_product(a, b):
    a1, a2 = halves(a)
    b1, b2 = halves(b)
    product = a * b
    return product, ((a1 * b1 - product) + a1 * b2 + a2 * b1) + a2 * b2


class Pair:
    def __init__(self, high, low):
        self.high, self.low = high, low

    def __add__(self, other):
        total, error = two_sum(self.high, other.high)
        return Pair(*quick_sum(total, error + (self.low + other.low)))

    def __neg__(self):
        return Pair(-self.high, -self.low)

    def __sub__(self, other):
        return self + (-other)

    def __mul__(self, other):
        if not isinstance(other, Pair):
            return Pair(self.high * other, self.low * other)
        product, error = two_product(self.high, other.high)
        return Pair(*quick_sum(product, error + (self.high * other.low + self.low * other.high)))

    def __truediv__(self, other):
        first = self.high / other.high
        rest = self - other * Pair(first, jnp.zeros_like(first))
        return Pair(*quick_sum(first, rest.high / other.high))

    def where(self, keep, other):
        return Pair(jnp.where(keep, self.high, other.high), jnp.where(keep, self.low, other.low))


SUMS = 9
STRIDE = TILE // SUMS


def grid_mask(k):
    lane = lax.broadcasted_iota(jnp.int32, (ROWS, TILE), 1)
    row = lax.broadcasted_iota(jnp.int32, (ROWS, TILE), 0)
    return (lane == row + STRIDE * k) & (row < RHS)


def accumulate(sums, term):
    total, left = two_sum(sums[0], term)
    return total, sums[1] + left


def lines(sums):
    row = lax.broadcasted_iota(jnp.int32, (8, TILE), 0)
    lane = lax.broadcasted_iota(jnp.int32, (8, TILE), 1)
    blocks = [[(high[0:8], low[0:8]), lane == row + STRIDE * k] for k, (high, low) in enumerate(sums)]
    for start in range(0, len(sums), 8):
        last = [jnp.zeros((8, TILE), F32), jnp.zeros((8, TILE), F32)]
        group = sums[start : start + 8]
        for k, pair in enumerate(group):
            last = [jnp.where(row == k, jnp.broadcast_to(v[8:9], (8, TILE)), t) for v, t in zip(pair, last)]
        mask = (lane == 8 + STRIDE * (start + row)) & (row < len(group))
        blocks.append([tuple(last), mask])
    placed = [jnp.zeros((8, TILE), F32), jnp.zeros((8, TILE), F32)]
    for (high, low), mask in blocks:
        for shift in (64, 32, 16, 8, 4, 2, 1):
            high, left = two_sum(high, pltpu.roll(high, shift, 1))
            low = (low + pltpu.roll(low, shift, 1)) + left
        high, low = quick_sum(high, low)
        placed = [jnp.where(mask, high, placed[0]), jnp.where(mask, low, placed[1])]
    return [jnp.sum(p, axis=0, keepdims=True) for p in placed]


def inner_kernel(
    first_ref, second_ref, consts_ref, left_ref, right_ref, spread0_ref, spread1_ref, feats_ref
):
    rows = feature_rows()
    for slot, (own_ref, weights_ref, spread_ref) in enumerate(
        ((first_ref, left_ref, spread0_ref), (second_ref, right_ref, spread1_ref))
    ):
        source_features(own_ref, constant(consts_ref, FACTOR), rows, feats_ref)
        targets = ((first_ref, slot, weights_ref, 0), (second_ref, slot - 1, weights_ref, 1))
        fill_weights(targets, feats_ref, consts_ref, rows)
        spread_sides(own_ref, spread_ref)


def outer_kernel(
    slot,
    other_ref,
    own_ref,
    consts_ref,
    left_ref,
    right_ref,
    spread0_ref,
    spread1_ref,
    weights_ref,
    out_ref,
    out_spread_ref,
    *more,
):
    beside_ref, feats_ref, spread_ref = more if slot else (None, *more)
    rows = feature_rows()
    source_features(other_ref, constant(consts_ref, FACTOR), rows, feats_ref)
    fill_weights(((own_ref, 2 * slot - 1, weights_ref, 0),), feats_ref, consts_ref, rows)
    spread_sides(other_ref, spread_ref)
    terms = ((spread_ref, weights_ref, 0), (spread0_ref, left_ref, slot), (spread1_ref, right_ref, slot))
    apply_row(own_ref, terms, consts_ref, out_ref, out_spread_ref, beside_ref)


def product_kernel(
    other_ref,
    own_ref,
    consts_ref,
    left_ref,
    right_ref,
    weights_ref,
    spread0_ref,
    spread1_ref,
    out_ref,
    out_spread_ref,
    spread_ref,
):
    spread(other_ref, spread_ref)
    terms = ((spread_ref, weights_ref, 0), (spread0_ref, left_ref, 0), (spread1_ref, right_ref, 0))
    apply_row(own_ref, terms, consts_ref, out_ref, out_spread_ref)


def gram_kernel(
    below_ref,
    b0_ref,
    b1_ref,
    f0_ref,
    f1_ref,
    g0_ref,
    b_beside_ref,
    consts_ref,
    left_ref,
    right_ref,
    under_ref,
    f0_spread_ref,
    f1_spread_ref,
    g0_spread_ref,
    g1_ref,
    sums_ref,
    spread_ref,
    g1_spread_ref,
    f_beside_ref,
):
    spread(below_ref, spread_ref)
    terms = ((spread_ref, under_ref, 0), (f0_spread_ref, left_ref, 1), (f1_spread_ref, right_ref, 1))
    apply_row(f1_ref, terms, consts_ref, g1_ref, g1_spread_ref, f_beside_ref)
    zero = jnp.zeros((ROWS, TILE), F32)
    noise = constant(consts_ref, NOISE)

    def group(g, sums):
        sums = list(sums)
        terms = [zero] * SUMS
        for j in range(8):
            tile = g * 8 + j
            here = lanes(tile)
            for half, refs in enumerate(((b0_ref, f0_ref, g0_ref), (b1_ref, f1_ref, g1_ref))):
                v = [ref[:, here] for ref in refs]
                for k, (i, m) in enumerate(((0, 0), (0, 1), (0, 2), (1, 1), (1, 2), (2, 2))):
                    terms[k] = terms[k] + v[i] * v[m]
                both = banded(g0_spread_ref, left_ref, half, tile)
                both = both + banded(g1_spread_ref, right_ref, half, tile)
                image = noise * v[2] + joined(both)
                for k in range(3):
                    terms[6 + k] = terms[6 + k] + v[k] * image
                if half == 1:
                    terms[6] = terms[6] + v[2] * b_beside_ref[:, here]
                    terms[7] = terms[7] + v[2] * f_beside_ref[:, here]
            if j % 2 == 1:
                sums = [accumulate(s, t) for s, t in zip(sums, terms)]
                terms = [zero] * SUMS
        return tuple(sums)

    sums = lax.fori_loop(0, GX // 8, group, ((zero, zero),) * SUMS)
    for k, (high, low) in enumerate(sums):
        sums_ref[k, 0] = high
        sums_ref[k, 1] = low


def moment_kernel(sums_ref, below_ref, b_ref, f_ref, g_ref, weights_ref, out_ref, spread_ref):
    spread(below_ref, spread_ref)
    zero = jnp.zeros((ROWS, TILE), F32)
    sums = [(sums_ref[k, 0], sums_ref[k, 1]) for k in range(SUMS)]
    terms = [zero] * 3
    for tile in range(GX):
        here = slice(tile * TILE, (tile + 1) * TILE)
        image = joined(banded(spread_ref, weights_ref, 0, tile))
        factors = (b_ref[:, here], f_ref[:, here], 2.0 * g_ref[:, here])
        terms = [t + v * image for t, v in zip(terms, factors)]
        if tile % 4 == 3:
            sums[6:] = [accumulate(s, t) for s, t in zip(sums[6:], terms)]
            terms = [zero] * 3
    both = jnp.concatenate(lines(sums), axis=1)
    out_ref[...] = jnp.broadcast_to(both[None], out_ref.shape)


def finish_kernel(
    points,
    cell_hbm,
    consts_ref,
    parts_ref,
    b0_ref,
    b1_ref,
    f0_ref,
    f1_ref,
    g0_ref,
    g1_ref,
    out_ref,
    quad_ref,
    cell_ref,
    grid_ref,
    sem,
):
    copy = pltpu.make_async_copy(cell_hbm, cell_ref, sem)
    copy.start()
    high, low = parts_ref[:, 0, 0:TILE], parts_ref[:, 0, TILE:]
    while high.shape[0] > 8:
        half = high.shape[0] // 2
        high, left = two_sum(high[:half], high[half:])
        low = (low[:half] + low[half:]) + left
    for shift in (4, 2, 1):
        high, left = two_sum(high, pltpu.roll(high, shift, 0))
        low = (low + pltpu.roll(low, shift, 0)) + left
    high, low = quick_sum(high, low)
    bb, bf, bg, ff, fg, gg, bag, fag, gag = (
        Pair(high, low)
        if k == 0
        else Pair(pltpu.roll(high, TILE - STRIDE * k, 1), pltpu.roll(low, TILE - STRIDE * k, 1))
        for k in range(SUMS)
    )
    zero = jnp.zeros_like(high)
    none = Pair(zero, zero)
    one = Pair(zero + 1.0, zero)
    most = jnp.broadcast_to(1.0 / constant(consts_ref, NOISE), high.shape)

    floor = bb.high * 1e-11

    def step(square, product):
        good = (square.high > floor) & (product.high > 0.0)
        ratio = square / product.where(good, one)
        fits = ratio.high < most
        return ratio.where(fits, Pair(most, zero)).where(good, none), good

    def over(a, b, good):
        return (a / b.where(good, one)).where(good, none)

    alpha0, good0 = step(bb, bf)
    rr1 = bb - alpha0 * (bf * 2.0 - alpha0 * ff)
    beta0 = over(rr1, bb, good0)
    p0, p1 = one + beta0, -alpha0
    alpha1, good1 = step(rr1, p0 * (p0 * bf + p1 * (bg + ff)) + p1 * p1 * fg)
    r1, r2 = -(alpha0 + alpha1 * p0), -(alpha1 * p1)
    rr2 = bb + r1 * (bf * 2.0 + r1 * ff) + r2 * (bg * 2.0 + r1 * fg * 2.0 + r2 * gg)
    beta1 = over(rr2, rr1, good1)
    q0, q1, q2 = one + beta1 * p0, r1 + beta1 * p1, r2
    alpha2, good2 = step(
        rr2,
        q0 * (q0 * bf + q1 * (bg + ff) + q2 * (fg + bag)) + q1 * (q1 * fg + q2 * (gg + fag)) + q2 * q2 * gag,
    )
    alpha2 = alpha2.where(good1, none)
    on_b = alpha0 + alpha1 * p0 + alpha2 * q0
    on_f = alpha1 * p1 + alpha2 * q1
    on_g = alpha2 * q2
    quad = on_b * bb + on_f * bf + on_g * bg
    quad_ref[...] = (quad.high / points)[0:1, 0:RHS]
    mask = grid_mask(0)
    c0, c1, c2 = (
        jnp.broadcast_to(
            jnp.sum(
                jnp.where(mask, jnp.concatenate([c.high, c.high], axis=0), 0.0), axis=1, keepdims=True
            ),
            (ROWS, TILE),
        )
        for c in (on_b, on_f, on_g)
    )
    for half, (b_ref, f_ref, g_ref) in enumerate(
        ((b0_ref, f0_ref, g0_ref), (b1_ref, f1_ref, g1_ref))
    ):
        for tile in range(GX):
            here = slice(tile * TILE, (tile + 1) * TILE)
            grid_ref[half * GX + tile] = (
                c0 * b_ref[:, here] + c1 * f_ref[:, here] + c2 * g_ref[:, here]
            )
    copy.wait()
    for s in range(cell_ref.shape[0]):
        out_ref[:, s * TILE : (s + 1) * TILE] = grid_ref[cell_ref[s], 0:RHS, :]


def shards(offsets, tile_cell, probes, target, lengthscale, amplitude, noise):
    size = lax.axis_size("rows")
    points = size * tile_cell.shape[0] * TILE
    down = [(i, i + 1) for i in range(size - 1)]
    up = [(i + 1, i) for i in range(size - 1)]

    tiles = tile_cell.shape[0]
    first, second, consts = call(
        pack_kernel,
        "pack",
        (pltpu.VMEM((ROWS, WIDE), F32), pltpu.VMEM((ROWS, WIDE), F32), pltpu.VMEM((8, TILE), F32)),
        [HBM] * 4 + [SMEM] * 3,
        [
            pltpu.SMEM((tiles,), jnp.int32),
            pltpu.SMEM((tiles,), jnp.int32),
            pltpu.VMEM((2, tiles * TILE), F32),
            pltpu.VMEM((8, tiles * TILE), jnp.int32),
            pltpu.VMEM((1, tiles * TILE), F32),
            pltpu.SemaphoreType.DMA((4,)),
        ],
        flops=1 << 20,
        limit=60.5,
    )(
        tile_cell,
        offsets,
        probes,
        target.reshape(1, -1),
        lengthscale,
        amplitude,
        noise,
    )

    def outer(slot, other, own):
        return call(
            lambda *refs: outer_kernel(slot, *refs),
            f"outer{slot}",
            (weight_rows(1), grid_row(), spread_row()) + (grid_row(),) * slot,
            [VMEM] * 7,
            [feature_tiles(), spread_row(ROWS)],
            flops=1 << 30,
        )(other, own, consts, left, right, b0_spread, b1_spread)

    above = lax.ppermute(second, "rows", down)
    below = lax.ppermute(first, "rows", up)
    left, right, b0_spread, b1_spread = call(
        inner_kernel,
        "inner",
        (weight_rows(2), weight_rows(2), spread_row(ROWS), spread_row(ROWS)),
        [VMEM] * 3,
        [feature_tiles()],
        flops=1 << 30,
    )(first, second, consts)
    under, f1, f1_spread, b_beside = outer(1, below, second)
    over, f0, f0_spread = outer(0, above, first)
    sent, f0 = lax.optimization_barrier((f1, f0))
    f_above = lax.ppermute(sent, "rows", down)
    f_below = lax.ppermute(f0, "rows", up)
    g0, g0_spread = call(
        product_kernel,
        "product",
        (grid_row(), spread_row()),
        [VMEM] * 8,
        [spread_row()],
        flops=1 << 29,
    )(f_above, f0, consts, left, right, over, f0_spread, f1_spread)
    g_below = lax.ppermute(g0, "rows", up)
    g1, sums = call(
        gram_kernel,
        "gram",
        (grid_row(), jax.ShapeDtypeStruct((SUMS, 2, ROWS, TILE), F32)),
        [VMEM] * 14,
        [spread_row(), spread_row(), pltpu.VMEM((ROWS, WIDE), F32)],
        flops=1 << 29,
    )(f_below, first, second, f0, f1, g0, b_beside, consts, left, right, under, f0_spread, f1_spread, g0_spread)
    parts = call(
        moment_kernel,
        "moment",
        jax.ShapeDtypeStruct((size, 1, 2 * TILE), F32),
        [VMEM] * 6,
        [spread_row()],
        flops=1 << 29,
    )(sums, g_below, second, f1, g1, under)
    parts = lax.all_to_all(parts, "rows", split_axis=0, concat_axis=0, tiled=True)

    solutions, quad = call(
        lambda *refs: finish_kernel(float(points), *refs),
        "finish",
        (
            jax.ShapeDtypeStruct((RHS, tiles * TILE), F32),
            jax.ShapeDtypeStruct((1, RHS), F32),
        ),
        [HBM] + [VMEM] * 8,
        [
            pltpu.SMEM((tiles,), jnp.int32),
            pltpu.VMEM((tiles, ROWS, TILE), F32),
            pltpu.SemaphoreType.DMA,
        ],
        flops=1 << 20,
    )(tile_cell, consts, parts, first, second, f0, f1, g0, g1)
    return (solutions, quad.reshape(RHS))


def solution(mesh):
    return jax.shard_map(
        shards,
        mesh=mesh,
        in_specs=(
            P(None, "rows"),
            P("rows"),
            P(None, "rows"),
            P("rows"),
            P("hyp"),
            P("hyp"),
            P("hyp"),
        ),
        out_specs=(P("hyp", "rows"), P("hyp")),
        check_vma=False,
    )
```

```python
import jax
import jax.numpy as jnp
from jax import lax
from jax.experimental import pallas as pl
from jax.experimental.pallas import tpu as pltpu
from jax.sharding import PartitionSpec as P

TILE = 128
GX = 16
RHS = 9
ROWS = 16
WIDE = GX * TILE
FEATURES = 32
PAD = GX + 2
BAND = 3 * 2 * TILE
F32 = jnp.float32
BF16 = jnp.bfloat16
TINY = 1e-30

VMEM = pl.BlockSpec(memory_space=pltpu.VMEM)
HBM = pl.BlockSpec(memory_space=pltpu.HBM)
SMEM = pl.BlockSpec(memory_space=pltpu.SMEM)
REACH, TOP, FACTOR, NOISE = range(4)


def call(kernel, name, out_shape, in_specs, scratch=(), flops=0, limit=12):
    return pl.pallas_call(
        kernel,
        name=name,
        out_shape=out_shape,
        in_specs=in_specs,
        out_specs=jax.tree.map(lambda _: VMEM, out_shape),
        scratch_shapes=list(scratch),
        cost_estimate=pl.CostEstimate(flops=flops, bytes_accessed=1 << 20, transcendentals=0),
        compiler_params=pltpu.CompilerParams(vmem_limit_bytes=int(limit * 2**20)),
    )


def grid_row():
    return jax.ShapeDtypeStruct((ROWS, WIDE), F32)


def spread_row(rows=2 * ROWS):
    return pltpu.VMEM((rows, PAD * 2 * TILE), BF16)


def weight_rows(count):
    return pltpu.VMEM((count, GX, BAND, TILE), BF16)


def feature_tiles():
    return pltpu.VMEM((PAD, TILE, FEATURES), BF16)


def lanes(tile, width=TILE):
    return pl.ds(pl.multiple_of(tile * width, width), width)


def pack_kernel(
    cell_hbm,
    offsets_hbm,
    probes_hbm,
    target_hbm,
    scale_ref,
    amp_ref,
    noise_ref,
    first_ref,
    second_ref,
    consts_ref,
    cell_ref,
    from_ref,
    offsets_ref,
    probes_ref,
    target_ref,
    sems,
):
    copies = [
        pltpu.make_async_copy(source, dest, sems.at[i])
        for i, (source, dest) in enumerate(
            (
                (cell_hbm, cell_ref),
                (offsets_hbm, offsets_ref),
                (probes_hbm, probes_ref),
                (target_hbm, target_ref),
            )
        )
    ]
    for copy in copies:
        copy.start()
    for copy in copies:
        copy.wait()
    for s in range(cell_ref.shape[0]):
        from_ref[cell_ref[s]] = s
    filler = jnp.zeros((ROWS - RHS - 2, TILE), F32)
    for cell in range(cell_ref.shape[0]):
        stored = lanes(from_ref[cell])
        here = slice(cell % GX * TILE, (cell % GX + 1) * TILE)
        ref = (first_ref, second_ref)[cell // GX]
        ref[0:8, here] = 2.0 * probes_ref[:, stored].astype(F32) - 1.0
        ref[8:16, here] = jnp.concatenate(
            [target_ref[:, stored], offsets_ref[:, stored], filler], axis=0
        )
    amp = jnp.full((1, TILE), amp_ref[0], F32)
    reach = jnp.exp(0.2 * jnp.log(4.0 * amp))
    square = reach * reach
    consts_ref[REACH : REACH + 1, :] = reach
    consts_ref[TOP : TOP + 1, :] = 5.0 * amp / (square * square)
    consts_ref[FACTOR : FACTOR + 1, :] = reach / jnp.full((1, TILE), scale_ref[0], F32)
    consts_ref[NOISE : NOISE + 1, :] = jnp.full((1, TILE), noise_ref[0], F32)


def constant(consts_ref, which):
    return consts_ref[which : which + 1, :]


def split_rows(values, level):
    first = values.astype(BF16).astype(F32)
    rest = values - first
    second = rest.astype(BF16).astype(F32)
    third = rest - second
    return jnp.where(level == 0, first, jnp.where(level == 1, second, third))


def feature_rows():
    row = lax.broadcasted_iota(jnp.int32, (FEATURES, TILE), 0)

    def level(order):
        out = jnp.zeros_like(row)
        for k, v in enumerate(order):
            if v:
                out = jnp.where(row == k, v, out)
        return out

    source = level([0, 0, 1, 1, 0, 2] * 2 + [0, 1, 2] + [0, 0, 0])
    target = level([0, 1, 0, 1, 2, 0] * 2 + [0, 0, 0] + [0, 1, 2])
    kind = jnp.where(row < 6, 0, jnp.where(row < 12, 1, jnp.where(row < 15, 2, jnp.where(row < 18, 3, 4))))
    return kind, source, target


def choose(kind, a, b, c, d):
    return jnp.where(
        kind == 0, a, jnp.where(kind == 1, b, jnp.where(kind == 2, c, jnp.where(kind == 3, d, 0.0)))
    )


def source_features(row_ref, factor, rows, out_ref):
    kind, source, _ = rows
    zero = jnp.zeros((TILE, FEATURES), BF16)
    out_ref[0] = zero
    out_ref[PAD - 1] = zero

    def one(tile, carry):
        a = factor * (row_ref[9:10, lanes(tile)] - 0.5)
        b = factor * (row_ref[10:11, lanes(tile)] - 0.5)
        values = choose(kind, a, b, a * a + b * b, 1.0)
        out_ref[tile + 1] = split_rows(values, source).T.astype(BF16)
        return carry

    lax.fori_loop(0, GX, one, 0, unroll=8)


def target_features(row_ref, tile, row_shift, col_shift, factor, rows):
    kind, _, target = rows
    a = factor * ((row_shift + 0.5) - row_ref[9:10, lanes(tile)])
    b = factor * ((col_shift + 0.5) - row_ref[10:11, lanes(tile)])
    values = choose(kind, 2.0 * a, 2.0 * b, 1.0, a * a + b * b)
    return split_rows(values, target).astype(BF16)


def fill_weights(targets, feats_ref, consts_ref, rows):
    factor = constant(consts_ref, FACTOR)
    reach = jnp.broadcast_to(constant(consts_ref, REACH), (TILE, TILE))
    top = jnp.broadcast_to(constant(consts_ref, TOP), (TILE, TILE))

    def one(tile, carry):
        for k in range(3):
            wanted = [
                target_features(ref, tile, float(row_shift), float(k - 1), factor, rows)
                for ref, row_shift, _, _ in targets
            ]
            squares = lax.dot_general(
                feats_ref[tile + k],
                wanted[0] if len(wanted) == 1 else jnp.concatenate(wanted, axis=1),
                (((1,), (0,)), ((), ())),
                preferred_element_type=F32,
            )
            for i, (_, _, weights_ref, combo) in enumerate(targets):
                here = jnp.maximum(squares[:, i * TILE : (i + 1) * TILE], 1e-12)
                close = jnp.maximum(reach - here * lax.rsqrt(here), 0.0)
                second = close * close
                weight = (second * second) * (top - close)
                high = weight.astype(BF16)
                low = (weight - high.astype(F32)).astype(BF16)
                base = k * 2 * TILE
                weights_ref[combo, tile, base : base + TILE, :] = high
                weights_ref[combo, tile, base + TILE : base + 2 * TILE, :] = low
        return carry

    lax.fori_loop(0, GX, one, 0, unroll=8 // len(targets))


def spread_ends(out_ref):
    empty = jnp.zeros((2 * ROWS, 2 * TILE), BF16)
    out_ref[:, 0 : 2 * TILE] = empty
    out_ref[:, (PAD - 1) * 2 * TILE :] = empty


def spread_tile(values, out_ref, tile):
    high = values.astype(BF16)
    low = (values - high.astype(F32)).astype(BF16)
    both = jnp.concatenate([high, low], axis=0)
    at = pl.multiple_of((tile + 1) * 2 * TILE, 2 * TILE)
    out_ref[:, pl.ds(at, 2 * TILE)] = jnp.concatenate([both, both], axis=1)


def spread(row_ref, out_ref):
    spread_ends(out_ref)
    for tile in range(GX):
        spread_tile(row_ref[:, tile * TILE : (tile + 1) * TILE], out_ref, tile)


def spread_sides(row_ref, out_ref):
    empty = jnp.zeros((ROWS, 2 * TILE), BF16)
    out_ref[:, 0 : 2 * TILE] = empty
    out_ref[:, (PAD - 1) * 2 * TILE :] = empty
    row = lax.broadcasted_iota(jnp.int32, (8, TILE), 0)
    for tile in range(GX):
        here = slice(tile * TILE, (tile + 1) * TILE)
        target = row_ref[8:9, here]
        high = target.astype(BF16).astype(F32)
        rest = jnp.where(row == 0, high, jnp.where(row == 1, target - high, 0.0))
        both = jnp.concatenate([row_ref[0:8, here], rest], axis=0).astype(BF16)
        at = (tile + 1) * 2 * TILE
        out_ref[:, at : at + 2 * TILE] = jnp.concatenate([both, both], axis=1)


def banded(spread_ref, weights_ref, combo, tile):
    at = pl.multiple_of(tile * 2 * TILE, 2 * TILE)
    return jnp.dot(
        spread_ref[:, pl.ds(at, BAND)],
        weights_ref[combo, tile],
        preferred_element_type=F32,
    )


def joined(both):
    if both.shape[0] == 2 * ROWS:
        return both[0:ROWS] + both[ROWS:]
    row = lax.broadcasted_iota(jnp.int32, both.shape, 0)
    return both + jnp.where(row == 8, pltpu.roll(both, ROWS - 1, 0), 0.0)


GROUP = 16


def apply_row(own_ref, terms, consts_ref, out_ref, out_spread_ref, beside_ref=None):
    noise = constant(consts_ref, NOISE)
    spread_ends(out_spread_ref)

    def group(g, carry):
        for j in range(GROUP):
            tile = g * GROUP + j
            here = lanes(tile)
            both = banded(*terms[0], tile)
            if beside_ref is not None:
                beside_ref[:, here] = joined(both)
            for term in terms[1:]:
                both = both + banded(*term, tile)
            total = noise * own_ref[:, here] + joined(both)
            out_ref[:, here] = total
            spread_tile(total, out_spread_ref, tile)
        return carry

    lax.fori_loop(0, GX // GROUP, group, 0)


def two_sum(a, b):
    total = a + b
    part = total - a
    return total, (a - (total - part)) + (b - part)


def quick_sum(a, b):
    total = a + b
    return total, b - (total - a)


def halves(a):
    scaled = 4097.0 * a
    high = scaled - (scaled - a)
    return high, a - high


def two_product(a, b):
    a1, a2 = halves(a)
    b1, b2 = halves(b)
    product = a * b
    return product, ((a1 * b1 - product) + a1 * b2 + a2 * b1) + a2 * b2


class Pair:
    def __init__(self, high, low):
        self.high, self.low = high, low

    def __add__(self, other):
        total, error = two_sum(self.high, other.high)
        return Pair(*quick_sum(total, error + (self.low + other.low)))

    def __neg__(self):
        return Pair(-self.high, -self.low)

    def __sub__(self, other):
        return self + (-other)

    def __mul__(self, other):
        if not isinstance(other, Pair):
            return Pair(self.high * other, self.low * other)
        product, error = two_product(self.high, other.high)
        return Pair(*quick_sum(product, error + (self.high * other.low + self.low * other.high)))

    def __truediv__(self, other):
        first = self.high / other.high
        rest = self - other * Pair(first, jnp.zeros_like(first))
        return Pair(*quick_sum(first, rest.high / other.high))

    def where(self, keep, other):
        return Pair(jnp.where(keep, self.high, other.high), jnp.where(keep, self.low, other.low))


SUMS = 9
STRIDE = TILE // SUMS


def grid_mask(k):
    lane = lax.broadcasted_iota(jnp.int32, (ROWS, TILE), 1)
    row = lax.broadcasted_iota(jnp.int32, (ROWS, TILE), 0)
    return (lane == row + STRIDE * k) & (row < RHS)


def accumulate(sums, term):
    total, left = two_sum(sums[0], term)
    return total, sums[1] + left


def lines(sums):
    row = lax.broadcasted_iota(jnp.int32, (8, TILE), 0)
    lane = lax.broadcasted_iota(jnp.int32, (8, TILE), 1)
    blocks = [[(high[0:8], low[0:8]), lane == row + STRIDE * k] for k, (high, low) in enumerate(sums)]
    for start in range(0, len(sums), 8):
        last = [jnp.zeros((8, TILE), F32), jnp.zeros((8, TILE), F32)]
        group = sums[start : start + 8]
        for k, pair in enumerate(group):
            last = [jnp.where(row == k, jnp.broadcast_to(v[8:9], (8, TILE)), t) for v, t in zip(pair, last)]
        mask = (lane == 8 + STRIDE * (start + row)) & (row < len(group))
        blocks.append([tuple(last), mask])
    placed = [jnp.zeros((8, TILE), F32), jnp.zeros((8, TILE), F32)]
    for (high, low), mask in blocks:
        for shift in (64, 32, 16, 8, 4, 2, 1):
            high, left = two_sum(high, pltpu.roll(high, shift, 1))
            low = (low + pltpu.roll(low, shift, 1)) + left
        high, low = quick_sum(high, low)
        placed = [jnp.where(mask, high, placed[0]), jnp.where(mask, low, placed[1])]
    return [jnp.sum(p, axis=0, keepdims=True) for p in placed]


def inner_kernel(
    first_ref, second_ref, consts_ref, left_ref, right_ref, spread0_ref, spread1_ref, feats_ref
):
    rows = feature_rows()
    for slot, (own_ref, weights_ref, spread_ref) in enumerate(
        ((first_ref, left_ref, spread0_ref), (second_ref, right_ref, spread1_ref))
    ):
        source_features(own_ref, constant(consts_ref, FACTOR), rows, feats_ref)
        targets = ((first_ref, slot, weights_ref, 0), (second_ref, slot - 1, weights_ref, 1))
        fill_weights(targets, feats_ref, consts_ref, rows)
        spread_sides(own_ref, spread_ref)


def outer_kernel(
    slot,
    other_ref,
    own_ref,
    consts_ref,
    left_ref,
    right_ref,
    spread0_ref,
    spread1_ref,
    weights_ref,
    out_ref,
    out_spread_ref,
    *more,
):
    beside_ref, feats_ref, spread_ref = more if slot else (None, *more)
    rows = feature_rows()
    source_features(other_ref, constant(consts_ref, FACTOR), rows, feats_ref)
    fill_weights(((own_ref, 2 * slot - 1, weights_ref, 0),), feats_ref, consts_ref, rows)
    spread_sides(other_ref, spread_ref)
    terms = ((spread_ref, weights_ref, 0), (spread0_ref, left_ref, slot), (spread1_ref, right_ref, slot))
    apply_row(own_ref, terms, consts_ref, out_ref, out_spread_ref, beside_ref)


def product_kernel(
    other_ref,
    own_ref,
    consts_ref,
    left_ref,
    right_ref,
    weights_ref,
    spread0_ref,
    spread1_ref,
    out_ref,
    out_spread_ref,
    spread_ref,
):
    spread(other_ref, spread_ref)
    terms = ((spread_ref, weights_ref, 0), (spread0_ref, left_ref, 0), (spread1_ref, right_ref, 0))
    apply_row(own_ref, terms, consts_ref, out_ref, out_spread_ref)


def gram_kernel(
    below_ref,
    b0_ref,
    b1_ref,
    f0_ref,
    f1_ref,
    g0_ref,
    b_beside_ref,
    consts_ref,
    left_ref,
    right_ref,
    under_ref,
    f0_spread_ref,
    f1_spread_ref,
    g0_spread_ref,
    g1_ref,
    sums_ref,
    spread_ref,
    g1_spread_ref,
    f_beside_ref,
):
    spread(below_ref, spread_ref)
    terms = ((spread_ref, under_ref, 0), (f0_spread_ref, left_ref, 1), (f1_spread_ref, right_ref, 1))
    apply_row(f1_ref, terms, consts_ref, g1_ref, g1_spread_ref, f_beside_ref)
    zero = jnp.zeros((ROWS, TILE), F32)
    noise = constant(consts_ref, NOISE)

    def group(g, sums):
        sums = list(sums)
        terms = [zero] * SUMS
        for j in range(8):
            tile = g * 8 + j
            here = lanes(tile)
            for half, refs in enumerate(((b0_ref, f0_ref, g0_ref), (b1_ref, f1_ref, g1_ref))):
                v = [ref[:, here] for ref in refs]
                for k, (i, m) in enumerate(((0, 0), (0, 1), (0, 2), (1, 1), (1, 2), (2, 2))):
                    terms[k] = terms[k] + v[i] * v[m]
                both = banded(g0_spread_ref, left_ref, half, tile)
                both = both + banded(g1_spread_ref, right_ref, half, tile)
                image = noise * v[2] + joined(both)
                for k in range(3):
                    terms[6 + k] = terms[6 + k] + v[k] * image
                if half == 1:
                    terms[6] = terms[6] + v[2] * b_beside_ref[:, here]
                    terms[7] = terms[7] + v[2] * f_beside_ref[:, here]
            if j % 2 == 1:
                sums = [accumulate(s, t) for s, t in zip(sums, terms)]
                terms = [zero] * SUMS
        return tuple(sums)

    sums = lax.fori_loop(0, GX // 8, group, ((zero, zero),) * SUMS)
    for k, (high, low) in enumerate(sums):
        sums_ref[k, 0] = high
        sums_ref[k, 1] = low


def moment_kernel(sums_ref, below_ref, b_ref, f_ref, g_ref, weights_ref, out_ref, spread_ref):
    spread(below_ref, spread_ref)
    zero = jnp.zeros((ROWS, TILE), F32)
    sums = [(sums_ref[k, 0], sums_ref[k, 1]) for k in range(SUMS)]
    terms = [zero] * 3
    for tile in range(GX):
        here = slice(tile * TILE, (tile + 1) * TILE)
        image = joined(banded(spread_ref, weights_ref, 0, tile))
        factors = (b_ref[:, here], f_ref[:, here], 2.0 * g_ref[:, here])
        terms = [t + v * image for t, v in zip(terms, factors)]
        if tile % 4 == 3:
            sums[6:] = [accumulate(s, t) for s, t in zip(sums[6:], terms)]
            terms = [zero] * 3
    both = jnp.concatenate(lines(sums), axis=1)
    out_ref[...] = jnp.broadcast_to(both[None], out_ref.shape)


def finish_kernel(
    points,
    cell_hbm,
    consts_ref,
    parts_ref,
    b0_ref,
    b1_ref,
    f0_ref,
    f1_ref,
    g0_ref,
    g1_ref,
    out_ref,
    quad_ref,
    cell_ref,
    grid_ref,
    sem,
):
    copy = pltpu.make_async_copy(cell_hbm, cell_ref, sem)
    copy.start()
    high, low = parts_ref[:, 0, 0:TILE], parts_ref[:, 0, TILE:]
    while high.shape[0] > 8:
        half = high.shape[0] // 2
        high, left = two_sum(high[:half], high[half:])
        low = (low[:half] + low[half:]) + left
    for shift in (4, 2, 1):
        high, left = two_sum(high, pltpu.roll(high, shift, 0))
        low = (low + pltpu.roll(low, shift, 0)) + left
    high, low = quick_sum(high, low)
    bb, bf, bg, ff, fg, gg, bag, fag, gag = (
        Pair(high, low)
        if k == 0
        else Pair(pltpu.roll(high, TILE - STRIDE * k, 1), pltpu.roll(low, TILE - STRIDE * k, 1))
        for k in range(SUMS)
    )
    zero = jnp.zeros_like(high)
    none = Pair(zero, zero)
    one = Pair(zero + 1.0, zero)
    most = jnp.broadcast_to(1.0 / constant(consts_ref, NOISE), high.shape)

    floor = bb.high * 1e-11

    def step(square, product):
        good = (square.high > floor) & (product.high > 0.0)
        ratio = square / product.where(good, one)
        fits = ratio.high < most
        return ratio.where(fits, Pair(most, zero)).where(good, none), good

    def over(a, b, good):
        return (a / b.where(good, one)).where(good, none)

    alpha0, good0 = step(bb, bf)
    rr1 = bb - alpha0 * (bf * 2.0 - alpha0 * ff)
    beta0 = over(rr1, bb, good0)
    p0, p1 = one + beta0, -alpha0
    alpha1, good1 = step(rr1, p0 * (p0 * bf + p1 * (bg + ff)) + p1 * p1 * fg)
    r1, r2 = -(alpha0 + alpha1 * p0), -(alpha1 * p1)
    rr2 = bb + r1 * (bf * 2.0 + r1 * ff) + r2 * (bg * 2.0 + r1 * fg * 2.0 + r2 * gg)
    beta1 = over(rr2, rr1, good1)
    q0, q1, q2 = one + beta1 * p0, r1 + beta1 * p1, r2
    alpha2, good2 = step(
        rr2,
        q0 * (q0 * bf + q1 * (bg + ff) + q2 * (fg + bag)) + q1 * (q1 * fg + q2 * (gg + fag)) + q2 * q2 * gag,
    )
    alpha2 = alpha2.where(good1, none)
    on_b = alpha0 + alpha1 * p0 + alpha2 * q0
    on_f = alpha1 * p1 + alpha2 * q1
    on_g = alpha2 * q2
    quad = on_b * bb + on_f * bf + on_g * bg
    quad_ref[...] = (quad.high / points)[0:1, 0:RHS]
    mask = grid_mask(0)
    c0, c1, c2 = (
        jnp.broadcast_to(
            jnp.sum(
                jnp.where(mask, jnp.concatenate([c.high, c.high], axis=0), 0.0), axis=1, keepdims=True
            ),
            (ROWS, TILE),
        )
        for c in (on_b, on_f, on_g)
    )
    for half, (b_ref, f_ref, g_ref) in enumerate(
        ((b0_ref, f0_ref, g0_ref), (b1_ref, f1_ref, g1_ref))
    ):
        for tile in range(GX):
            here = slice(tile * TILE, (tile + 1) * TILE)
            grid_ref[half * GX + tile] = (
                c0 * b_ref[:, here] + c1 * f_ref[:, here] + c2 * g_ref[:, here]
            )
    copy.wait()
    for s in range(cell_ref.shape[0]):
        out_ref[:, s * TILE : (s + 1) * TILE] = grid_ref[cell_ref[s], 0:RHS, :]


def shards(offsets, tile_cell, probes, target, lengthscale, amplitude, noise):
    size = lax.axis_size("rows")
    points = size * tile_cell.shape[0] * TILE
    down = [(i, i + 1) for i in range(size - 1)]
    up = [(i + 1, i) for i in range(size - 1)]

    tiles = tile_cell.shape[0]
    first, second, consts = call(
        pack_kernel,
        "pack",
        (pltpu.VMEM((ROWS, WIDE), F32), pltpu.VMEM((ROWS, WIDE), F32), pltpu.VMEM((8, TILE), F32)),
        [HBM] * 4 + [SMEM] * 3,
        [
            pltpu.SMEM((tiles,), jnp.int32),
            pltpu.SMEM((tiles,), jnp.int32),
            pltpu.VMEM((2, tiles * TILE), F32),
            pltpu.VMEM((8, tiles * TILE), jnp.int32),
            pltpu.VMEM((1, tiles * TILE), F32),
            pltpu.SemaphoreType.DMA((4,)),
        ],
        flops=1 << 20,
        limit=60.5,
    )(
        tile_cell,
        offsets,
        probes,
        target.reshape(1, -1),
        lengthscale,
        amplitude,
        noise,
    )

    def outer(slot, other, own):
        return call(
            lambda *refs: outer_kernel(slot, *refs),
            f"outer{slot}",
            (weight_rows(1), grid_row(), spread_row()) + (grid_row(),) * slot,
            [VMEM] * 7,
            [feature_tiles(), spread_row(ROWS)],
            flops=1 << 30,
        )(other, own, consts, left, right, b0_spread, b1_spread)

    above = lax.ppermute(second, "rows", down)
    below = lax.ppermute(first, "rows", up)
    left, right, b0_spread, b1_spread = call(
        inner_kernel,
        "inner",
        (weight_rows(2), weight_rows(2), spread_row(ROWS), spread_row(ROWS)),
        [VMEM] * 3,
        [feature_tiles()],
        flops=1 << 30,
    )(first, second, consts)
    over, f0, f0_spread = outer(0, above, first)
    f_below = lax.ppermute(f0, "rows", up)
    under, f1, f1_spread, b_beside = outer(1, below, second)
    f_above = lax.ppermute(f1, "rows", down)
    g0, g0_spread = call(
        product_kernel,
        "product",
        (grid_row(), spread_row()),
        [VMEM] * 8,
        [spread_row()],
        flops=1 << 29,
    )(f_above, f0, consts, left, right, over, f0_spread, f1_spread)
    g_below = lax.ppermute(g0, "rows", up)
    g1, sums = call(
        gram_kernel,
        "gram",
        (grid_row(), jax.ShapeDtypeStruct((SUMS, 2, ROWS, TILE), F32)),
        [VMEM] * 14,
        [spread_row(), spread_row(), pltpu.VMEM((ROWS, WIDE), F32)],
        flops=1 << 29,
    )(f_below, first, second, f0, f1, g0, b_beside, consts, left, right, under, f0_spread, f1_spread, g0_spread)
    parts = call(
        moment_kernel,
        "moment",
        jax.ShapeDtypeStruct((size, 1, 2 * TILE), F32),
        [VMEM] * 6,
        [spread_row()],
        flops=1 << 29,
    )(sums, g_below, second, f1, g1, under)
    parts = lax.all_to_all(parts, "rows", split_axis=0, concat_axis=0, tiled=True)

    solutions, quad = call(
        lambda *refs: finish_kernel(float(points), *refs),
        "finish",
        (
            jax.ShapeDtypeStruct((RHS, tiles * TILE), F32),
            jax.ShapeDtypeStruct((1, RHS), F32),
        ),
        [HBM] + [VMEM] * 8,
        [
            pltpu.SMEM((tiles,), jnp.int32),
            pltpu.VMEM((tiles, ROWS, TILE), F32),
            pltpu.SemaphoreType.DMA,
        ],
        flops=1 << 20,
    )(tile_cell, consts, parts, first, second, f0, f1, g0, g1)
    return (solutions, quad.reshape(RHS))


def solution(mesh):
    return jax.shard_map(
        shards,
        mesh=mesh,
        in_specs=(
            P(None, "rows"),
            P("rows"),
            P(None, "rows"),
            P("rows"),
            P("hyp"),
            P("hyp"),
            P("hyp"),
        ),
        out_specs=(P("hyp", "rows"), P("hyp")),
        check_vma=False,
    )
```

```python
import jax
import jax.numpy as jnp
from jax import lax
from jax.experimental import pallas as pl
from jax.experimental.pallas import tpu as pltpu
from jax.sharding import PartitionSpec as P

TILE = 128
GX = 16
RHS = 9
ROWS = 16
WIDE = GX * TILE
FEATURES = 32
PAD = GX + 2
BAND = 3 * 2 * TILE
F32 = jnp.float32
BF16 = jnp.bfloat16
TINY = 1e-30

VMEM = pl.BlockSpec(memory_space=pltpu.VMEM)
HBM = pl.BlockSpec(memory_space=pltpu.HBM)
SMEM = pl.BlockSpec(memory_space=pltpu.SMEM)
REACH, TOP, FACTOR, NOISE = range(4)


def call(kernel, name, out_shape, in_specs, scratch=(), flops=0, limit=12):
    return pl.pallas_call(
        kernel,
        name=name,
        out_shape=out_shape,
        in_specs=in_specs,
        out_specs=jax.tree.map(lambda _: VMEM, out_shape),
        scratch_shapes=list(scratch),
        cost_estimate=pl.CostEstimate(flops=flops, bytes_accessed=1 << 20, transcendentals=0),
        compiler_params=pltpu.CompilerParams(vmem_limit_bytes=int(limit * 2**20)),
    )


def grid_row():
    return jax.ShapeDtypeStruct((ROWS, WIDE), F32)


def spread_row(rows=2 * ROWS):
    return pltpu.VMEM((rows, PAD * 2 * TILE), BF16)


def weight_rows(count):
    return pltpu.VMEM((count, GX, BAND, TILE), BF16)


def feature_tiles():
    return pltpu.VMEM((PAD, TILE, FEATURES), BF16)


def lanes(tile, width=TILE):
    return pl.ds(pl.multiple_of(tile * width, width), width)


def pack_kernel(
    cell_hbm,
    offsets_hbm,
    probes_hbm,
    target_hbm,
    scale_ref,
    amp_ref,
    noise_ref,
    first_ref,
    second_ref,
    consts_ref,
    cell_ref,
    from_ref,
    offsets_ref,
    probes_ref,
    target_ref,
    sems,
):
    copies = [
        pltpu.make_async_copy(source, dest, sems.at[i])
        for i, (source, dest) in enumerate(
            (
                (cell_hbm, cell_ref),
                (offsets_hbm, offsets_ref),
                (probes_hbm, probes_ref),
                (target_hbm, target_ref),
            )
        )
    ]
    for copy in copies:
        copy.start()
    for copy in copies:
        copy.wait()
    for s in range(cell_ref.shape[0]):
        from_ref[cell_ref[s]] = s
    filler = jnp.zeros((ROWS - RHS - 2, TILE), F32)
    for cell in range(cell_ref.shape[0]):
        stored = lanes(from_ref[cell])
        here = slice(cell % GX * TILE, (cell % GX + 1) * TILE)
        ref = (first_ref, second_ref)[cell // GX]
        ref[0:8, here] = 2.0 * probes_ref[:, stored].astype(F32) - 1.0
        ref[8:16, here] = jnp.concatenate(
            [target_ref[:, stored], offsets_ref[:, stored], filler], axis=0
        )
    amp = jnp.full((1, TILE), amp_ref[0], F32)
    reach = jnp.exp(0.2 * jnp.log(4.0 * amp))
    square = reach * reach
    consts_ref[REACH : REACH + 1, :] = reach
    consts_ref[TOP : TOP + 1, :] = 5.0 * amp / (square * square)
    consts_ref[FACTOR : FACTOR + 1, :] = reach / jnp.full((1, TILE), scale_ref[0], F32)
    consts_ref[NOISE : NOISE + 1, :] = jnp.full((1, TILE), noise_ref[0], F32)


def constant(consts_ref, which):
    return consts_ref[which : which + 1, :]


def split_rows(values, level):
    first = values.astype(BF16).astype(F32)
    rest = values - first
    second = rest.astype(BF16).astype(F32)
    third = rest - second
    return jnp.where(level == 0, first, jnp.where(level == 1, second, third))


def feature_rows():
    row = lax.broadcasted_iota(jnp.int32, (FEATURES, TILE), 0)

    def level(order):
        out = jnp.zeros_like(row)
        for k, v in enumerate(order):
            if v:
                out = jnp.where(row == k, v, out)
        return out

    source = level([0, 0, 1, 1, 0, 2] * 2 + [0, 1, 2] + [0, 0, 0])
    target = level([0, 1, 0, 1, 2, 0] * 2 + [0, 0, 0] + [0, 1, 2])
    kind = jnp.where(row < 6, 0, jnp.where(row < 12, 1, jnp.where(row < 15, 2, jnp.where(row < 18, 3, 4))))
    return kind, source, target


def choose(kind, a, b, c, d):
    return jnp.where(
        kind == 0, a, jnp.where(kind == 1, b, jnp.where(kind == 2, c, jnp.where(kind == 3, d, 0.0)))
    )


def source_features(row_ref, factor, rows, out_ref):
    kind, source, _ = rows
    zero = jnp.zeros((TILE, FEATURES), BF16)
    out_ref[0] = zero
    out_ref[PAD - 1] = zero

    def one(tile, carry):
        a = factor * (row_ref[9:10, lanes(tile)] - 0.5)
        b = factor * (row_ref[10:11, lanes(tile)] - 0.5)
        values = choose(kind, a, b, a * a + b * b, 1.0)
        out_ref[tile + 1] = split_rows(values, source).T.astype(BF16)
        return carry

    lax.fori_loop(0, GX, one, 0, unroll=8)


def target_features(row_ref, tile, row_shift, col_shift, factor, rows):
    kind, _, target = rows
    a = factor * ((row_shift + 0.5) - row_ref[9:10, lanes(tile)])
    b = factor * ((col_shift + 0.5) - row_ref[10:11, lanes(tile)])
    values = choose(kind, 2.0 * a, 2.0 * b, 1.0, a * a + b * b)
    return split_rows(values, target).astype(BF16)


def fill_weights(targets, feats_ref, consts_ref, rows, also=None):
    factor = constant(consts_ref, FACTOR)
    reach = jnp.broadcast_to(constant(consts_ref, REACH), (TILE, TILE))
    top = jnp.broadcast_to(constant(consts_ref, TOP), (TILE, TILE))

    def one(tile, carry):
        for k in range(3):
            wanted = [
                target_features(ref, tile, float(row_shift), float(k - 1), factor, rows)
                for ref, row_shift, _, _ in targets
            ]
            squares = lax.dot_general(
                feats_ref[tile + k],
                wanted[0] if len(wanted) == 1 else jnp.concatenate(wanted, axis=1),
                (((1,), (0,)), ((), ())),
                preferred_element_type=F32,
            )
            for i, (_, _, weights_ref, combo) in enumerate(targets):
                here = jnp.maximum(squares[:, i * TILE : (i + 1) * TILE], 1e-12)
                close = jnp.maximum(reach - here * lax.rsqrt(here), 0.0)
                second = close * close
                weight = (second * second) * (top - close)
                high = weight.astype(BF16)
                low = (weight - high.astype(F32)).astype(BF16)
                base = k * 2 * TILE
                weights_ref[combo, tile, base : base + TILE, :] = high
                weights_ref[combo, tile, base + TILE : base + 2 * TILE, :] = low
        if also is not None:
            also(tile)
        return carry

    lax.fori_loop(0, GX, one, 0, unroll=8 // len(targets))


def spread_ends(out_ref):
    empty = jnp.zeros((2 * ROWS, 2 * TILE), BF16)
    out_ref[:, 0 : 2 * TILE] = empty
    out_ref[:, (PAD - 1) * 2 * TILE :] = empty


def spread_tile(values, out_ref, tile):
    high = values.astype(BF16)
    low = (values - high.astype(F32)).astype(BF16)
    both = jnp.concatenate([high, low], axis=0)
    at = pl.multiple_of((tile + 1) * 2 * TILE, 2 * TILE)
    out_ref[:, pl.ds(at, 2 * TILE)] = jnp.concatenate([both, both], axis=1)


def spread(row_ref, out_ref):
    spread_ends(out_ref)
    for tile in range(GX):
        spread_tile(row_ref[:, tile * TILE : (tile + 1) * TILE], out_ref, tile)


def spread_sides(row_ref, out_ref):
    empty = jnp.zeros((ROWS, 2 * TILE), BF16)
    out_ref[:, 0 : 2 * TILE] = empty
    out_ref[:, (PAD - 1) * 2 * TILE :] = empty
    row = lax.broadcasted_iota(jnp.int32, (8, TILE), 0)
    for tile in range(GX):
        here = slice(tile * TILE, (tile + 1) * TILE)
        target = row_ref[8:9, here]
        high = target.astype(BF16).astype(F32)
        rest = jnp.where(row == 0, high, jnp.where(row == 1, target - high, 0.0))
        both = jnp.concatenate([row_ref[0:8, here], rest], axis=0).astype(BF16)
        at = (tile + 1) * 2 * TILE
        out_ref[:, at : at + 2 * TILE] = jnp.concatenate([both, both], axis=1)


def banded(spread_ref, weights_ref, combo, tile):
    at = pl.multiple_of(tile * 2 * TILE, 2 * TILE)
    return jnp.dot(
        spread_ref[:, pl.ds(at, BAND)],
        weights_ref[combo, tile],
        preferred_element_type=F32,
    )


def joined(both):
    if both.shape[0] == 2 * ROWS:
        return both[0:ROWS] + both[ROWS:]
    row = lax.broadcasted_iota(jnp.int32, both.shape, 0)
    return both + jnp.where(row == 8, pltpu.roll(both, ROWS - 1, 0), 0.0)


GROUP = 16


def apply_row(own_ref, terms, consts_ref, out_ref, out_spread_ref, beside_ref=None):
    noise = constant(consts_ref, NOISE)
    spread_ends(out_spread_ref)

    def group(g, carry):
        for j in range(GROUP):
            tile = g * GROUP + j
            here = lanes(tile)
            both = banded(*terms[0], tile)
            if beside_ref is not None:
                beside_ref[:, here] = joined(both)
            for term in terms[1:]:
                both = both + banded(*term, tile)
            total = noise * own_ref[:, here] + joined(both)
            out_ref[:, here] = total
            spread_tile(total, out_spread_ref, tile)
        return carry

    lax.fori_loop(0, GX // GROUP, group, 0)


def two_sum(a, b):
    total = a + b
    part = total - a
    return total, (a - (total - part)) + (b - part)


def quick_sum(a, b):
    total = a + b
    return total, b - (total - a)


def halves(a):
    scaled = 4097.0 * a
    high = scaled - (scaled - a)
    return high, a - high


def two_product(a, b):
    a1, a2 = halves(a)
    b1, b2 = halves(b)
    product = a * b
    return product, ((a1 * b1 - product) + a1 * b2 + a2 * b1) + a2 * b2


class Pair:
    def __init__(self, high, low):
        self.high, self.low = high, low

    def __add__(self, other):
        total, error = two_sum(self.high, other.high)
        return Pair(*quick_sum(total, error + (self.low + other.low)))

    def __neg__(self):
        return Pair(-self.high, -self.low)

    def __sub__(self, other):
        return self + (-other)

    def __mul__(self, other):
        if not isinstance(other, Pair):
            return Pair(self.high * other, self.low * other)
        product, error = two_product(self.high, other.high)
        return Pair(*quick_sum(product, error + (self.high * other.low + self.low * other.high)))

    def __truediv__(self, other):
        first = self.high / other.high
        rest = self - other * Pair(first, jnp.zeros_like(first))
        return Pair(*quick_sum(first, rest.high / other.high))

    def where(self, keep, other):
        return Pair(jnp.where(keep, self.high, other.high), jnp.where(keep, self.low, other.low))


SUMS = 9
STRIDE = TILE // SUMS


def grid_mask(k):
    lane = lax.broadcasted_iota(jnp.int32, (ROWS, TILE), 1)
    row = lax.broadcasted_iota(jnp.int32, (ROWS, TILE), 0)
    return (lane == row + STRIDE * k) & (row < RHS)


def accumulate(sums, term):
    total, left = two_sum(sums[0], term)
    return total, sums[1] + left


def lines(sums):
    row = lax.broadcasted_iota(jnp.int32, (8, TILE), 0)
    lane = lax.broadcasted_iota(jnp.int32, (8, TILE), 1)
    blocks = [[(high[0:8], low[0:8]), lane == row + STRIDE * k] for k, (high, low) in enumerate(sums)]
    for start in range(0, len(sums), 8):
        last = [jnp.zeros((8, TILE), F32), jnp.zeros((8, TILE), F32)]
        group = sums[start : start + 8]
        for k, pair in enumerate(group):
            last = [jnp.where(row == k, jnp.broadcast_to(v[8:9], (8, TILE)), t) for v, t in zip(pair, last)]
        mask = (lane == 8 + STRIDE * (start + row)) & (row < len(group))
        blocks.append([tuple(last), mask])
    placed = [jnp.zeros((8, TILE), F32), jnp.zeros((8, TILE), F32)]
    for (high, low), mask in blocks:
        for shift in (64, 32, 16, 8, 4, 2, 1):
            high, left = two_sum(high, pltpu.roll(high, shift, 1))
            low = (low + pltpu.roll(low, shift, 1)) + left
        high, low = quick_sum(high, low)
        placed = [jnp.where(mask, high, placed[0]), jnp.where(mask, low, placed[1])]
    return [jnp.sum(p, axis=0, keepdims=True) for p in placed]


def inner_kernel(
    first_ref, second_ref, consts_ref, left_ref, right_ref, spread0_ref, spread1_ref, feats_ref
):
    rows = feature_rows()
    for slot, (own_ref, weights_ref, spread_ref) in enumerate(
        ((first_ref, left_ref, spread0_ref), (second_ref, right_ref, spread1_ref))
    ):
        source_features(own_ref, constant(consts_ref, FACTOR), rows, feats_ref)
        targets = ((first_ref, slot, weights_ref, 0), (second_ref, slot - 1, weights_ref, 1))
        fill_weights(targets, feats_ref, consts_ref, rows)
        spread_sides(own_ref, spread_ref)


def outer_kernel(
    slot,
    other_ref,
    own_ref,
    consts_ref,
    left_ref,
    right_ref,
    spread0_ref,
    spread1_ref,
    weights_ref,
    out_ref,
    out_spread_ref,
    *more,
):
    beside_ref, feats_ref, spread_ref = more if slot else (None, *more)
    rows = feature_rows()
    source_features(other_ref, constant(consts_ref, FACTOR), rows, feats_ref)
    noise = constant(consts_ref, NOISE)

    def own_part(tile):
        here = lanes(tile)
        both = banded(spread0_ref, left_ref, slot, tile) + banded(spread1_ref, right_ref, slot, tile)
        out_ref[:, here] = noise * own_ref[:, here] + joined(both)

    targets = ((own_ref, 2 * slot - 1, weights_ref, 0),)
    fill_weights(targets, feats_ref, consts_ref, rows, own_part)
    spread_sides(other_ref, spread_ref)
    spread_ends(out_spread_ref)
    for tile in range(GX):
        here = slice(tile * TILE, (tile + 1) * TILE)
        halo = joined(banded(spread_ref, weights_ref, 0, tile))
        if beside_ref is not None:
            beside_ref[:, here] = halo
        total = out_ref[:, here] + halo
        out_ref[:, here] = total
        spread_tile(total, out_spread_ref, tile)


def product_kernel(
    other_ref,
    own_ref,
    consts_ref,
    left_ref,
    right_ref,
    weights_ref,
    spread0_ref,
    spread1_ref,
    out_ref,
    out_spread_ref,
    spread_ref,
):
    spread(other_ref, spread_ref)
    terms = ((spread_ref, weights_ref, 0), (spread0_ref, left_ref, 0), (spread1_ref, right_ref, 0))
    apply_row(own_ref, terms, consts_ref, out_ref, out_spread_ref)


def gram_kernel(
    below_ref,
    b0_ref,
    b1_ref,
    f0_ref,
    f1_ref,
    g0_ref,
    b_beside_ref,
    consts_ref,
    left_ref,
    right_ref,
    under_ref,
    f0_spread_ref,
    f1_spread_ref,
    g0_spread_ref,
    g1_ref,
    sums_ref,
    spread_ref,
    g1_spread_ref,
    f_beside_ref,
):
    spread(below_ref, spread_ref)
    terms = ((spread_ref, under_ref, 0), (f0_spread_ref, left_ref, 1), (f1_spread_ref, right_ref, 1))
    apply_row(f1_ref, terms, consts_ref, g1_ref, g1_spread_ref, f_beside_ref)
    zero = jnp.zeros((ROWS, TILE), F32)
    noise = constant(consts_ref, NOISE)

    def group(g, sums):
        sums = list(sums)
        terms = [zero] * SUMS
        for j in range(8):
            tile = g * 8 + j
            here = lanes(tile)
            for half, refs in enumerate(((b0_ref, f0_ref, g0_ref), (b1_ref, f1_ref, g1_ref))):
                v = [ref[:, here] for ref in refs]
                for k, (i, m) in enumerate(((0, 0), (0, 1), (0, 2), (1, 1), (1, 2), (2, 2))):
                    terms[k] = terms[k] + v[i] * v[m]
                both = banded(g0_spread_ref, left_ref, half, tile)
                both = both + banded(g1_spread_ref, right_ref, half, tile)
                image = noise * v[2] + joined(both)
                for k in range(3):
                    terms[6 + k] = terms[6 + k] + v[k] * image
                if half == 1:
                    terms[6] = terms[6] + v[2] * b_beside_ref[:, here]
                    terms[7] = terms[7] + v[2] * f_beside_ref[:, here]
            if j % 2 == 1:
                sums = [accumulate(s, t) for s, t in zip(sums, terms)]
                terms = [zero] * SUMS
        return tuple(sums)

    sums = lax.fori_loop(0, GX // 8, group, ((zero, zero),) * SUMS)
    for k, (high, low) in enumerate(sums):
        sums_ref[k, 0] = high
        sums_ref[k, 1] = low


def moment_kernel(sums_ref, below_ref, b_ref, f_ref, g_ref, weights_ref, out_ref, spread_ref):
    spread(below_ref, spread_ref)
    zero = jnp.zeros((ROWS, TILE), F32)
    sums = [(sums_ref[k, 0], sums_ref[k, 1]) for k in range(SUMS)]
    terms = [zero] * 3
    for tile in range(GX):
        here = slice(tile * TILE, (tile + 1) * TILE)
        image = joined(banded(spread_ref, weights_ref, 0, tile))
        factors = (b_ref[:, here], f_ref[:, here], 2.0 * g_ref[:, here])
        terms = [t + v * image for t, v in zip(terms, factors)]
        if tile % 4 == 3:
            sums[6:] = [accumulate(s, t) for s, t in zip(sums[6:], terms)]
            terms = [zero] * 3
    both = jnp.concatenate(lines(sums), axis=1)
    out_ref[...] = jnp.broadcast_to(both[None], out_ref.shape)


def finish_kernel(
    points,
    cell_hbm,
    consts_ref,
    parts_ref,
    b0_ref,
    b1_ref,
    f0_ref,
    f1_ref,
    g0_ref,
    g1_ref,
    out_ref,
    quad_ref,
    cell_ref,
    grid_ref,
    sem,
):
    copy = pltpu.make_async_copy(cell_hbm, cell_ref, sem)
    copy.start()
    high, low = parts_ref[:, 0, 0:TILE], parts_ref[:, 0, TILE:]
    while high.shape[0] > 8:
        half = high.shape[0] // 2
        high, left = two_sum(high[:half], high[half:])
        low = (low[:half] + low[half:]) + left
    for shift in (4, 2, 1):
        high, left = two_sum(high, pltpu.roll(high, shift, 0))
        low = (low + pltpu.roll(low, shift, 0)) + left
    high, low = quick_sum(high, low)
    bb, bf, bg, ff, fg, gg, bag, fag, gag = (
        Pair(high, low)
        if k == 0
        else Pair(pltpu.roll(high, TILE - STRIDE * k, 1), pltpu.roll(low, TILE - STRIDE * k, 1))
        for k in range(SUMS)
    )
    zero = jnp.zeros_like(high)
    none = Pair(zero, zero)
    one = Pair(zero + 1.0, zero)
    most = jnp.broadcast_to(1.0 / constant(consts_ref, NOISE), high.shape)

    floor = bb.high * 1e-11

    def step(square, product):
        good = (square.high > floor) & (product.high > 0.0)
        ratio = square / product.where(good, one)
        fits = ratio.high < most
        return ratio.where(fits, Pair(most, zero)).where(good, none), good

    def over(a, b, good):
        return (a / b.where(good, one)).where(good, none)

    alpha0, good0 = step(bb, bf)
    rr1 = bb - alpha0 * (bf * 2.0 - alpha0 * ff)
    beta0 = over(rr1, bb, good0)
    p0, p1 = one + beta0, -alpha0
    alpha1, good1 = step(rr1, p0 * (p0 * bf + p1 * (bg + ff)) + p1 * p1 * fg)
    r1, r2 = -(alpha0 + alpha1 * p0), -(alpha1 * p1)
    rr2 = bb + r1 * (bf * 2.0 + r1 * ff) + r2 * (bg * 2.0 + r1 * fg * 2.0 + r2 * gg)
    beta1 = over(rr2, rr1, good1)
    q0, q1, q2 = one + beta1 * p0, r1 + beta1 * p1, r2
    alpha2, good2 = step(
        rr2,
        q0 * (q0 * bf + q1 * (bg + ff) + q2 * (fg + bag)) + q1 * (q1 * fg + q2 * (gg + fag)) + q2 * q2 * gag,
    )
    alpha2 = alpha2.where(good1, none)
    on_b = alpha0 + alpha1 * p0 + alpha2 * q0
    on_f = alpha1 * p1 + alpha2 * q1
    on_g = alpha2 * q2
    quad = on_b * bb + on_f * bf + on_g * bg
    quad_ref[...] = (quad.high / points)[0:1, 0:RHS]
    mask = grid_mask(0)
    c0, c1, c2 = (
        jnp.broadcast_to(
            jnp.sum(
                jnp.where(mask, jnp.concatenate([c.high, c.high], axis=0), 0.0), axis=1, keepdims=True
            ),
            (ROWS, TILE),
        )
        for c in (on_b, on_f, on_g)
    )
    for half, (b_ref, f_ref, g_ref) in enumerate(
        ((b0_ref, f0_ref, g0_ref), (b1_ref, f1_ref, g1_ref))
    ):
        for tile in range(GX):
            here = slice(tile * TILE, (tile + 1) * TILE)
            grid_ref[half * GX + tile] = (
                c0 * b_ref[:, here] + c1 * f_ref[:, here] + c2 * g_ref[:, here]
            )
    copy.wait()
    for s in range(cell_ref.shape[0]):
        out_ref[:, s * TILE : (s + 1) * TILE] = grid_ref[cell_ref[s], 0:RHS, :]


def shards(offsets, tile_cell, probes, target, lengthscale, amplitude, noise):
    size = lax.axis_size("rows")
    points = size * tile_cell.shape[0] * TILE
    down = [(i, i + 1) for i in range(size - 1)]
    up = [(i + 1, i) for i in range(size - 1)]

    tiles = tile_cell.shape[0]
    first, second, consts = call(
        pack_kernel,
        "pack",
        (pltpu.VMEM((ROWS, WIDE), F32), pltpu.VMEM((ROWS, WIDE), F32), pltpu.VMEM((8, TILE), F32)),
        [HBM] * 4 + [SMEM] * 3,
        [
            pltpu.SMEM((tiles,), jnp.int32),
            pltpu.SMEM((tiles,), jnp.int32),
            pltpu.VMEM((2, tiles * TILE), F32),
            pltpu.VMEM((8, tiles * TILE), jnp.int32),
            pltpu.VMEM((1, tiles * TILE), F32),
            pltpu.SemaphoreType.DMA((4,)),
        ],
        flops=1 << 20,
        limit=60.5,
    )(
        tile_cell,
        offsets,
        probes,
        target.reshape(1, -1),
        lengthscale,
        amplitude,
        noise,
    )

    def outer(slot, other, own):
        return call(
            lambda *refs: outer_kernel(slot, *refs),
            f"outer{slot}",
            (weight_rows(1), grid_row(), spread_row()) + (grid_row(),) * slot,
            [VMEM] * 7,
            [feature_tiles(), spread_row(ROWS)],
            flops=1 << 30,
        )(other, own, consts, left, right, b0_spread, b1_spread)

    above = lax.ppermute(second, "rows", down)
    below = lax.ppermute(first, "rows", up)
    left, right, b0_spread, b1_spread = call(
        inner_kernel,
        "inner",
        (weight_rows(2), weight_rows(2), spread_row(ROWS), spread_row(ROWS)),
        [VMEM] * 3,
        [feature_tiles()],
        flops=1 << 30,
    )(first, second, consts)
    over, f0, f0_spread = outer(0, above, first)
    f_below = lax.ppermute(f0, "rows", up)
    under, f1, f1_spread, b_beside = outer(1, below, second)
    f_above = lax.ppermute(f1, "rows", down)
    g0, g0_spread = call(
        product_kernel,
        "product",
        (grid_row(), spread_row()),
        [VMEM] * 8,
        [spread_row()],
        flops=1 << 29,
    )(f_above, f0, consts, left, right, over, f0_spread, f1_spread)
    g_below = lax.ppermute(g0, "rows", up)
    g1, sums = call(
        gram_kernel,
        "gram",
        (grid_row(), jax.ShapeDtypeStruct((SUMS, 2, ROWS, TILE), F32)),
        [VMEM] * 14,
        [spread_row(), spread_row(), pltpu.VMEM((ROWS, WIDE), F32)],
        flops=1 << 29,
    )(f_below, first, second, f0, f1, g0, b_beside, consts, left, right, under, f0_spread, f1_spread, g0_spread)
    parts = call(
        moment_kernel,
        "moment",
        jax.ShapeDtypeStruct((size, 1, 2 * TILE), F32),
        [VMEM] * 6,
        [spread_row()],
        flops=1 << 29,
    )(sums, g_below, second, f1, g1, under)
    parts = lax.all_to_all(parts, "rows", split_axis=0, concat_axis=0, tiled=True)

    solutions, quad = call(
        lambda *refs: finish_kernel(float(points), *refs),
        "finish",
        (
            jax.ShapeDtypeStruct((RHS, tiles * TILE), F32),
            jax.ShapeDtypeStruct((1, RHS), F32),
        ),
        [HBM] + [VMEM] * 8,
        [
            pltpu.SMEM((tiles,), jnp.int32),
            pltpu.VMEM((tiles, ROWS, TILE), F32),
            pltpu.SemaphoreType.DMA,
        ],
        flops=1 << 20,
    )(tile_cell, consts, parts, first, second, f0, f1, g0, g1)
    return (solutions, quad.reshape(RHS))


def solution(mesh):
    return jax.shard_map(
        shards,
        mesh=mesh,
        in_specs=(
            P(None, "rows"),
            P("rows"),
            P(None, "rows"),
            P("rows"),
            P("hyp"),
            P("hyp"),
            P("hyp"),
        ),
        out_specs=(P("hyp", "rows"), P("hyp")),
        check_vma=False,
    )
```

```python
import jax
import jax.numpy as jnp
from jax import lax
from jax.experimental import pallas as pl
from jax.experimental.pallas import tpu as pltpu
from jax.sharding import PartitionSpec as P

TILE = 128
GX = 16
RHS = 9
ROWS = 16
WIDE = GX * TILE
FEATURES = 32
PAD = GX + 2
BAND = 3 * 2 * TILE
F32 = jnp.float32
BF16 = jnp.bfloat16
TINY = 1e-30

VMEM = pl.BlockSpec(memory_space=pltpu.VMEM)
HBM = pl.BlockSpec(memory_space=pltpu.HBM)
SMEM = pl.BlockSpec(memory_space=pltpu.SMEM)
REACH, TOP, FACTOR, NOISE = range(4)


def call(kernel, name, out_shape, in_specs, scratch=(), flops=0, limit=12):
    return pl.pallas_call(
        kernel,
        name=name,
        out_shape=out_shape,
        in_specs=in_specs,
        out_specs=jax.tree.map(lambda _: VMEM, out_shape),
        scratch_shapes=list(scratch),
        cost_estimate=pl.CostEstimate(flops=flops, bytes_accessed=1 << 20, transcendentals=0),
        compiler_params=pltpu.CompilerParams(vmem_limit_bytes=int(limit * 2**20)),
    )


def grid_row():
    return jax.ShapeDtypeStruct((ROWS, WIDE), F32)


def spread_row(rows=2 * ROWS):
    return pltpu.VMEM((rows, PAD * 2 * TILE), BF16)


def weight_rows(count):
    return pltpu.VMEM((count, GX, BAND, TILE), BF16)


def feature_tiles():
    return pltpu.VMEM((PAD, TILE, FEATURES), BF16)


def lanes(tile, width=TILE):
    return pl.ds(pl.multiple_of(tile * width, width), width)


def pack_kernel(
    cell_hbm,
    offsets_hbm,
    probes_hbm,
    target_hbm,
    scale_ref,
    amp_ref,
    noise_ref,
    first_ref,
    second_ref,
    consts_ref,
    cell_ref,
    from_ref,
    offsets_ref,
    probes_ref,
    target_ref,
    sems,
):
    copies = [
        pltpu.make_async_copy(source, dest, sems.at[i])
        for i, (source, dest) in enumerate(
            (
                (cell_hbm, cell_ref),
                (offsets_hbm, offsets_ref),
                (probes_hbm, probes_ref),
                (target_hbm, target_ref),
            )
        )
    ]
    for copy in copies:
        copy.start()
    for copy in copies:
        copy.wait()
    for s in range(cell_ref.shape[0]):
        from_ref[cell_ref[s]] = s
    filler = jnp.zeros((ROWS - RHS - 2, TILE), F32)
    for cell in range(cell_ref.shape[0]):
        stored = lanes(from_ref[cell])
        here = slice(cell % GX * TILE, (cell % GX + 1) * TILE)
        ref = (first_ref, second_ref)[cell // GX]
        ref[0:8, here] = 2.0 * probes_ref[:, stored].astype(F32) - 1.0
        ref[8:16, here] = jnp.concatenate(
            [target_ref[:, stored], offsets_ref[:, stored], filler], axis=0
        )
    amp = jnp.full((1, TILE), amp_ref[0], F32)
    reach = jnp.exp(0.2 * jnp.log(4.0 * amp))
    square = reach * reach
    consts_ref[REACH : REACH + 1, :] = reach
    consts_ref[TOP : TOP + 1, :] = 5.0 * amp / (square * square)
    consts_ref[FACTOR : FACTOR + 1, :] = reach / jnp.full((1, TILE), scale_ref[0], F32)
    consts_ref[NOISE : NOISE + 1, :] = jnp.full((1, TILE), noise_ref[0], F32)


def constant(consts_ref, which):
    return consts_ref[which : which + 1, :]


def split_rows(values, level):
    first = values.astype(BF16).astype(F32)
    rest = values - first
    second = rest.astype(BF16).astype(F32)
    third = rest - second
    return jnp.where(level == 0, first, jnp.where(level == 1, second, third))


def feature_rows():
    row = lax.broadcasted_iota(jnp.int32, (FEATURES, TILE), 0)

    def level(order):
        out = jnp.zeros_like(row)
        for k, v in enumerate(order):
            if v:
                out = jnp.where(row == k, v, out)
        return out

    source = level([0, 0, 1, 1, 0, 2] * 2 + [0, 1, 2] + [0, 0, 0])
    target = level([0, 1, 0, 1, 2, 0] * 2 + [0, 0, 0] + [0, 1, 2])
    kind = jnp.where(row < 6, 0, jnp.where(row < 12, 1, jnp.where(row < 15, 2, jnp.where(row < 18, 3, 4))))
    return kind, source, target


def choose(kind, a, b, c, d):
    return jnp.where(
        kind == 0, a, jnp.where(kind == 1, b, jnp.where(kind == 2, c, jnp.where(kind == 3, d, 0.0)))
    )


def source_features(row_ref, factor, rows, out_ref):
    kind, source, _ = rows
    zero = jnp.zeros((TILE, FEATURES), BF16)
    out_ref[0] = zero
    out_ref[PAD - 1] = zero

    def one(tile, carry):
        a = factor * (row_ref[9:10, lanes(tile)] - 0.5)
        b = factor * (row_ref[10:11, lanes(tile)] - 0.5)
        values = choose(kind, a, b, a * a + b * b, 1.0)
        out_ref[tile + 1] = split_rows(values, source).T.astype(BF16)
        return carry

    lax.fori_loop(0, GX, one, 0, unroll=8)


def target_features(row_ref, tile, row_shift, col_shift, factor, rows):
    kind, _, target = rows
    a = factor * ((row_shift + 0.5) - row_ref[9:10, lanes(tile)])
    b = factor * ((col_shift + 0.5) - row_ref[10:11, lanes(tile)])
    values = choose(kind, 2.0 * a, 2.0 * b, 1.0, a * a + b * b)
    return split_rows(values, target).astype(BF16)


def fill_weights(targets, feats_ref, consts_ref, rows, also=None):
    factor = constant(consts_ref, FACTOR)
    reach = jnp.broadcast_to(constant(consts_ref, REACH), (TILE, TILE))
    top = jnp.broadcast_to(constant(consts_ref, TOP), (TILE, TILE))

    def one(tile, carry):
        for k in range(3):
            wanted = [
                target_features(ref, tile, float(row_shift), float(k - 1), factor, rows)
                for ref, row_shift, _, _ in targets
            ]
            squares = lax.dot_general(
                feats_ref[tile + k],
                wanted[0] if len(wanted) == 1 else jnp.concatenate(wanted, axis=1),
                (((1,), (0,)), ((), ())),
                preferred_element_type=F32,
            )
            for i, (_, _, weights_ref, combo) in enumerate(targets):
                here = jnp.maximum(squares[:, i * TILE : (i + 1) * TILE], 1e-12)
                close = jnp.maximum(reach - here * lax.rsqrt(here), 0.0)
                second = close * close
                weight = (second * second) * (top - close)
                high = weight.astype(BF16)
                low = (weight - high.astype(F32)).astype(BF16)
                base = k * 2 * TILE
                weights_ref[combo, tile, base : base + TILE, :] = high
                weights_ref[combo, tile, base + TILE : base + 2 * TILE, :] = low
        if also is not None:
            also(tile)
        return carry

    lax.fori_loop(0, GX, one, 0, unroll=8 // len(targets))


def spread_ends(out_ref):
    empty = jnp.zeros((2 * ROWS, 2 * TILE), BF16)
    out_ref[:, 0 : 2 * TILE] = empty
    out_ref[:, (PAD - 1) * 2 * TILE :] = empty


def spread_tile(values, out_ref, tile):
    high = values.astype(BF16)
    low = (values - high.astype(F32)).astype(BF16)
    both = jnp.concatenate([high, low], axis=0)
    at = pl.multiple_of((tile + 1) * 2 * TILE, 2 * TILE)
    out_ref[:, pl.ds(at, 2 * TILE)] = jnp.concatenate([both, both], axis=1)


def spread(row_ref, out_ref):
    spread_ends(out_ref)
    for tile in range(GX):
        spread_tile(row_ref[:, tile * TILE : (tile + 1) * TILE], out_ref, tile)


def spread_sides(row_ref, out_ref):
    empty = jnp.zeros((ROWS, 2 * TILE), BF16)
    out_ref[:, 0 : 2 * TILE] = empty
    out_ref[:, (PAD - 1) * 2 * TILE :] = empty
    row = lax.broadcasted_iota(jnp.int32, (8, TILE), 0)
    for tile in range(GX):
        here = slice(tile * TILE, (tile + 1) * TILE)
        target = row_ref[8:9, here]
        high = target.astype(BF16).astype(F32)
        rest = jnp.where(row == 0, high, jnp.where(row == 1, target - high, 0.0))
        both = jnp.concatenate([row_ref[0:8, here], rest], axis=0).astype(BF16)
        at = (tile + 1) * 2 * TILE
        out_ref[:, at : at + 2 * TILE] = jnp.concatenate([both, both], axis=1)


def banded(spread_ref, weights_ref, combo, tile):
    at = pl.multiple_of(tile * 2 * TILE, 2 * TILE)
    return jnp.dot(
        spread_ref[:, pl.ds(at, BAND)],
        weights_ref[combo, tile],
        preferred_element_type=F32,
    )


def joined(both):
    if both.shape[0] == 2 * ROWS:
        return both[0:ROWS] + both[ROWS:]
    row = lax.broadcasted_iota(jnp.int32, both.shape, 0)
    return both + jnp.where(row == 8, pltpu.roll(both, ROWS - 1, 0), 0.0)


GROUP = 16


def apply_row(own_ref, ahead_ref, terms, consts_ref, out_ref, out_spread_ref, beside_ref=None):
    noise = constant(consts_ref, NOISE)
    spread_ends(out_spread_ref)

    def group(g, carry):
        for j in range(GROUP):
            tile = g * GROUP + j
            here = lanes(tile)
            both = banded(*terms[0], tile)
            if beside_ref is not None:
                beside_ref[:, here] = joined(both)
            for term in terms[1:]:
                both = both + banded(*term, tile)
            total = noise * own_ref[:, here] + ahead_ref[:, here] + joined(both)
            out_ref[:, here] = total
            spread_tile(total, out_spread_ref, tile)
        return carry

    lax.fori_loop(0, GX // GROUP, group, 0)


def two_sum(a, b):
    total = a + b
    part = total - a
    return total, (a - (total - part)) + (b - part)


def quick_sum(a, b):
    total = a + b
    return total, b - (total - a)


def halves(a):
    scaled = 4097.0 * a
    high = scaled - (scaled - a)
    return high, a - high


def two_product(a, b):
    a1, a2 = halves(a)
    b1, b2 = halves(b)
    product = a * b
    return product, ((a1 * b1 - product) + a1 * b2 + a2 * b1) + a2 * b2


class Pair:
    def __init__(self, high, low):
        self.high, self.low = high, low

    def __add__(self, other):
        total, error = two_sum(self.high, other.high)
        return Pair(*quick_sum(total, error + (self.low + other.low)))

    def __neg__(self):
        return Pair(-self.high, -self.low)

    def __sub__(self, other):
        return self + (-other)

    def __mul__(self, other):
        if not isinstance(other, Pair):
            return Pair(self.high * other, self.low * other)
        product, error = two_product(self.high, other.high)
        return Pair(*quick_sum(product, error + (self.high * other.low + self.low * other.high)))

    def __truediv__(self, other):
        first = self.high / other.high
        rest = self - other * Pair(first, jnp.zeros_like(first))
        return Pair(*quick_sum(first, rest.high / other.high))

    def where(self, keep, other):
        return Pair(jnp.where(keep, self.high, other.high), jnp.where(keep, self.low, other.low))


SUMS = 9
STRIDE = TILE // SUMS


def grid_mask(k):
    lane = lax.broadcasted_iota(jnp.int32, (ROWS, TILE), 1)
    row = lax.broadcasted_iota(jnp.int32, (ROWS, TILE), 0)
    return (lane == row + STRIDE * k) & (row < RHS)


def accumulate(sums, term):
    total, left = two_sum(sums[0], term)
    return total, sums[1] + left


def lines(sums):
    row = lax.broadcasted_iota(jnp.int32, (8, TILE), 0)
    lane = lax.broadcasted_iota(jnp.int32, (8, TILE), 1)
    blocks = [[(high[0:8], low[0:8]), lane == row + STRIDE * k] for k, (high, low) in enumerate(sums)]
    for start in range(0, len(sums), 8):
        last = [jnp.zeros((8, TILE), F32), jnp.zeros((8, TILE), F32)]
        group = sums[start : start + 8]
        for k, pair in enumerate(group):
            last = [jnp.where(row == k, jnp.broadcast_to(v[8:9], (8, TILE)), t) for v, t in zip(pair, last)]
        mask = (lane == 8 + STRIDE * (start + row)) & (row < len(group))
        blocks.append([tuple(last), mask])
    placed = [jnp.zeros((8, TILE), F32), jnp.zeros((8, TILE), F32)]
    for (high, low), mask in blocks:
        for shift in (64, 32, 16, 8, 4, 2, 1):
            high, left = two_sum(high, pltpu.roll(high, shift, 1))
            low = (low + pltpu.roll(low, shift, 1)) + left
        high, low = quick_sum(high, low)
        placed = [jnp.where(mask, high, placed[0]), jnp.where(mask, low, placed[1])]
    return [jnp.sum(p, axis=0, keepdims=True) for p in placed]


def inner_kernel(
    first_ref,
    second_ref,
    consts_ref,
    left_ref,
    right_ref,
    spread0_ref,
    spread1_ref,
    part0_ref,
    part1_ref,
    feats_ref,
):
    rows = feature_rows()

    def first_part(tile):
        for slot, part_ref in enumerate((part0_ref, part1_ref)):
            part_ref[:, lanes(tile)] = joined(banded(spread0_ref, left_ref, slot, tile))

    for slot, (own_ref, weights_ref, spread_ref) in enumerate(
        ((first_ref, left_ref, spread0_ref), (second_ref, right_ref, spread1_ref))
    ):
        source_features(own_ref, constant(consts_ref, FACTOR), rows, feats_ref)
        targets = ((first_ref, slot, weights_ref, 0), (second_ref, slot - 1, weights_ref, 1))
        fill_weights(targets, feats_ref, consts_ref, rows, first_part if slot else None)
        spread_sides(own_ref, spread_ref)


def outer_kernel(slot, other_ref, own_ref, consts_ref, part_ref, right_ref, spread1_ref, *more):
    if slot:
        weights_ref, out_ref, out_spread_ref, beside_ref, feats_ref, spread_ref = more
        ahead, beside = (), beside_ref
    else:
        f1_ref, weights_ref, out_ref, out_spread_ref, ahead0_ref, ahead1_ref, feats_ref, spread_ref = more
        ahead, beside = (ahead0_ref, ahead1_ref), None
    rows = feature_rows()
    source_features(other_ref, constant(consts_ref, FACTOR), rows, feats_ref)
    noise = constant(consts_ref, NOISE)

    def own_part(tile):
        here = lanes(tile)
        own = noise * own_ref[:, here] + part_ref[:, here]
        out_ref[:, here] = own + joined(banded(spread1_ref, right_ref, slot, tile))
        for i, ahead_ref in enumerate(ahead):
            ahead_ref[:, here] = joined(banded(f1_ref, right_ref, i, tile))

    targets = ((own_ref, 2 * slot - 1, weights_ref, 0),)
    fill_weights(targets, feats_ref, consts_ref, rows, own_part)
    spread_sides(other_ref, spread_ref)
    spread_ends(out_spread_ref)
    for tile in range(GX):
        here = slice(tile * TILE, (tile + 1) * TILE)
        halo = joined(banded(spread_ref, weights_ref, 0, tile))
        if beside is not None:
            beside[:, here] = halo
        total = out_ref[:, here] + halo
        out_ref[:, here] = total
        spread_tile(total, out_spread_ref, tile)


def product_kernel(
    other_ref,
    own_ref,
    ahead_ref,
    consts_ref,
    left_ref,
    weights_ref,
    spread0_ref,
    out_ref,
    out_spread_ref,
    spread_ref,
):
    spread(other_ref, spread_ref)
    terms = ((spread_ref, weights_ref, 0), (spread0_ref, left_ref, 0))
    apply_row(own_ref, ahead_ref, terms, consts_ref, out_ref, out_spread_ref)


def gram_kernel(
    below_ref,
    b0_ref,
    b1_ref,
    f0_ref,
    f1_ref,
    g0_ref,
    b_beside_ref,
    consts_ref,
    left_ref,
    right_ref,
    under_ref,
    f0_spread_ref,
    ahead_ref,
    g0_spread_ref,
    g1_ref,
    sums_ref,
    spread_ref,
    g1_spread_ref,
    f_beside_ref,
):
    spread(below_ref, spread_ref)
    terms = ((spread_ref, under_ref, 0), (f0_spread_ref, left_ref, 1))
    apply_row(f1_ref, ahead_ref, terms, consts_ref, g1_ref, g1_spread_ref, f_beside_ref)
    zero = jnp.zeros((ROWS, TILE), F32)
    noise = constant(consts_ref, NOISE)

    def group(g, sums):
        sums = list(sums)
        terms = [zero] * SUMS
        for j in range(8):
            tile = g * 8 + j
            here = lanes(tile)
            for half, refs in enumerate(((b0_ref, f0_ref, g0_ref), (b1_ref, f1_ref, g1_ref))):
                v = [ref[:, here] for ref in refs]
                for k, (i, m) in enumerate(((0, 0), (0, 1), (0, 2), (1, 1), (1, 2), (2, 2))):
                    terms[k] = terms[k] + v[i] * v[m]
                both = banded(g0_spread_ref, left_ref, half, tile)
                both = both + banded(g1_spread_ref, right_ref, half, tile)
                image = noise * v[2] + joined(both)
                for k in range(3):
                    terms[6 + k] = terms[6 + k] + v[k] * image
                if half == 1:
                    terms[6] = terms[6] + v[2] * b_beside_ref[:, here]
                    terms[7] = terms[7] + v[2] * f_beside_ref[:, here]
            if j % 2 == 1:
                sums = [accumulate(s, t) for s, t in zip(sums, terms)]
                terms = [zero] * SUMS
        return tuple(sums)

    sums = lax.fori_loop(0, GX // 8, group, ((zero, zero),) * SUMS)
    for k, (high, low) in enumerate(sums):
        sums_ref[k, 0] = high
        sums_ref[k, 1] = low


def moment_kernel(sums_ref, below_ref, b_ref, f_ref, g_ref, weights_ref, out_ref, spread_ref):
    spread(below_ref, spread_ref)
    zero = jnp.zeros((ROWS, TILE), F32)
    sums = [(sums_ref[k, 0], sums_ref[k, 1]) for k in range(SUMS)]
    terms = [zero] * 3
    for tile in range(GX):
        here = slice(tile * TILE, (tile + 1) * TILE)
        image = joined(banded(spread_ref, weights_ref, 0, tile))
        factors = (b_ref[:, here], f_ref[:, here], 2.0 * g_ref[:, here])
        terms = [t + v * image for t, v in zip(terms, factors)]
        if tile % 4 == 3:
            sums[6:] = [accumulate(s, t) for s, t in zip(sums[6:], terms)]
            terms = [zero] * 3
    both = jnp.concatenate(lines(sums), axis=1)
    out_ref[...] = jnp.broadcast_to(both[None], out_ref.shape)


def finish_kernel(
    points,
    cell_hbm,
    consts_ref,
    parts_ref,
    b0_ref,
    b1_ref,
    f0_ref,
    f1_ref,
    g0_ref,
    g1_ref,
    out_ref,
    quad_ref,
    cell_ref,
    grid_ref,
    sem,
):
    copy = pltpu.make_async_copy(cell_hbm, cell_ref, sem)
    copy.start()
    high, low = parts_ref[:, 0, 0:TILE], parts_ref[:, 0, TILE:]
    while high.shape[0] > 8:
        half = high.shape[0] // 2
        high, left = two_sum(high[:half], high[half:])
        low = (low[:half] + low[half:]) + left
    for shift in (4, 2, 1):
        high, left = two_sum(high, pltpu.roll(high, shift, 0))
        low = (low + pltpu.roll(low, shift, 0)) + left
    high, low = quick_sum(high, low)
    bb, bf, bg, ff, fg, gg, bag, fag, gag = (
        Pair(high, low)
        if k == 0
        else Pair(pltpu.roll(high, TILE - STRIDE * k, 1), pltpu.roll(low, TILE - STRIDE * k, 1))
        for k in range(SUMS)
    )
    zero = jnp.zeros_like(high)
    none = Pair(zero, zero)
    one = Pair(zero + 1.0, zero)
    most = jnp.broadcast_to(1.0 / constant(consts_ref, NOISE), high.shape)

    floor = bb.high * 1e-11

    def step(square, product):
        good = (square.high > floor) & (product.high > 0.0)
        ratio = square / product.where(good, one)
        fits = ratio.high < most
        return ratio.where(fits, Pair(most, zero)).where(good, none), good

    def over(a, b, good):
        return (a / b.where(good, one)).where(good, none)

    alpha0, good0 = step(bb, bf)
    rr1 = bb - alpha0 * (bf * 2.0 - alpha0 * ff)
    beta0 = over(rr1, bb, good0)
    p0, p1 = one + beta0, -alpha0
    alpha1, good1 = step(rr1, p0 * (p0 * bf + p1 * (bg + ff)) + p1 * p1 * fg)
    r1, r2 = -(alpha0 + alpha1 * p0), -(alpha1 * p1)
    rr2 = bb + r1 * (bf * 2.0 + r1 * ff) + r2 * (bg * 2.0 + r1 * fg * 2.0 + r2 * gg)
    beta1 = over(rr2, rr1, good1)
    q0, q1, q2 = one + beta1 * p0, r1 + beta1 * p1, r2
    alpha2, good2 = step(
        rr2,
        q0 * (q0 * bf + q1 * (bg + ff) + q2 * (fg + bag)) + q1 * (q1 * fg + q2 * (gg + fag)) + q2 * q2 * gag,
    )
    alpha2 = alpha2.where(good1, none)
    on_b = alpha0 + alpha1 * p0 + alpha2 * q0
    on_f = alpha1 * p1 + alpha2 * q1
    on_g = alpha2 * q2
    quad = on_b * bb + on_f * bf + on_g * bg
    quad_ref[...] = (quad.high / points)[0:1, 0:RHS]
    mask = grid_mask(0)
    c0, c1, c2 = (
        jnp.broadcast_to(
            jnp.sum(
                jnp.where(mask, jnp.concatenate([c.high, c.high], axis=0), 0.0), axis=1, keepdims=True
            ),
            (ROWS, TILE),
        )
        for c in (on_b, on_f, on_g)
    )
    for half, (b_ref, f_ref, g_ref) in enumerate(
        ((b0_ref, f0_ref, g0_ref), (b1_ref, f1_ref, g1_ref))
    ):
        for tile in range(GX):
            here = slice(tile * TILE, (tile + 1) * TILE)
            grid_ref[half * GX + tile] = (
                c0 * b_ref[:, here] + c1 * f_ref[:, here] + c2 * g_ref[:, here]
            )
    copy.wait()
    for s in range(cell_ref.shape[0]):
        out_ref[:, s * TILE : (s + 1) * TILE] = grid_ref[cell_ref[s], 0:RHS, :]


def shards(offsets, tile_cell, probes, target, lengthscale, amplitude, noise):
    size = lax.axis_size("rows")
    points = size * tile_cell.shape[0] * TILE
    down = [(i, i + 1) for i in range(size - 1)]
    up = [(i + 1, i) for i in range(size - 1)]

    tiles = tile_cell.shape[0]
    first, second, consts = call(
        pack_kernel,
        "pack",
        (pltpu.VMEM((ROWS, WIDE), F32), pltpu.VMEM((ROWS, WIDE), F32), pltpu.VMEM((8, TILE), F32)),
        [HBM] * 4 + [SMEM] * 3,
        [
            pltpu.SMEM((tiles,), jnp.int32),
            pltpu.SMEM((tiles,), jnp.int32),
            pltpu.VMEM((2, tiles * TILE), F32),
            pltpu.VMEM((8, tiles * TILE), jnp.int32),
            pltpu.VMEM((1, tiles * TILE), F32),
            pltpu.SemaphoreType.DMA((4,)),
        ],
        flops=1 << 20,
        limit=60.5,
    )(
        tile_cell,
        offsets,
        probes,
        target.reshape(1, -1),
        lengthscale,
        amplitude,
        noise,
    )

    def outer(slot, other, own, part, *ahead):
        return call(
            lambda *refs: outer_kernel(slot, *refs),
            f"outer{slot}",
            (weight_rows(1), grid_row(), spread_row()) + (pltpu.VMEM((ROWS, WIDE), F32),) * (2 - slot),
            [VMEM] * (7 - slot),
            [feature_tiles(), spread_row(ROWS)],
            flops=1 << 30,
        )(other, own, consts, part, right, b1_spread, *ahead)

    above = lax.ppermute(second, "rows", down)
    below = lax.ppermute(first, "rows", up)
    left, right, _, b1_spread, part0, part1 = call(
        inner_kernel,
        "inner",
        (weight_rows(2), weight_rows(2), spread_row(ROWS), spread_row(ROWS), *(pltpu.VMEM((ROWS, WIDE), F32),) * 2),
        [VMEM] * 3,
        [feature_tiles()],
        flops=1 << 30,
    )(first, second, consts)
    under, f1, f1_spread, b_beside = outer(1, below, second, part1)
    f_above = lax.ppermute(f1, "rows", down)
    over, f0, f0_spread, ahead0, ahead1 = outer(0, above, first, part0, f1_spread)
    f_below = lax.ppermute(f0, "rows", up)
    g0, g0_spread = call(
        product_kernel,
        "product",
        (grid_row(), spread_row()),
        [VMEM] * 7,
        [spread_row()],
        flops=1 << 29,
    )(f_above, f0, ahead0, consts, left, over, f0_spread)
    g_below = lax.ppermute(g0, "rows", up)
    g1, sums = call(
        gram_kernel,
        "gram",
        (grid_row(), jax.ShapeDtypeStruct((SUMS, 2, ROWS, TILE), F32)),
        [VMEM] * 14,
        [spread_row(), spread_row(), pltpu.VMEM((ROWS, WIDE), F32)],
        flops=1 << 29,
    )(f_below, first, second, f0, f1, g0, b_beside, consts, left, right, under, f0_spread, ahead1, g0_spread)
    parts = call(
        moment_kernel,
        "moment",
        jax.ShapeDtypeStruct((size, 1, 2 * TILE), F32),
        [VMEM] * 6,
        [spread_row()],
        flops=1 << 29,
    )(sums, g_below, second, f1, g1, under)
    parts = lax.all_to_all(parts, "rows", split_axis=0, concat_axis=0, tiled=True)

    solutions, quad = call(
        lambda *refs: finish_kernel(float(points), *refs),
        "finish",
        (
            jax.ShapeDtypeStruct((RHS, tiles * TILE), F32),
            jax.ShapeDtypeStruct((1, RHS), F32),
        ),
        [HBM] + [VMEM] * 8,
        [
            pltpu.SMEM((tiles,), jnp.int32),
            pltpu.VMEM((tiles, ROWS, TILE), F32),
            pltpu.SemaphoreType.DMA,
        ],
        flops=1 << 20,
    )(tile_cell, consts, parts, first, second, f0, f1, g0, g1)
    return (solutions, quad.reshape(RHS))


def solution(mesh):
    return jax.shard_map(
        shards,
        mesh=mesh,
        in_specs=(
            P(None, "rows"),
            P("rows"),
            P(None, "rows"),
            P("rows"),
            P("hyp"),
            P("hyp"),
            P("hyp"),
        ),
        out_specs=(P("hyp", "rows"), P("hyp")),
        check_vma=False,
    )
```

```python
import jax
import jax.numpy as jnp
from jax import lax
from jax.experimental import pallas as pl
from jax.experimental.pallas import tpu as pltpu
from jax.sharding import PartitionSpec as P

TILE = 128
GX = 16
RHS = 9
ROWS = 16
WIDE = GX * TILE
FEATURES = 32
PAD = GX + 2
BAND = 3 * 2 * TILE
F32 = jnp.float32
BF16 = jnp.bfloat16
TINY = 1e-30

VMEM = pl.BlockSpec(memory_space=pltpu.VMEM)
HBM = pl.BlockSpec(memory_space=pltpu.HBM)
SMEM = pl.BlockSpec(memory_space=pltpu.SMEM)
REACH, TOP, FACTOR, NOISE = range(4)


def call(kernel, name, out_shape, in_specs, scratch=(), flops=0, limit=12):
    return pl.pallas_call(
        kernel,
        name=name,
        out_shape=out_shape,
        in_specs=in_specs,
        out_specs=jax.tree.map(lambda _: VMEM, out_shape),
        scratch_shapes=list(scratch),
        cost_estimate=pl.CostEstimate(flops=flops, bytes_accessed=1 << 20, transcendentals=0),
        compiler_params=pltpu.CompilerParams(vmem_limit_bytes=int(limit * 2**20)),
    )


def grid_row():
    return jax.ShapeDtypeStruct((ROWS, WIDE), F32)


def spread_row(rows=2 * ROWS):
    return pltpu.VMEM((rows, PAD * 2 * TILE), BF16)


def weight_rows(count):
    return pltpu.VMEM((count, GX, BAND, TILE), BF16)


def feature_tiles():
    return pltpu.VMEM((PAD, TILE, FEATURES), BF16)


def lanes(tile, width=TILE):
    return pl.ds(pl.multiple_of(tile * width, width), width)


def pack_kernel(
    cell_hbm,
    offsets_hbm,
    probes_hbm,
    target_hbm,
    scale_ref,
    amp_ref,
    noise_ref,
    first_ref,
    second_ref,
    consts_ref,
    cell_ref,
    from_ref,
    offsets_ref,
    probes_ref,
    target_ref,
    sems,
):
    copies = [
        pltpu.make_async_copy(source, dest, sems.at[i])
        for i, (source, dest) in enumerate(
            (
                (cell_hbm, cell_ref),
                (offsets_hbm, offsets_ref),
                (probes_hbm, probes_ref),
                (target_hbm, target_ref),
            )
        )
    ]
    for copy in copies:
        copy.start()
    for copy in copies:
        copy.wait()
    for s in range(cell_ref.shape[0]):
        from_ref[cell_ref[s]] = s
    filler = jnp.zeros((ROWS - RHS - 2, TILE), F32)
    for cell in range(cell_ref.shape[0]):
        stored = lanes(from_ref[cell])
        here = slice(cell % GX * TILE, (cell % GX + 1) * TILE)
        ref = (first_ref, second_ref)[cell // GX]
        ref[0:8, here] = 2.0 * probes_ref[:, stored].astype(F32) - 1.0
        ref[8:16, here] = jnp.concatenate(
            [target_ref[:, stored], offsets_ref[:, stored], filler], axis=0
        )
    amp = jnp.full((1, TILE), amp_ref[0], F32)
    reach = jnp.exp(0.2 * jnp.log(4.0 * amp))
    square = reach * reach
    consts_ref[REACH : REACH + 1, :] = reach
    consts_ref[TOP : TOP + 1, :] = 5.0 * amp / (square * square)
    consts_ref[FACTOR : FACTOR + 1, :] = reach / jnp.full((1, TILE), scale_ref[0], F32)
    consts_ref[NOISE : NOISE + 1, :] = jnp.full((1, TILE), noise_ref[0], F32)


def constant(consts_ref, which):
    return consts_ref[which : which + 1, :]


def split_rows(values, level):
    first = values.astype(BF16).astype(F32)
    rest = values - first
    second = rest.astype(BF16).astype(F32)
    third = rest - second
    return jnp.where(level == 0, first, jnp.where(level == 1, second, third))


def feature_rows():
    row = lax.broadcasted_iota(jnp.int32, (FEATURES, TILE), 0)

    def level(order):
        out = jnp.zeros_like(row)
        for k, v in enumerate(order):
            if v:
                out = jnp.where(row == k, v, out)
        return out

    source = level([0, 0, 1, 1, 0, 2] * 2 + [0, 1, 2] + [0, 0, 0])
    target = level([0, 1, 0, 1, 2, 0] * 2 + [0, 0, 0] + [0, 1, 2])
    kind = jnp.where(row < 6, 0, jnp.where(row < 12, 1, jnp.where(row < 15, 2, jnp.where(row < 18, 3, 4))))
    return kind, source, target


def choose(kind, a, b, c, d):
    return jnp.where(
        kind == 0, a, jnp.where(kind == 1, b, jnp.where(kind == 2, c, jnp.where(kind == 3, d, 0.0)))
    )


def source_features(row_ref, factor, rows, out_ref):
    kind, source, _ = rows
    zero = jnp.zeros((TILE, FEATURES), BF16)
    out_ref[0] = zero
    out_ref[PAD - 1] = zero

    def one(tile, carry):
        a = factor * (row_ref[9:10, lanes(tile)] - 0.5)
        b = factor * (row_ref[10:11, lanes(tile)] - 0.5)
        values = choose(kind, a, b, a * a + b * b, 1.0)
        out_ref[tile + 1] = split_rows(values, source).T.astype(BF16)
        return carry

    lax.fori_loop(0, GX, one, 0, unroll=8)


def target_features(row_ref, tile, row_shift, col_shift, factor, rows):
    kind, _, target = rows
    a = factor * ((row_shift + 0.5) - row_ref[9:10, lanes(tile)])
    b = factor * ((col_shift + 0.5) - row_ref[10:11, lanes(tile)])
    values = choose(kind, 2.0 * a, 2.0 * b, 1.0, a * a + b * b)
    return split_rows(values, target).astype(BF16)


def fill_weights(targets, feats_ref, consts_ref, rows, also=None):
    factor = constant(consts_ref, FACTOR)
    reach = jnp.broadcast_to(constant(consts_ref, REACH), (TILE, TILE))
    top = jnp.broadcast_to(constant(consts_ref, TOP), (TILE, TILE))

    def one(tile, carry):
        for k in range(3):
            wanted = [
                target_features(ref, tile, float(row_shift), float(k - 1), factor, rows)
                for ref, row_shift, _, _ in targets
            ]
            squares = lax.dot_general(
                feats_ref[tile + k],
                wanted[0] if len(wanted) == 1 else jnp.concatenate(wanted, axis=1),
                (((1,), (0,)), ((), ())),
                preferred_element_type=F32,
            )
            for i, (_, _, weights_ref, combo) in enumerate(targets):
                here = jnp.maximum(squares[:, i * TILE : (i + 1) * TILE], 1e-12)
                close = jnp.maximum(reach - here * lax.rsqrt(here), 0.0)
                second = close * close
                weight = (second * second) * (top - close)
                high = weight.astype(BF16)
                low = (weight - high.astype(F32)).astype(BF16)
                base = k * 2 * TILE
                weights_ref[combo, tile, base : base + TILE, :] = high
                weights_ref[combo, tile, base + TILE : base + 2 * TILE, :] = low
        if also is not None:
            also(tile)
        return carry

    lax.fori_loop(0, GX, one, 0, unroll=8 // len(targets))


def spread_ends(out_ref):
    empty = jnp.zeros((2 * ROWS, 2 * TILE), BF16)
    out_ref[:, 0 : 2 * TILE] = empty
    out_ref[:, (PAD - 1) * 2 * TILE :] = empty


def spread_tile(values, out_ref, tile):
    high = values.astype(BF16)
    low = (values - high.astype(F32)).astype(BF16)
    both = jnp.concatenate([high, low], axis=0)
    at = pl.multiple_of((tile + 1) * 2 * TILE, 2 * TILE)
    out_ref[:, pl.ds(at, 2 * TILE)] = jnp.concatenate([both, both], axis=1)


def spread(row_ref, out_ref):
    spread_ends(out_ref)
    for tile in range(GX):
        spread_tile(row_ref[:, tile * TILE : (tile + 1) * TILE], out_ref, tile)


def spread_sides(row_ref, out_ref):
    empty = jnp.zeros((ROWS, 2 * TILE), BF16)
    out_ref[:, 0 : 2 * TILE] = empty
    out_ref[:, (PAD - 1) * 2 * TILE :] = empty
    row = lax.broadcasted_iota(jnp.int32, (8, TILE), 0)
    for tile in range(GX):
        here = slice(tile * TILE, (tile + 1) * TILE)
        target = row_ref[8:9, here]
        high = target.astype(BF16).astype(F32)
        rest = jnp.where(row == 0, high, jnp.where(row == 1, target - high, 0.0))
        both = jnp.concatenate([row_ref[0:8, here], rest], axis=0).astype(BF16)
        at = (tile + 1) * 2 * TILE
        out_ref[:, at : at + 2 * TILE] = jnp.concatenate([both, both], axis=1)


def banded(spread_ref, weights_ref, combo, tile):
    at = pl.multiple_of(tile * 2 * TILE, 2 * TILE)
    return jnp.dot(
        spread_ref[:, pl.ds(at, BAND)],
        weights_ref[combo, tile],
        preferred_element_type=F32,
    )


def joined(both):
    if both.shape[0] == 2 * ROWS:
        return both[0:ROWS] + both[ROWS:]
    row = lax.broadcasted_iota(jnp.int32, both.shape, 0)
    return both + jnp.where(row == 8, pltpu.roll(both, ROWS - 1, 0), 0.0)


GROUP = 16


def apply_row(own_ref, ahead_ref, terms, consts_ref, out_ref, out_spread_ref, beside_ref=None):
    noise = constant(consts_ref, NOISE)
    spread_ends(out_spread_ref)

    def group(g, carry):
        for j in range(GROUP):
            tile = g * GROUP + j
            here = lanes(tile)
            both = banded(*terms[0], tile)
            if beside_ref is not None:
                beside_ref[:, here] = joined(both)
            for term in terms[1:]:
                both = both + banded(*term, tile)
            total = noise * own_ref[:, here] + ahead_ref[:, here] + joined(both)
            out_ref[:, here] = total
            spread_tile(total, out_spread_ref, tile)
        return carry

    lax.fori_loop(0, GX // GROUP, group, 0)


def two_sum(a, b):
    total = a + b
    part = total - a
    return total, (a - (total - part)) + (b - part)


def quick_sum(a, b):
    total = a + b
    return total, b - (total - a)


def halves(a):
    scaled = 4097.0 * a
    high = scaled - (scaled - a)
    return high, a - high


def two_product(a, b):
    a1, a2 = halves(a)
    b1, b2 = halves(b)
    product = a * b
    return product, ((a1 * b1 - product) + a1 * b2 + a2 * b1) + a2 * b2


class Pair:
    def __init__(self, high, low):
        self.high, self.low = high, low

    def __add__(self, other):
        total, error = two_sum(self.high, other.high)
        return Pair(*quick_sum(total, error + (self.low + other.low)))

    def __neg__(self):
        return Pair(-self.high, -self.low)

    def __sub__(self, other):
        return self + (-other)

    def __mul__(self, other):
        if not isinstance(other, Pair):
            return Pair(self.high * other, self.low * other)
        product, error = two_product(self.high, other.high)
        return Pair(*quick_sum(product, error + (self.high * other.low + self.low * other.high)))

    def __truediv__(self, other):
        first = self.high / other.high
        rest = self - other * Pair(first, jnp.zeros_like(first))
        return Pair(*quick_sum(first, rest.high / other.high))

    def where(self, keep, other):
        return Pair(jnp.where(keep, self.high, other.high), jnp.where(keep, self.low, other.low))


SUMS = 9
STRIDE = TILE // SUMS


def grid_mask(k):
    lane = lax.broadcasted_iota(jnp.int32, (ROWS, TILE), 1)
    row = lax.broadcasted_iota(jnp.int32, (ROWS, TILE), 0)
    return (lane == row + STRIDE * k) & (row < RHS)


def accumulate(sums, term):
    total, left = two_sum(sums[0], term)
    return total, sums[1] + left


def lines(sums):
    row = lax.broadcasted_iota(jnp.int32, (8, TILE), 0)
    lane = lax.broadcasted_iota(jnp.int32, (8, TILE), 1)
    blocks = [[(high[0:8], low[0:8]), lane == row + STRIDE * k] for k, (high, low) in enumerate(sums)]
    for start in range(0, len(sums), 8):
        last = [jnp.zeros((8, TILE), F32), jnp.zeros((8, TILE), F32)]
        group = sums[start : start + 8]
        for k, pair in enumerate(group):
            last = [jnp.where(row == k, jnp.broadcast_to(v[8:9], (8, TILE)), t) for v, t in zip(pair, last)]
        mask = (lane == 8 + STRIDE * (start + row)) & (row < len(group))
        blocks.append([tuple(last), mask])
    placed = [jnp.zeros((8, TILE), F32), jnp.zeros((8, TILE), F32)]
    for (high, low), mask in blocks:
        for shift in (64, 32, 16, 8, 4, 2, 1):
            high, left = two_sum(high, pltpu.roll(high, shift, 1))
            low = (low + pltpu.roll(low, shift, 1)) + left
        high, low = quick_sum(high, low)
        placed = [jnp.where(mask, high, placed[0]), jnp.where(mask, low, placed[1])]
    return [jnp.sum(p, axis=0, keepdims=True) for p in placed]


def inner_kernel(
    first_ref, second_ref, consts_ref, left_ref, right_ref, spread0_ref, spread1_ref, feats_ref
):
    rows = feature_rows()
    for slot, (own_ref, weights_ref, spread_ref) in enumerate(
        ((first_ref, left_ref, spread0_ref), (second_ref, right_ref, spread1_ref))
    ):
        source_features(own_ref, constant(consts_ref, FACTOR), rows, feats_ref)
        targets = ((first_ref, slot, weights_ref, 0), (second_ref, slot - 1, weights_ref, 1))
        fill_weights(targets, feats_ref, consts_ref, rows)
        spread_sides(own_ref, spread_ref)


def outer_kernel(
    slot, other_ref, own_ref, consts_ref, left_ref, right_ref, spread0_ref, spread1_ref, *more
):
    if slot:
        weights_ref, out_ref, out_spread_ref, beside_ref, feats_ref, spread_ref = more
        ahead, beside = (), beside_ref
    else:
        f1_ref, weights_ref, out_ref, out_spread_ref, ahead0_ref, ahead1_ref, feats_ref, spread_ref = more
        ahead, beside = (ahead0_ref, ahead1_ref), None
    rows = feature_rows()
    source_features(other_ref, constant(consts_ref, FACTOR), rows, feats_ref)
    noise = constant(consts_ref, NOISE)

    def own_part(tile):
        here = lanes(tile)
        both = banded(spread0_ref, left_ref, slot, tile) + banded(spread1_ref, right_ref, slot, tile)
        out_ref[:, here] = noise * own_ref[:, here] + joined(both)
        for i, ahead_ref in enumerate(ahead):
            ahead_ref[:, here] = joined(banded(f1_ref, right_ref, i, tile))

    targets = ((own_ref, 2 * slot - 1, weights_ref, 0),)
    fill_weights(targets, feats_ref, consts_ref, rows, own_part)
    spread_sides(other_ref, spread_ref)
    spread_ends(out_spread_ref)
    for tile in range(GX):
        here = slice(tile * TILE, (tile + 1) * TILE)
        halo = joined(banded(spread_ref, weights_ref, 0, tile))
        if beside is not None:
            beside[:, here] = halo
        total = out_ref[:, here] + halo
        out_ref[:, here] = total
        spread_tile(total, out_spread_ref, tile)


def product_kernel(
    other_ref,
    own_ref,
    ahead_ref,
    consts_ref,
    left_ref,
    weights_ref,
    spread0_ref,
    out_ref,
    out_spread_ref,
    spread_ref,
):
    spread(other_ref, spread_ref)
    terms = ((spread_ref, weights_ref, 0), (spread0_ref, left_ref, 0))
    apply_row(own_ref, ahead_ref, terms, consts_ref, out_ref, out_spread_ref)


def gram_kernel(
    below_ref,
    b0_ref,
    b1_ref,
    f0_ref,
    f1_ref,
    g0_ref,
    b_beside_ref,
    consts_ref,
    left_ref,
    right_ref,
    under_ref,
    f0_spread_ref,
    ahead_ref,
    g0_spread_ref,
    g1_ref,
    sums_ref,
    spread_ref,
    g1_spread_ref,
    f_beside_ref,
):
    spread(below_ref, spread_ref)
    terms = ((spread_ref, under_ref, 0), (f0_spread_ref, left_ref, 1))
    apply_row(f1_ref, ahead_ref, terms, consts_ref, g1_ref, g1_spread_ref, f_beside_ref)
    zero = jnp.zeros((ROWS, TILE), F32)
    noise = constant(consts_ref, NOISE)

    def group(g, sums):
        sums = list(sums)
        terms = [zero] * SUMS
        for j in range(8):
            tile = g * 8 + j
            here = lanes(tile)
            for half, refs in enumerate(((b0_ref, f0_ref, g0_ref), (b1_ref, f1_ref, g1_ref))):
                v = [ref[:, here] for ref in refs]
                for k, (i, m) in enumerate(((0, 0), (0, 1), (0, 2), (1, 1), (1, 2), (2, 2))):
                    terms[k] = terms[k] + v[i] * v[m]
                both = banded(g0_spread_ref, left_ref, half, tile)
                both = both + banded(g1_spread_ref, right_ref, half, tile)
                image = noise * v[2] + joined(both)
                for k in range(3):
                    terms[6 + k] = terms[6 + k] + v[k] * image
                if half == 1:
                    terms[6] = terms[6] + v[2] * b_beside_ref[:, here]
                    terms[7] = terms[7] + v[2] * f_beside_ref[:, here]
            if j % 2 == 1:
                sums = [accumulate(s, t) for s, t in zip(sums, terms)]
                terms = [zero] * SUMS
        return tuple(sums)

    sums = lax.fori_loop(0, GX // 8, group, ((zero, zero),) * SUMS)
    for k, (high, low) in enumerate(sums):
        sums_ref[k, 0] = high
        sums_ref[k, 1] = low


def moment_kernel(sums_ref, below_ref, b_ref, f_ref, g_ref, weights_ref, out_ref, spread_ref):
    spread(below_ref, spread_ref)
    zero = jnp.zeros((ROWS, TILE), F32)
    sums = [(sums_ref[k, 0], sums_ref[k, 1]) for k in range(SUMS)]
    terms = [zero] * 3
    for tile in range(GX):
        here = slice(tile * TILE, (tile + 1) * TILE)
        image = joined(banded(spread_ref, weights_ref, 0, tile))
        factors = (b_ref[:, here], f_ref[:, here], 2.0 * g_ref[:, here])
        terms = [t + v * image for t, v in zip(terms, factors)]
        if tile % 4 == 3:
            sums[6:] = [accumulate(s, t) for s, t in zip(sums[6:], terms)]
            terms = [zero] * 3
    both = jnp.concatenate(lines(sums), axis=1)
    out_ref[...] = jnp.broadcast_to(both[None], out_ref.shape)


def finish_kernel(
    points,
    cell_hbm,
    consts_ref,
    parts_ref,
    b0_ref,
    b1_ref,
    f0_ref,
    f1_ref,
    g0_ref,
    g1_ref,
    out_ref,
    quad_ref,
    cell_ref,
    grid_ref,
    sem,
):
    copy = pltpu.make_async_copy(cell_hbm, cell_ref, sem)
    copy.start()
    high, low = parts_ref[:, 0, 0:TILE], parts_ref[:, 0, TILE:]
    while high.shape[0] > 8:
        half = high.shape[0] // 2
        high, left = two_sum(high[:half], high[half:])
        low = (low[:half] + low[half:]) + left
    for shift in (4, 2, 1):
        high, left = two_sum(high, pltpu.roll(high, shift, 0))
        low = (low + pltpu.roll(low, shift, 0)) + left
    high, low = quick_sum(high, low)
    bb, bf, bg, ff, fg, gg, bag, fag, gag = (
        Pair(high, low)
        if k == 0
        else Pair(pltpu.roll(high, TILE - STRIDE * k, 1), pltpu.roll(low, TILE - STRIDE * k, 1))
        for k in range(SUMS)
    )
    zero = jnp.zeros_like(high)
    none = Pair(zero, zero)
    one = Pair(zero + 1.0, zero)
    most = jnp.broadcast_to(1.0 / constant(consts_ref, NOISE), high.shape)

    floor = bb.high * 1e-11

    def step(square, product):
        good = (square.high > floor) & (product.high > 0.0)
        ratio = square / product.where(good, one)
        fits = ratio.high < most
        return ratio.where(fits, Pair(most, zero)).where(good, none), good

    def over(a, b, good):
        return (a / b.where(good, one)).where(good, none)

    alpha0, good0 = step(bb, bf)
    rr1 = bb - alpha0 * (bf * 2.0 - alpha0 * ff)
    beta0 = over(rr1, bb, good0)
    p0, p1 = one + beta0, -alpha0
    alpha1, good1 = step(rr1, p0 * (p0 * bf + p1 * (bg + ff)) + p1 * p1 * fg)
    r1, r2 = -(alpha0 + alpha1 * p0), -(alpha1 * p1)
    rr2 = bb + r1 * (bf * 2.0 + r1 * ff) + r2 * (bg * 2.0 + r1 * fg * 2.0 + r2 * gg)
    beta1 = over(rr2, rr1, good1)
    q0, q1, q2 = one + beta1 * p0, r1 + beta1 * p1, r2
    alpha2, good2 = step(
        rr2,
        q0 * (q0 * bf + q1 * (bg + ff) + q2 * (fg + bag)) + q1 * (q1 * fg + q2 * (gg + fag)) + q2 * q2 * gag,
    )
    alpha2 = alpha2.where(good1, none)
    on_b = alpha0 + alpha1 * p0 + alpha2 * q0
    on_f = alpha1 * p1 + alpha2 * q1
    on_g = alpha2 * q2
    quad = on_b * bb + on_f * bf + on_g * bg
    quad_ref[...] = (quad.high / points)[0:1, 0:RHS]
    mask = grid_mask(0)
    c0, c1, c2 = (
        jnp.broadcast_to(
            jnp.sum(
                jnp.where(mask, jnp.concatenate([c.high, c.high], axis=0), 0.0), axis=1, keepdims=True
            ),
            (ROWS, TILE),
        )
        for c in (on_b, on_f, on_g)
    )
    for half, (b_ref, f_ref, g_ref) in enumerate(
        ((b0_ref, f0_ref, g0_ref), (b1_ref, f1_ref, g1_ref))
    ):
        for tile in range(GX):
            here = slice(tile * TILE, (tile + 1) * TILE)
            grid_ref[half * GX + tile] = (
                c0 * b_ref[:, here] + c1 * f_ref[:, here] + c2 * g_ref[:, here]
            )
    copy.wait()
    for s in range(cell_ref.shape[0]):
        out_ref[:, s * TILE : (s + 1) * TILE] = grid_ref[cell_ref[s], 0:RHS, :]


def shards(offsets, tile_cell, probes, target, lengthscale, amplitude, noise):
    size = lax.axis_size("rows")
    points = size * tile_cell.shape[0] * TILE
    down = [(i, i + 1) for i in range(size - 1)]
    up = [(i + 1, i) for i in range(size - 1)]

    tiles = tile_cell.shape[0]
    first, second, consts = call(
        pack_kernel,
        "pack",
        (pltpu.VMEM((ROWS, WIDE), F32), pltpu.VMEM((ROWS, WIDE), F32), pltpu.VMEM((8, TILE), F32)),
        [HBM] * 4 + [SMEM] * 3,
        [
            pltpu.SMEM((tiles,), jnp.int32),
            pltpu.SMEM((tiles,), jnp.int32),
            pltpu.VMEM((2, tiles * TILE), F32),
            pltpu.VMEM((8, tiles * TILE), jnp.int32),
            pltpu.VMEM((1, tiles * TILE), F32),
            pltpu.SemaphoreType.DMA((4,)),
        ],
        flops=1 << 20,
        limit=60.5,
    )(
        tile_cell,
        offsets,
        probes,
        target.reshape(1, -1),
        lengthscale,
        amplitude,
        noise,
    )

    def outer(slot, other, own, *ahead):
        return call(
            lambda *refs: outer_kernel(slot, *refs),
            f"outer{slot}",
            (weight_rows(1), grid_row(), spread_row()) + (pltpu.VMEM((ROWS, WIDE), F32),) * (2 - slot),
            [VMEM] * (8 - slot),
            [feature_tiles(), spread_row(ROWS)],
            flops=1 << 30,
        )(other, own, consts, left, right, b0_spread, b1_spread, *ahead)

    above = lax.ppermute(second, "rows", down)
    below = lax.ppermute(first, "rows", up)
    left, right, b0_spread, b1_spread = call(
        inner_kernel,
        "inner",
        (weight_rows(2), weight_rows(2), spread_row(ROWS), spread_row(ROWS)),
        [VMEM] * 3,
        [feature_tiles()],
        flops=1 << 30,
    )(first, second, consts)
    under, f1, f1_spread, b_beside = outer(1, below, second)
    f_above = lax.ppermute(f1, "rows", down)
    over, f0, f0_spread, ahead0, ahead1 = outer(0, above, first, f1_spread)
    f_below = lax.ppermute(f0, "rows", up)
    g0, g0_spread = call(
        product_kernel,
        "product",
        (grid_row(), spread_row()),
        [VMEM] * 7,
        [spread_row()],
        flops=1 << 29,
    )(f_above, f0, ahead0, consts, left, over, f0_spread)
    g_below = lax.ppermute(g0, "rows", up)
    g1, sums = call(
        gram_kernel,
        "gram",
        (grid_row(), jax.ShapeDtypeStruct((SUMS, 2, ROWS, TILE), F32)),
        [VMEM] * 14,
        [spread_row(), spread_row(), pltpu.VMEM((ROWS, WIDE), F32)],
        flops=1 << 29,
    )(f_below, first, second, f0, f1, g0, b_beside, consts, left, right, under, f0_spread, ahead1, g0_spread)
    parts = call(
        moment_kernel,
        "moment",
        jax.ShapeDtypeStruct((size, 1, 2 * TILE), F32),
        [VMEM] * 6,
        [spread_row()],
        flops=1 << 29,
    )(sums, g_below, second, f1, g1, under)
    parts = lax.all_to_all(parts, "rows", split_axis=0, concat_axis=0, tiled=True)

    solutions, quad = call(
        lambda *refs: finish_kernel(float(points), *refs),
        "finish",
        (
            jax.ShapeDtypeStruct((RHS, tiles * TILE), F32),
            jax.ShapeDtypeStruct((1, RHS), F32),
        ),
        [HBM] + [VMEM] * 8,
        [
            pltpu.SMEM((tiles,), jnp.int32),
            pltpu.VMEM((tiles, ROWS, TILE), F32),
            pltpu.SemaphoreType.DMA,
        ],
        flops=1 << 20,
    )(tile_cell, consts, parts, first, second, f0, f1, g0, g1)
    return (solutions, quad.reshape(RHS))


def solution(mesh):
    return jax.shard_map(
        shards,
        mesh=mesh,
        in_specs=(
            P(None, "rows"),
            P("rows"),
            P(None, "rows"),
            P("rows"),
            P("hyp"),
            P("hyp"),
            P("hyp"),
        ),
        out_specs=(P("hyp", "rows"), P("hyp")),
        check_vma=False,
    )
```

```python
import jax
import jax.numpy as jnp
from jax import lax
from jax.experimental import pallas as pl
from jax.experimental.pallas import tpu as pltpu
from jax.sharding import PartitionSpec as P

TILE = 128
GX = 16
RHS = 9
ROWS = 16
WIDE = GX * TILE
FEATURES = 32
PAD = GX + 2
BAND = 3 * 2 * TILE
F32 = jnp.float32
BF16 = jnp.bfloat16
TINY = 1e-30

VMEM = pl.BlockSpec(memory_space=pltpu.VMEM)
HBM = pl.BlockSpec(memory_space=pltpu.HBM)
SMEM = pl.BlockSpec(memory_space=pltpu.SMEM)
REACH, TOP, FACTOR, NOISE = range(4)


def call(kernel, name, out_shape, in_specs, scratch=(), flops=0, limit=12):
    return pl.pallas_call(
        kernel,
        name=name,
        out_shape=out_shape,
        in_specs=in_specs,
        out_specs=jax.tree.map(lambda _: VMEM, out_shape),
        scratch_shapes=list(scratch),
        cost_estimate=pl.CostEstimate(flops=flops, bytes_accessed=1 << 20, transcendentals=0),
        compiler_params=pltpu.CompilerParams(vmem_limit_bytes=int(limit * 2**20)),
    )


def grid_row():
    return jax.ShapeDtypeStruct((ROWS, WIDE), F32)


def spread_row(rows=2 * ROWS):
    return pltpu.VMEM((rows, PAD * 2 * TILE), BF16)


def weight_rows(count):
    return pltpu.VMEM((count, GX, BAND, TILE), BF16)


def feature_tiles():
    return pltpu.VMEM((PAD, TILE, FEATURES), BF16)


def lanes(tile, width=TILE):
    return pl.ds(pl.multiple_of(tile * width, width), width)


def pack_kernel(
    cell_hbm,
    offsets_hbm,
    probes_hbm,
    target_hbm,
    scale_ref,
    amp_ref,
    noise_ref,
    first_ref,
    second_ref,
    consts_ref,
    cell_ref,
    from_ref,
    offsets_ref,
    probes_ref,
    target_ref,
    sems,
):
    copies = [
        pltpu.make_async_copy(source, dest, sems.at[i])
        for i, (source, dest) in enumerate(
            (
                (cell_hbm, cell_ref),
                (offsets_hbm, offsets_ref),
                (probes_hbm, probes_ref),
                (target_hbm, target_ref),
            )
        )
    ]
    for copy in copies:
        copy.start()
    for copy in copies:
        copy.wait()
    for s in range(cell_ref.shape[0]):
        from_ref[cell_ref[s]] = s
    filler = jnp.zeros((ROWS - RHS - 2, TILE), F32)
    for cell in range(cell_ref.shape[0]):
        stored = lanes(from_ref[cell])
        here = slice(cell % GX * TILE, (cell % GX + 1) * TILE)
        ref = (first_ref, second_ref)[cell // GX]
        ref[0:8, here] = 2.0 * probes_ref[:, stored].astype(F32) - 1.0
        ref[8:16, here] = jnp.concatenate(
            [target_ref[:, stored], offsets_ref[:, stored], filler], axis=0
        )
    amp = jnp.full((1, TILE), amp_ref[0], F32)
    reach = jnp.exp(0.2 * jnp.log(4.0 * amp))
    square = reach * reach
    consts_ref[REACH : REACH + 1, :] = reach
    consts_ref[TOP : TOP + 1, :] = 5.0 * amp / (square * square)
    consts_ref[FACTOR : FACTOR + 1, :] = reach / jnp.full((1, TILE), scale_ref[0], F32)
    consts_ref[NOISE : NOISE + 1, :] = jnp.full((1, TILE), noise_ref[0], F32)


def constant(consts_ref, which):
    return consts_ref[which : which + 1, :]


def split_rows(values, level):
    first = values.astype(BF16).astype(F32)
    rest = values - first
    second = rest.astype(BF16).astype(F32)
    third = rest - second
    return jnp.where(level == 0, first, jnp.where(level == 1, second, third))


def feature_rows():
    row = lax.broadcasted_iota(jnp.int32, (FEATURES, TILE), 0)

    def level(order):
        out = jnp.zeros_like(row)
        for k, v in enumerate(order):
            if v:
                out = jnp.where(row == k, v, out)
        return out

    source = level([0, 0, 1, 1, 0, 2] * 2 + [0, 1, 2] + [0, 0, 0])
    target = level([0, 1, 0, 1, 2, 0] * 2 + [0, 0, 0] + [0, 1, 2])
    kind = jnp.where(row < 6, 0, jnp.where(row < 12, 1, jnp.where(row < 15, 2, jnp.where(row < 18, 3, 4))))
    return kind, source, target


def choose(kind, a, b, c, d):
    return jnp.where(
        kind == 0, a, jnp.where(kind == 1, b, jnp.where(kind == 2, c, jnp.where(kind == 3, d, 0.0)))
    )


def source_features(row_ref, factor, rows, out_ref):
    kind, source, _ = rows
    zero = jnp.zeros((TILE, FEATURES), BF16)
    out_ref[0] = zero
    out_ref[PAD - 1] = zero

    def one(tile, carry):
        a = factor * (row_ref[9:10, lanes(tile)] - 0.5)
        b = factor * (row_ref[10:11, lanes(tile)] - 0.5)
        values = choose(kind, a, b, a * a + b * b, 1.0)
        out_ref[tile + 1] = split_rows(values, source).T.astype(BF16)
        return carry

    lax.fori_loop(0, GX, one, 0, unroll=8)


def target_features(row_ref, tile, row_shift, col_shift, factor, rows):
    kind, _, target = rows
    a = factor * ((row_shift + 0.5) - row_ref[9:10, lanes(tile)])
    b = factor * ((col_shift + 0.5) - row_ref[10:11, lanes(tile)])
    values = choose(kind, 2.0 * a, 2.0 * b, 1.0, a * a + b * b)
    return split_rows(values, target).astype(BF16)


def fill_weights(targets, feats_ref, consts_ref, rows, also=None):
    factor = constant(consts_ref, FACTOR)
    reach = jnp.broadcast_to(constant(consts_ref, REACH), (TILE, TILE))
    top = jnp.broadcast_to(constant(consts_ref, TOP), (TILE, TILE))

    def one(tile, carry):
        for k in range(3):
            wanted = [
                target_features(ref, tile, float(row_shift), float(k - 1), factor, rows)
                for ref, row_shift, _, _ in targets
            ]
            squares = lax.dot_general(
                feats_ref[tile + k],
                wanted[0] if len(wanted) == 1 else jnp.concatenate(wanted, axis=1),
                (((1,), (0,)), ((), ())),
                preferred_element_type=F32,
            )
            for i, (_, _, weights_ref, combo) in enumerate(targets):
                here = jnp.maximum(squares[:, i * TILE : (i + 1) * TILE], 1e-12)
                close = jnp.maximum(reach - here * lax.rsqrt(here), 0.0)
                second = close * close
                weight = (second * second) * (top - close)
                high = weight.astype(BF16)
                low = (weight - high.astype(F32)).astype(BF16)
                base = k * 2 * TILE
                weights_ref[combo, tile, base : base + TILE, :] = high
                weights_ref[combo, tile, base + TILE : base + 2 * TILE, :] = low
        if also is not None:
            also(tile)
        return carry

    lax.fori_loop(0, GX, one, 0, unroll=8 // len(targets))


def spread_ends(out_ref):
    empty = jnp.zeros((2 * ROWS, 2 * TILE), BF16)
    out_ref[:, 0 : 2 * TILE] = empty
    out_ref[:, (PAD - 1) * 2 * TILE :] = empty


def spread_tile(values, out_ref, tile):
    high = values.astype(BF16)
    low = (values - high.astype(F32)).astype(BF16)
    both = jnp.concatenate([high, low], axis=0)
    at = pl.multiple_of((tile + 1) * 2 * TILE, 2 * TILE)
    out_ref[:, pl.ds(at, 2 * TILE)] = jnp.concatenate([both, both], axis=1)


def spread(row_ref, out_ref):
    spread_ends(out_ref)
    for tile in range(GX):
        spread_tile(row_ref[:, tile * TILE : (tile + 1) * TILE], out_ref, tile)


def spread_sides(row_ref, out_ref):
    empty = jnp.zeros((ROWS, 2 * TILE), BF16)
    out_ref[:, 0 : 2 * TILE] = empty
    out_ref[:, (PAD - 1) * 2 * TILE :] = empty
    row = lax.broadcasted_iota(jnp.int32, (8, TILE), 0)
    for tile in range(GX):
        here = slice(tile * TILE, (tile + 1) * TILE)
        target = row_ref[8:9, here]
        high = target.astype(BF16).astype(F32)
        rest = jnp.where(row == 0, high, jnp.where(row == 1, target - high, 0.0))
        both = jnp.concatenate([row_ref[0:8, here], rest], axis=0).astype(BF16)
        at = (tile + 1) * 2 * TILE
        out_ref[:, at : at + 2 * TILE] = jnp.concatenate([both, both], axis=1)


def banded(spread_ref, weights_ref, combo, tile):
    at = pl.multiple_of(tile * 2 * TILE, 2 * TILE)
    return jnp.dot(
        spread_ref[:, pl.ds(at, BAND)],
        weights_ref[combo, tile],
        preferred_element_type=F32,
    )


def joined(both):
    if both.shape[0] == 2 * ROWS:
        return both[0:ROWS] + both[ROWS:]
    row = lax.broadcasted_iota(jnp.int32, both.shape, 0)
    return both + jnp.where(row == 8, pltpu.roll(both, ROWS - 1, 0), 0.0)


GROUP = 16


def apply_row(own_ref, ahead_ref, terms, consts_ref, out_ref, out_spread_ref, beside_ref=None):
    noise = constant(consts_ref, NOISE)
    spread_ends(out_spread_ref)

    def group(g, carry):
        for j in range(GROUP):
            tile = g * GROUP + j
            here = lanes(tile)
            both = banded(*terms[0], tile)
            if beside_ref is not None:
                beside_ref[:, here] = joined(both)
            for term in terms[1:]:
                both = both + banded(*term, tile)
            total = noise * own_ref[:, here] + ahead_ref[:, here] + joined(both)
            out_ref[:, here] = total
            spread_tile(total, out_spread_ref, tile)
        return carry

    lax.fori_loop(0, GX // GROUP, group, 0)


def two_sum(a, b):
    total = a + b
    part = total - a
    return total, (a - (total - part)) + (b - part)


def quick_sum(a, b):
    total = a + b
    return total, b - (total - a)


def halves(a):
    scaled = 4097.0 * a
    high = scaled - (scaled - a)
    return high, a - high


def two_product(a, b):
    a1, a2 = halves(a)
    b1, b2 = halves(b)
    product = a * b
    return product, ((a1 * b1 - product) + a1 * b2 + a2 * b1) + a2 * b2


class Pair:
    def __init__(self, high, low):
        self.high, self.low = high, low

    def __add__(self, other):
        total, error = two_sum(self.high, other.high)
        return Pair(*quick_sum(total, error + (self.low + other.low)))

    def __neg__(self):
        return Pair(-self.high, -self.low)

    def __sub__(self, other):
        return self + (-other)

    def __mul__(self, other):
        if not isinstance(other, Pair):
            return Pair(self.high * other, self.low * other)
        product, error = two_product(self.high, other.high)
        return Pair(*quick_sum(product, error + (self.high * other.low + self.low * other.high)))

    def __truediv__(self, other):
        first = self.high / other.high
        rest = self - other * Pair(first, jnp.zeros_like(first))
        return Pair(*quick_sum(first, rest.high / other.high))

    def where(self, keep, other):
        return Pair(jnp.where(keep, self.high, other.high), jnp.where(keep, self.low, other.low))


SUMS = 9
STRIDE = TILE // SUMS


def grid_mask(k):
    lane = lax.broadcasted_iota(jnp.int32, (ROWS, TILE), 1)
    row = lax.broadcasted_iota(jnp.int32, (ROWS, TILE), 0)
    return (lane == row + STRIDE * k) & (row < RHS)


def accumulate(sums, term):
    total, left = two_sum(sums[0], term)
    return total, sums[1] + left


def lines(sums):
    row = lax.broadcasted_iota(jnp.int32, (8, TILE), 0)
    lane = lax.broadcasted_iota(jnp.int32, (8, TILE), 1)
    blocks = [[(high[0:8], low[0:8]), lane == row + STRIDE * k] for k, (high, low) in enumerate(sums)]
    for start in range(0, len(sums), 8):
        last = [jnp.zeros((8, TILE), F32), jnp.zeros((8, TILE), F32)]
        group = sums[start : start + 8]
        for k, pair in enumerate(group):
            last = [jnp.where(row == k, jnp.broadcast_to(v[8:9], (8, TILE)), t) for v, t in zip(pair, last)]
        mask = (lane == 8 + STRIDE * (start + row)) & (row < len(group))
        blocks.append([tuple(last), mask])
    placed = [jnp.zeros((8, TILE), F32), jnp.zeros((8, TILE), F32)]
    for (high, low), mask in blocks:
        for shift in (64, 32, 16, 8, 4, 2, 1):
            high, left = two_sum(high, pltpu.roll(high, shift, 1))
            low = (low + pltpu.roll(low, shift, 1)) + left
        high, low = quick_sum(high, low)
        placed = [jnp.where(mask, high, placed[0]), jnp.where(mask, low, placed[1])]
    return [jnp.sum(p, axis=0, keepdims=True) for p in placed]


def inner_kernel(
    first_ref, second_ref, consts_ref, left_ref, right_ref, spread0_ref, spread1_ref, feats_ref
):
    rows = feature_rows()
    for slot, (own_ref, weights_ref, spread_ref) in enumerate(
        ((first_ref, left_ref, spread0_ref), (second_ref, right_ref, spread1_ref))
    ):
        source_features(own_ref, constant(consts_ref, FACTOR), rows, feats_ref)
        targets = ((first_ref, slot, weights_ref, 0), (second_ref, slot - 1, weights_ref, 1))
        fill_weights(targets, feats_ref, consts_ref, rows)
        spread_sides(own_ref, spread_ref)


def outer_kernel(
    slot, other_ref, own_ref, consts_ref, left_ref, right_ref, spread0_ref, spread1_ref, *more
):
    if slot:
        weights_ref, out_ref, out_spread_ref, beside_ref, feats_ref, spread_ref = more
        ahead, beside = (), beside_ref
    else:
        f1_ref, weights_ref, out_ref, out_spread_ref, ahead0_ref, ahead1_ref, feats_ref, spread_ref = more
        ahead, beside = (ahead0_ref, ahead1_ref), None
    rows = feature_rows()
    source_features(other_ref, constant(consts_ref, FACTOR), rows, feats_ref)
    noise = constant(consts_ref, NOISE)

    def own_part(tile):
        here = lanes(tile)
        both = banded(spread0_ref, left_ref, slot, tile) + banded(spread1_ref, right_ref, slot, tile)
        out_ref[:, here] = noise * own_ref[:, here] + joined(both)
        for i, ahead_ref in enumerate(ahead):
            ahead_ref[:, here] = joined(banded(f1_ref, right_ref, i, tile))

    targets = ((own_ref, 2 * slot - 1, weights_ref, 0),)
    fill_weights(targets, feats_ref, consts_ref, rows, own_part)
    spread_sides(other_ref, spread_ref)
    spread_ends(out_spread_ref)
    for tile in range(GX):
        here = slice(tile * TILE, (tile + 1) * TILE)
        halo = joined(banded(spread_ref, weights_ref, 0, tile))
        if beside is not None:
            beside[:, here] = halo
        total = out_ref[:, here] + halo
        out_ref[:, here] = total
        spread_tile(total, out_spread_ref, tile)


def product_kernel(
    other_ref,
    own_ref,
    ahead_ref,
    consts_ref,
    left_ref,
    weights_ref,
    spread0_ref,
    out_ref,
    out_spread_ref,
    spread_ref,
):
    spread(other_ref, spread_ref)
    terms = ((spread_ref, weights_ref, 0), (spread0_ref, left_ref, 0))
    apply_row(own_ref, ahead_ref, terms, consts_ref, out_ref, out_spread_ref)


def gram_kernel(
    below_ref,
    b0_ref,
    b1_ref,
    f0_ref,
    f1_ref,
    g0_ref,
    b_beside_ref,
    consts_ref,
    left_ref,
    right_ref,
    under_ref,
    f0_spread_ref,
    ahead_ref,
    g0_spread_ref,
    g1_ref,
    sums_ref,
    spread_ref,
    g1_spread_ref,
    f_beside_ref,
):
    spread(below_ref, spread_ref)
    terms = ((spread_ref, under_ref, 0), (f0_spread_ref, left_ref, 1))
    apply_row(f1_ref, ahead_ref, terms, consts_ref, g1_ref, g1_spread_ref, f_beside_ref)
    zero = jnp.zeros((ROWS, TILE), F32)
    noise = constant(consts_ref, NOISE)

    def group(g, sums):
        sums = list(sums)
        terms = [zero] * SUMS
        for j in range(GROUP):
            tile = g * GROUP + j
            here = lanes(tile)
            for half, refs in enumerate(((b0_ref, f0_ref, g0_ref), (b1_ref, f1_ref, g1_ref))):
                v = [ref[:, here] for ref in refs]
                for k, (i, m) in enumerate(((0, 0), (0, 1), (0, 2), (1, 1), (1, 2), (2, 2))):
                    terms[k] = terms[k] + v[i] * v[m]
                both = banded(g0_spread_ref, left_ref, half, tile)
                both = both + banded(g1_spread_ref, right_ref, half, tile)
                image = noise * v[2] + joined(both)
                for k in range(3):
                    terms[6 + k] = terms[6 + k] + v[k] * image
                if half == 1:
                    terms[6] = terms[6] + v[2] * b_beside_ref[:, here]
                    terms[7] = terms[7] + v[2] * f_beside_ref[:, here]
            if j % 4 == 3:
                sums = [accumulate(s, t) for s, t in zip(sums, terms)]
                terms = [zero] * SUMS
        return tuple(sums)

    sums = lax.fori_loop(0, GX // GROUP, group, ((zero, zero),) * SUMS)
    for k, (high, low) in enumerate(sums):
        sums_ref[k, 0] = high
        sums_ref[k, 1] = low


def moment_kernel(sums_ref, below_ref, b_ref, f_ref, g_ref, weights_ref, out_ref, spread_ref):
    spread(below_ref, spread_ref)
    zero = jnp.zeros((ROWS, TILE), F32)
    sums = [(sums_ref[k, 0], sums_ref[k, 1]) for k in range(SUMS)]
    terms = [zero] * 3
    for tile in range(GX):
        here = slice(tile * TILE, (tile + 1) * TILE)
        image = joined(banded(spread_ref, weights_ref, 0, tile))
        factors = (b_ref[:, here], f_ref[:, here], 2.0 * g_ref[:, here])
        terms = [t + v * image for t, v in zip(terms, factors)]
        if tile % 4 == 3:
            sums[6:] = [accumulate(s, t) for s, t in zip(sums[6:], terms)]
            terms = [zero] * 3
    both = jnp.concatenate(lines(sums), axis=1)
    out_ref[...] = jnp.broadcast_to(both[None], out_ref.shape)


def finish_kernel(
    points,
    cell_hbm,
    consts_ref,
    parts_ref,
    b0_ref,
    b1_ref,
    f0_ref,
    f1_ref,
    g0_ref,
    g1_ref,
    out_ref,
    quad_ref,
    cell_ref,
    grid_ref,
    sem,
):
    copy = pltpu.make_async_copy(cell_hbm, cell_ref, sem)
    copy.start()
    high, low = parts_ref[:, 0, 0:TILE], parts_ref[:, 0, TILE:]
    while high.shape[0] > 8:
        half = high.shape[0] // 2
        high, left = two_sum(high[:half], high[half:])
        low = (low[:half] + low[half:]) + left
    for shift in (4, 2, 1):
        high, left = two_sum(high, pltpu.roll(high, shift, 0))
        low = (low + pltpu.roll(low, shift, 0)) + left
    high, low = quick_sum(high, low)
    bb, bf, bg, ff, fg, gg, bag, fag, gag = (
        Pair(high, low)
        if k == 0
        else Pair(pltpu.roll(high, TILE - STRIDE * k, 1), pltpu.roll(low, TILE - STRIDE * k, 1))
        for k in range(SUMS)
    )
    zero = jnp.zeros_like(high)
    none = Pair(zero, zero)
    one = Pair(zero + 1.0, zero)
    most = jnp.broadcast_to(1.0 / constant(consts_ref, NOISE), high.shape)

    floor = bb.high * 1e-11

    def step(square, product):
        good = (square.high > floor) & (product.high > 0.0)
        ratio = square / product.where(good, one)
        fits = ratio.high < most
        return ratio.where(fits, Pair(most, zero)).where(good, none), good

    def over(a, b, good):
        return (a / b.where(good, one)).where(good, none)

    alpha0, good0 = step(bb, bf)
    rr1 = bb - alpha0 * (bf * 2.0 - alpha0 * ff)
    beta0 = over(rr1, bb, good0)
    p0, p1 = one + beta0, -alpha0
    alpha1, good1 = step(rr1, p0 * (p0 * bf + p1 * (bg + ff)) + p1 * p1 * fg)
    r1, r2 = -(alpha0 + alpha1 * p0), -(alpha1 * p1)
    rr2 = bb + r1 * (bf * 2.0 + r1 * ff) + r2 * (bg * 2.0 + r1 * fg * 2.0 + r2 * gg)
    beta1 = over(rr2, rr1, good1)
    q0, q1, q2 = one + beta1 * p0, r1 + beta1 * p1, r2
    alpha2, good2 = step(
        rr2,
        q0 * (q0 * bf + q1 * (bg + ff) + q2 * (fg + bag)) + q1 * (q1 * fg + q2 * (gg + fag)) + q2 * q2 * gag,
    )
    alpha2 = alpha2.where(good1, none)
    on_b = alpha0 + alpha1 * p0 + alpha2 * q0
    on_f = alpha1 * p1 + alpha2 * q1
    on_g = alpha2 * q2
    quad = on_b * bb + on_f * bf + on_g * bg
    quad_ref[...] = (quad.high / points)[0:1, 0:RHS]
    mask = grid_mask(0)
    c0, c1, c2 = (
        jnp.broadcast_to(
            jnp.sum(
                jnp.where(mask, jnp.concatenate([c.high, c.high], axis=0), 0.0), axis=1, keepdims=True
            ),
            (ROWS, TILE),
        )
        for c in (on_b, on_f, on_g)
    )
    for half, (b_ref, f_ref, g_ref) in enumerate(
        ((b0_ref, f0_ref, g0_ref), (b1_ref, f1_ref, g1_ref))
    ):
        for tile in range(GX):
            here = slice(tile * TILE, (tile + 1) * TILE)
            grid_ref[half * GX + tile] = (
                c0 * b_ref[:, here] + c1 * f_ref[:, here] + c2 * g_ref[:, here]
            )
    copy.wait()
    for s in range(cell_ref.shape[0]):
        out_ref[:, s * TILE : (s + 1) * TILE] = grid_ref[cell_ref[s], 0:RHS, :]


def shards(offsets, tile_cell, probes, target, lengthscale, amplitude, noise):
    size = lax.axis_size("rows")
    points = size * tile_cell.shape[0] * TILE
    down = [(i, i + 1) for i in range(size - 1)]
    up = [(i + 1, i) for i in range(size - 1)]

    tiles = tile_cell.shape[0]
    first, second, consts = call(
        pack_kernel,
        "pack",
        (pltpu.VMEM((ROWS, WIDE), F32), pltpu.VMEM((ROWS, WIDE), F32), pltpu.VMEM((8, TILE), F32)),
        [HBM] * 4 + [SMEM] * 3,
        [
            pltpu.SMEM((tiles,), jnp.int32),
            pltpu.SMEM((tiles,), jnp.int32),
            pltpu.VMEM((2, tiles * TILE), F32),
            pltpu.VMEM((8, tiles * TILE), jnp.int32),
            pltpu.VMEM((1, tiles * TILE), F32),
            pltpu.SemaphoreType.DMA((4,)),
        ],
        flops=1 << 20,
        limit=60.5,
    )(
        tile_cell,
        offsets,
        probes,
        target.reshape(1, -1),
        lengthscale,
        amplitude,
        noise,
    )

    def outer(slot, other, own, *ahead):
        return call(
            lambda *refs: outer_kernel(slot, *refs),
            f"outer{slot}",
            (weight_rows(1), grid_row(), spread_row()) + (pltpu.VMEM((ROWS, WIDE), F32),) * (2 - slot),
            [VMEM] * (8 - slot),
            [feature_tiles(), spread_row(ROWS)],
            flops=1 << 30,
        )(other, own, consts, left, right, b0_spread, b1_spread, *ahead)

    above = lax.ppermute(second, "rows", down)
    below = lax.ppermute(first, "rows", up)
    left, right, b0_spread, b1_spread = call(
        inner_kernel,
        "inner",
        (weight_rows(2), weight_rows(2), spread_row(ROWS), spread_row(ROWS)),
        [VMEM] * 3,
        [feature_tiles()],
        flops=1 << 30,
    )(first, second, consts)
    under, f1, f1_spread, b_beside = outer(1, below, second)
    f_above = lax.ppermute(f1, "rows", down)
    over, f0, f0_spread, ahead0, ahead1 = outer(0, above, first, f1_spread)
    f_below = lax.ppermute(f0, "rows", up)
    g0, g0_spread = call(
        product_kernel,
        "product",
        (grid_row(), spread_row()),
        [VMEM] * 7,
        [spread_row()],
        flops=1 << 29,
    )(f_above, f0, ahead0, consts, left, over, f0_spread)
    g_below = lax.ppermute(g0, "rows", up)
    g1, sums = call(
        gram_kernel,
        "gram",
        (grid_row(), jax.ShapeDtypeStruct((SUMS, 2, ROWS, TILE), F32)),
        [VMEM] * 14,
        [spread_row(), spread_row(), pltpu.VMEM((ROWS, WIDE), F32)],
        flops=1 << 29,
    )(f_below, first, second, f0, f1, g0, b_beside, consts, left, right, under, f0_spread, ahead1, g0_spread)
    parts = call(
        moment_kernel,
        "moment",
        jax.ShapeDtypeStruct((size, 1, 2 * TILE), F32),
        [VMEM] * 6,
        [spread_row()],
        flops=1 << 29,
    )(sums, g_below, second, f1, g1, under)
    parts = lax.all_to_all(parts, "rows", split_axis=0, concat_axis=0, tiled=True)

    solutions, quad = call(
        lambda *refs: finish_kernel(float(points), *refs),
        "finish",
        (
            jax.ShapeDtypeStruct((RHS, tiles * TILE), F32),
            jax.ShapeDtypeStruct((1, RHS), F32),
        ),
        [HBM] + [VMEM] * 8,
        [
            pltpu.SMEM((tiles,), jnp.int32),
            pltpu.VMEM((tiles, ROWS, TILE), F32),
            pltpu.SemaphoreType.DMA,
        ],
        flops=1 << 20,
    )(tile_cell, consts, parts, first, second, f0, f1, g0, g1)
    return (solutions, quad.reshape(RHS))


def solution(mesh):
    return jax.shard_map(
        shards,
        mesh=mesh,
        in_specs=(
            P(None, "rows"),
            P("rows"),
            P(None, "rows"),
            P("rows"),
            P("hyp"),
            P("hyp"),
            P("hyp"),
        ),
        out_specs=(P("hyp", "rows"), P("hyp")),
        check_vma=False,
    )
```
